32 devices in a mesh: dp: 16 (over z, y, x), fsdp: 2 (over core).
Axes of the slice: x: 2, y: 2, z: 4, core: 2. Of those that a mesh axis runs over, the one named last changes fastest.
Arguments:
- features: bfloat16 [64, 1128, 512], P(('dp', 'fsdp')), may hold values from -6 to 6
- cotangent: bfloat16 [64, 1128, 512], P(('dp', 'fsdp')), may hold values from -6 to 6
- counts: int32 [64], P(('dp', 'fsdp')), may hold values from 1 to 100, as said below
- weights: float32 [4096, 512], P(('dp', 'fsdp'))
- small_params: float32 [3584], replicated
- moments_old: float32 [2, 4096, 512], P(None, ('dp', 'fsdp')), as said below
- small_moments: float32 [2, 3584], replicated, as said below
- basis_attn: float32 [4, 512, 512], replicated, as said below
- basis_ffn: float32 [2, 1024, 1024], replicated, as said below
- basis_cols: float32 [6, 512, 512], replicated, as said below
Outputs:
- output: bfloat16 [64, 1128, 512], P(('dp', 'fsdp'))
- grad_input: float32 [64, 1128, 512], P(('dp', 'fsdp'))
- grad_weights: float32 [4096, 512], P(('dp', 'fsdp'))
- moments_new: float32 [2, 4096, 512], P(None, ('dp', 'fsdp'))
- weights_new: float32 [4096, 512], P(('dp', 'fsdp'))
- grad_small: float32 [3584], replicated
- small_moments_new: float32 [2, 3584], replicated
- small_new: float32 [3584], replicated
The draws below stay inside these ranges and needn't reach their ends.
Inputs may be any that keep to these rules, and one draw needn't show every extreme that they name: `counts`: some neighbourhood has 100 live queries and some has 1. `basis_attn`: each of the four matrices is orthogonal. `basis_ffn`: each of the two matrices is orthogonal. `basis_cols`: each of the six matrices is orthogonal. `moments_old`: second moments (index 1) are positive. `small_moments`: second moments (index 1) are positive.
All inputs are finite; a program needn't handle non-finite values.
Results may differ from the reference program's by a relative error of at most 0.014.
The reference program's roundings to bfloat16 on the way count: a program that leaves them out, or rounds other values in their place, can miss the bound.
Values may be sent and summed in bfloat16 or wider, within the bound.
No kernel may reach another device: no remote copies, remote signals or barrier semaphores. Data moves between devices by JAX's collectives and lax.ppermute only.
A program may use at most 320 MiB of HBM per device.

```python
import math
import jax
import jax.numpy as jnp
from jax import lax

D = 512
HEADS = 4
FF = 1024
HD = 128
CTX = 1024
QCAP = 104
QMAX = 100
STEP = 10
SLOTS = 1128
NB = 64
MROWS = 4096
SMALL = 3584


def butterfly(key, size):
    levels = size.bit_length() - 1
    angles = jax.random.uniform(key, (levels, size // 2), jnp.float32, -math.pi, math.pi)
    row_ids = jnp.arange(size, dtype=jnp.int32)[:, None]
    col_ids = jnp.arange(size, dtype=jnp.int32)[None, :]
    result = jnp.ones((size, size), jnp.float32)
    for section_number in range(levels):
        below = (1 << section_number) - 1
        current = row_ids & below | col_ids & ~below
        pair_ids = current >> section_number + 1 << section_number | current & below
        theta = angles[section_number][pair_ids]
        cosine = jnp.cos(theta)
        sine = jnp.sin(theta)
        in_bit = col_ids >> section_number & 1
        out_bit = row_ids >> section_number & 1
        factor = jnp.where(in_bit == out_bit, cosine, jnp.where(out_bit == 0, -sine, sine))
        result = result * factor
    return result


def draw_basis_attn(key, part):
    return jnp.stack([butterfly(jax.random.fold_in(key, 11 + block_number), D) for block_number in range(4)])


def draw_basis_ffn(key, part):
    return jnp.stack([butterfly(jax.random.fold_in(key, 21 + block_number), FF) for block_number in range(2)])


def draw_basis_cols(key, part):
    return jnp.stack([butterfly(jax.random.fold_in(key, 31 + block_number), D) for block_number in range(6)])


def row_factors(factors):
    return jnp.tile(jnp.array(factors, jnp.float32), MROWS // 8)


def draw_weights(key, part):
    base = jax.random.truncated_normal(key, -4.0, 4.0, (MROWS, D), jnp.float32)
    inv_d = D ** (-0.5)
    inv_f = FF ** (-0.5)
    scales = row_factors([2.0 * inv_d, inv_d, inv_d, 4.0 * inv_d, inv_d, inv_d, inv_f, inv_f])
    return base * scales[:, None]


def draw_small_params(key, part):
    key_gain = jax.random.fold_in(key, 1)
    key_bias = jax.random.fold_in(key, 2)
    gains = 1.0 + jax.random.uniform(key_gain, (2, D), jnp.float32, -0.3, 0.3)
    biases = 0.3 * jax.random.truncated_normal(key_bias, -4.0, 4.0, (3 * D + FF,), jnp.float32)
    return jnp.concatenate([gains[0], biases[0:D], biases[D:D + FF], biases[D + FF:2 * D + FF], gains[1], biases[2 * D + FF:3 * D + FF]])


def moment_pair(key, shape, grad_scale):
    key_first = jax.random.fold_in(key, 3)
    key_second = jax.random.fold_in(key, 4)
    first = 0.11 * grad_scale * jax.random.truncated_normal(key_first, -4.0, 4.0, shape, jnp.float32)
    level = jax.random.uniform(key_second, shape, jnp.float32, math.log(0.0005), math.log(0.008))
    second = jnp.exp(level) * grad_scale * grad_scale
    return jnp.stack([first, second])


def draw_moments_old(key, part):
    grad_size = (NB * SLOTS) ** 0.5
    scales = row_factors([1.0, 1.0, 1.0, 0.3, 0.6, 0.6, 0.6, 0.6])[:, None] * grad_size
    return moment_pair(key, (MROWS, D), scales)


def draw_small_moments(key, part):
    grad_size = (NB * SLOTS) ** 0.5
    return moment_pair(key, (SMALL,), grad_size)


def draw_counts(key, part):
    key_base = jax.random.fold_in(key, 5)
    key_spot = jax.random.fold_in(key, 6)
    values_drawn = jax.random.randint(key_base, (NB,), 1, QMAX + 1)
    spots = jax.random.randint(key_spot, (2,), 0, NB)
    values_drawn = values_drawn.at[spots[0]].set(QMAX)
    other = (spots[0] + 1 + spots[1] % (NB - 1)) % NB
    return values_drawn.at[other].set(1).astype(jnp.int32)


def block_scale(rng, extent, split, low, high):
    loudness, own = 1.0, jax.random.fold_in(rng, 6)
    for position, shards_of in split:
        steps = jnp.exp(jax.random.uniform(jax.random.fold_in(own, position), (shards_of,), jnp.float32, low / len(split), high / len(split)))
        loudness = loudness * jnp.repeat(steps, extent[position] // shards_of).reshape([-1 if axis == position else 1 for axis in range(len(extent))])
    return loudness


def centred(stream_key, shape, deviation, limit, shards=(), held_as=jnp.bfloat16):
    level = block_scale(stream_key, shape, shards, -0.22, 0.18) if shards else 1.0
    values = jax.random.normal(stream_key, shape, jnp.float32) * deviation * level
    return jnp.minimum(jnp.maximum(values, -limit), limit).astype(held_as)


def setup_inputs(seed: int = 0) -> dict:
    splits = jax.random.split(jax.random.key(seed), 11)
    return {
        "features": centred(splits[0], (NB, SLOTS, D), 1.0, 6.0, ((0, 32),)),
        "cotangent": centred(splits[1], (NB, SLOTS, D), 1.0, 6.0, ((0, 32),)),
        "counts": draw_counts(jax.random.fold_in(splits[10], 71), 0),
        "weights": draw_weights(jax.random.fold_in(splits[10], 71), 0),
        "small_params": draw_small_params(jax.random.fold_in(splits[10], 71), 0),
        "moments_old": draw_moments_old(jax.random.fold_in(splits[10], 71), 0),
        "small_moments": draw_small_moments(jax.random.fold_in(splits[10], 71), 0),
        "basis_attn": draw_basis_attn(jax.random.fold_in(splits[10], 71), 0),
        "basis_ffn": draw_basis_ffn(jax.random.fold_in(splits[10], 71), 0),
        "basis_cols": draw_basis_cols(jax.random.fold_in(splits[10], 71), 0),
    }


@jax.custom_vjp
def low(v):
    return lax.optimization_barrier(v.astype(jnp.bfloat16)).astype(jnp.float32)

@jax.custom_vjp
def low_back(v):
    return v

def low_keep(v):
    return (low(v), None)

def low_pass(kept, grad):
    return (grad,)

def back_keep(v):
    return (v, None)

def back_low(kept, grad):
    return (low(grad),)
low.defvjp(low_keep, low_pass)
low_back.defvjp(back_keep, back_low)
eps_norm = 1e-05
eps_adam = 1e-08
beta_one = 0.9
beta_two = 0.999
rate_mats = 0.1
rate_small = 0.5
highest = lax.Precision.HIGHEST

def to_plain(stacked):
    width = stacked.shape[1]
    groups = stacked.reshape(D, 8, width)
    return jnp.concatenate([groups[:, 0], groups[:, 1], groups[:, 2], groups[:, 3], groups[:, 4:6].reshape(FF, width), groups[:, 6:8].reshape(FF, width)], axis=0)

def to_stacked(plain):
    width = plain.shape[1]
    attn = jnp.transpose(plain[0:4 * D].reshape(4, D, width), (1, 0, 2))
    inner = plain[4 * D:4 * D + FF].reshape(D, 2, width)
    outer = plain[4 * D + FF:4 * D + 2 * FF].reshape(D, 2, width)
    return jnp.concatenate([attn, inner, outer], axis=1).reshape(MROWS, width)

def both_ways(values):
    return low_back(low(values))

def matmul(first_mat, second_mat):
    return jnp.dot(first_mat, second_mat, precision=highest)

def layer_norm(values, gain_vec, shift_vec):
    center = values - lax.optimization_barrier(jnp.mean(values, axis=-1, keepdims=True))
    spread = lax.optimization_barrier(jnp.mean(center * center, axis=-1, keepdims=True))
    return center * lax.rsqrt(spread + eps_norm) * gain_vec + shift_vec

def gelu_exact(values):
    return 0.5 * values * (1.0 + lax.erf(values * 0.7071067811865476))

def split_small(small_params):
    return (small_params[0:D], small_params[D:2 * D], small_params[2 * D:2 * D + FF], small_params[2 * D + FF:3 * D + FF], small_params[3 * D + FF:4 * D + FF], small_params[4 * D + FF:5 * D + FF])

def one_hood(weights, small_params, rows_in, live_rows):
    scaling = HD ** (-0.5)
    plain = to_plain(weights)
    w_query = plain[0:D]
    w_key = plain[D:2 * D]
    w_value = plain[2 * D:3 * D]
    w_output = plain[3 * D:4 * D]
    w_hidden = plain[4 * D:4 * D + FF]
    w_back = plain[4 * D + FF:4 * D + 2 * FF]
    gain_one, shift_one, bias_hidden, bias_output, gain_two, shift_two = split_small(small_params)
    context = rows_in[0:CTX]
    queries = both_ways(matmul(rows_in, w_query.T) * scaling).reshape(SLOTS, HEADS, HD)
    key_rows = both_ways(matmul(context, w_key.T)).reshape(CTX, HEADS, HD)
    value_rows = both_ways(matmul(context, w_value.T)).reshape(CTX, HEADS, HD)
    scores = low_back(jnp.einsum('shd,chd->hsc', queries, key_rows, precision=highest))
    row_top = lax.optimization_barrier(jnp.max(scores, axis=-1, keepdims=True))
    exponent = jnp.exp(scores - row_top)
    soft_weights = exponent / lax.optimization_barrier(jnp.sum(exponent, axis=-1, keepdims=True))
    mixture = both_ways(jnp.einsum('hsc,chd->shd', low(soft_weights), value_rows, precision=highest).reshape(SLOTS, D))
    attended = low_back(matmul(mixture, w_output.T))
    normed = layer_norm(rows_in + attended, gain_one, shift_one)
    hidden = low_back(matmul(low(normed), w_hidden.T) + bias_hidden)
    activated = low(gelu_exact(hidden))
    branch = low_back(matmul(activated, w_back) + bias_output)
    return layer_norm(normed + branch, gain_two, shift_two) * live_rows[:, None]

def rotate_forward(grad, basis_attn, basis_ffn, basis_cols):
    plain = to_plain(grad)
    attn_part = plain[0:4 * D].reshape(4, D, D)
    ffn_part = plain[4 * D:].reshape(2, FF, D)
    attn_rot = jnp.einsum('bji,bjk,bkl->bil', basis_attn, attn_part, basis_cols[0:4], precision=highest)
    ffn_rot = jnp.einsum('bji,bjk,bkl->bil', basis_ffn, ffn_part, basis_cols[4:6], precision=highest)
    return to_stacked(jnp.concatenate([attn_rot.reshape(4 * D, D), ffn_rot.reshape(2 * FF, D)], axis=0))

def rotate_back(step_rot, basis_attn, basis_ffn, basis_cols):
    plain = to_plain(step_rot)
    attn_part = plain[0:4 * D].reshape(4, D, D)
    ffn_part = plain[4 * D:].reshape(2, FF, D)
    attn_back = jnp.einsum('bij,bjk,blk->bil', basis_attn, attn_part, basis_cols[0:4], precision=highest)
    ffn_back = jnp.einsum('bij,bjk,blk->bil', basis_ffn, ffn_part, basis_cols[4:6], precision=highest)
    return to_stacked(jnp.concatenate([attn_back.reshape(4 * D, D), ffn_back.reshape(2 * FF, D)], axis=0))

def adam_step(grad, moments):
    first_new = beta_one * moments[0] + (1.0 - beta_one) * grad
    second_new = beta_two * moments[1] + (1.0 - beta_two) * grad * grad
    direction = first_new / (1.0 - beta_one ** STEP) / (jnp.sqrt(second_new / (1.0 - beta_two ** STEP)) + eps_adam)
    return (jnp.stack([first_new, second_new]), direction)

def reference(features, cotangent, counts, weights, small_params, moments_old, small_moments, basis_attn, basis_ffn, basis_cols):
    rows_all = features.astype(jnp.float32)
    back_all = cotangent.astype(jnp.float32)
    slot_ids = jnp.arange(QCAP, dtype=jnp.int32)
    live_query = (slot_ids[None, :] < counts[:, None]).astype(jnp.float32)
    live_all = jnp.concatenate([jnp.ones((NB, CTX), jnp.float32), live_query], axis=1)
    weights_low = low(weights)

    def whole(weight_in, small_in, rows_in):
        checked = jax.checkpoint(one_hood)

        def per_hood(packed):
            return checked(weight_in, small_in, packed[0], packed[1])
        return lax.map(per_hood, (rows_in, live_all))
    result, pullback = jax.vjp(whole, weights_low, small_params, rows_all)
    grad_weights, grad_small, grad_input = pullback(back_all)
    rotated = rotate_forward(grad_weights, basis_attn, basis_ffn, basis_cols)
    moments_new, direction = adam_step(rotated, moments_old)
    weights_new = weights - rate_mats * rotate_back(direction, basis_attn, basis_ffn, basis_cols)
    small_moments_new, small_direction = adam_step(grad_small, small_moments)
    small_new = small_params - rate_small * small_direction
    return (result.astype(jnp.bfloat16), grad_input, grad_weights, moments_new, weights_new, grad_small, small_moments_new, small_new)
```

```python
import jax
import jax.numpy as jnp
from jax import lax
from jax.sharding import PartitionSpec as P
from jax.experimental import pallas as pl
from jax.experimental.pallas import tpu as pltpu

D = 512
HEADS = 4
FF = 1024
HD = 128
CTX = 1024
SLOTS = 1128
QCAP = 104
STEP = 10
MROWS = 4096
SMALL = 3584
PAD = 1152
RB = 384
NRB = PAD // RB
scaling = HD ** (-0.5)
eps_norm = 1e-05
eps_adam = 1e-08
beta_one = 0.9
beta_two = 0.999
rate_mats = 0.1
rate_small = 0.5
highest = lax.Precision.HIGHEST
bf16 = jnp.bfloat16
f32 = jnp.float32
VLIM = 58 * 1024 * 1024


def nt(a, b):
    return lax.dot_general(a, b, (((1,), (1,)), ((), ())), preferred_element_type=f32)


def nn(a, b):
    return lax.dot_general(a, b, (((1,), (0,)), ((), ())), preferred_element_type=f32)


def tn(a, b):
    return lax.dot_general(a, b, (((0,), (0,)), ((), ())), preferred_element_type=f32)


def attn_fwd_body(xc_ref, xr_ref, w_ref, q_ref, k_ref, v_ref, e_ref, o_ref, li_ref, ve_ref):
    rb = pl.program_id(1)

    @pl.when(rb == 0)
    def _():
        xc = xc_ref[0]
        k_ref[0] = nt(xc, w_ref[1]).astype(bf16)
        v_ref[0] = nt(xc, w_ref[2]).astype(bf16)
        for h in range(HEADS):
            ve_ref[h, :, 0:HD] = v_ref[0, :, h * HD : (h + 1) * HD]
            ve_ref[h, :, HD : 2 * HD] = jnp.ones((CTX, HD), bf16)

    rows = rb * RB + lax.broadcasted_iota(jnp.int32, (RB, 1), 0)
    xr = jnp.where(rows < SLOTS, xr_ref[0].astype(f32), 0.0).astype(bf16)
    q_ref[0] = (nt(xr, w_ref[0]) * scaling).astype(bf16)
    for h in range(HEADS):
        hs = slice(h * HD, (h + 1) * HD)
        s = nt(q_ref[0, :, hs], k_ref[0, :, hs])
        m = jnp.max(s, axis=-1, keepdims=True)
        e_ref[0, h] = jnp.exp(s - m).astype(bf16)
        ov = nn(e_ref[0, h], ve_ref[h])
        li = 1.0 / ov[:, HD:]
        li_ref[0, :, hs] = li
        o_ref[0, :, hs] = (ov[:, :HD] * li).astype(bf16)


def attn_fwd(x, wqkv):
    n = x.shape[0]
    sd = jax.ShapeDtypeStruct
    return pl.pallas_call(
        attn_fwd_body,
        grid=(n, NRB),
        in_specs=[
            pl.BlockSpec((1, CTX, D), lambda i, r: (i, 0, 0)),
            pl.BlockSpec((1, RB, D), lambda i, r: (i, r, 0)),
            pl.BlockSpec((3, D, D), lambda i, r: (0, 0, 0)),
        ],
        out_specs=[
            pl.BlockSpec((1, RB, D), lambda i, r: (i, r, 0)),
            pl.BlockSpec((1, CTX, D), lambda i, r: (i, 0, 0)),
            pl.BlockSpec((1, CTX, D), lambda i, r: (i, 0, 0)),
            pl.BlockSpec((1, HEADS, RB, CTX), lambda i, r: (i, 0, r, 0)),
            pl.BlockSpec((1, RB, D), lambda i, r: (i, r, 0)),
            pl.BlockSpec((1, RB, D), lambda i, r: (i, r, 0)),
        ],
        out_shape=[
            sd((n, PAD, D), bf16),
            sd((n, CTX, D), bf16),
            sd((n, CTX, D), bf16),
            sd((n, HEADS, PAD, CTX), bf16),
            sd((n, PAD, D), bf16),
            sd((n, PAD, D), f32),
        ],
        scratch_shapes=[pltpu.VMEM((HEADS, CTX, 2 * HD), bf16)],
        compiler_params=pltpu.CompilerParams(
            dimension_semantics=("arbitrary", "arbitrary"), vmem_limit_bytes=VLIM
        ),
        cost_estimate=pl.CostEstimate(
            flops=n * 14_000_000_000 // 2, transcendentals=n * HEADS * PAD * CTX, bytes_accessed=n * 20_000_000
        ),
        name="attention_forward",
    )(x, x, wqkv)


def lane_mean(v):
    return jnp.sum(v, axis=-1, keepdims=True) * (1.0 / D)


def rows_body(cnt_ref, x_ref, o_ref, li_ref, c_ref, wo_ref, wi_ref, wb_ref, sp_ref,
              out_ref, d1_ref, do_ref, go_ref, gi_ref, gb_ref, gs_ref):
    n, rb = pl.program_id(0), pl.program_id(1)
    first = jnp.logical_and(n == 0, rb == 0)

    @pl.when(first)
    def _():
        go_ref[...] = jnp.zeros_like(go_ref)
        gi_ref[...] = jnp.zeros_like(gi_ref)
        gb_ref[...] = jnp.zeros_like(gb_ref)
        gs_ref[...] = jnp.zeros_like(gs_ref)

    rows = rb * RB + lax.broadcasted_iota(jnp.int32, (RB, 1), 0)
    valid = rows < SLOTS
    live = rows < CTX + cnt_ref[n]
    gain1, shift1 = sp_ref[0:1], sp_ref[1:2]
    bias2, gain2, shift2 = sp_ref[4:5], sp_ref[5:6], sp_ref[6:7]
    bias1 = jnp.concatenate([sp_ref[2:3], sp_ref[3:4]], axis=1)
    o = o_ref[0]
    r1 = jnp.where(valid, x_ref[0].astype(f32), 0.0) + nt(o, wo_ref[...])
    c1 = r1 - lane_mean(r1)
    is1 = lax.rsqrt(lane_mean(c1 * c1) + eps_norm)
    xh1 = c1 * is1
    h = xh1 * gain1 + shift1
    hb = h.astype(bf16)
    u = nt(hb, wi_ref[...]) + bias1
    au = jnp.abs(u)
    ex = jnp.exp(-0.5 * u * u)
    t = 1.0 / (1.0 + 0.23164189 * au)
    poly = t * (0.127414796 + t * (-0.142248368 + t * (0.7107068705 + t * (-0.7265760135 + t * 0.5307027145))))
    tail = poly * ex
    phi = jnp.where(u >= 0.0, 1.0 - tail, tail)
    gb = (u * phi).astype(bf16)
    dgelu = phi + u * ex * 0.3989422804014327
    r2 = h + nn(gb, wb_ref[...]) + bias2
    c2 = r2 - lane_mean(r2)
    is2 = lax.rsqrt(lane_mean(c2 * c2) + eps_norm)
    xh2 = c2 * is2
    out_ref[0] = jnp.where(live, xh2 * gain2 + shift2, 0.0).astype(bf16)
    dy = jnp.where(live, c_ref[0].astype(f32), 0.0)
    gs_ref[5:6] += jnp.sum(dy * xh2, axis=0, keepdims=True)
    gs_ref[6:7] += jnp.sum(dy, axis=0, keepdims=True)
    e2 = dy * gain2
    d2 = (e2 - lane_mean(e2) - xh2 * lane_mean(e2 * xh2)) * is2
    df = d2.astype(bf16)
    gs_ref[4:5] += jnp.sum(df.astype(f32), axis=0, keepdims=True)
    gb_ref[...] += tn(gb, df)
    du = (nt(df, wb_ref[...]) * dgelu).astype(bf16)
    dub = jnp.sum(du.astype(f32), axis=0, keepdims=True)
    gs_ref[2:3] += dub[:, :D]
    gs_ref[3:4] += dub[:, D:]
    gi_ref[...] += tn(du, hb)
    dh = d2 + nn(du, wi_ref[...])
    gs_ref[0:1] += jnp.sum(dh * xh1, axis=0, keepdims=True)
    gs_ref[1:2] += jnp.sum(dh, axis=0, keepdims=True)
    e1 = dh * gain1
    d1 = (e1 - lane_mean(e1) - xh1 * lane_mean(e1 * xh1)) * is1
    d1_ref[0] = d1
    da = d1.astype(bf16)
    go_ref[...] += tn(da, o)
    do_ref[0] = (nn(da, wo_ref[...]) * li_ref[0]).astype(bf16)


def rows_pass(counts, x, o, li, cot, wo, wi, wb, sp):
    n = x.shape[0]
    sd = jax.ShapeDtypeStruct
    blk = pl.BlockSpec((1, RB, D), lambda i, r, c: (i, r, 0))
    const = lambda *s: pl.BlockSpec(s, lambda i, r, c: (0,) * len(s))
    return pl.pallas_call(
        rows_body,
        grid_spec=pltpu.PrefetchScalarGridSpec(
            num_scalar_prefetch=1,
            grid=(n, NRB),
            in_specs=[blk, blk, blk, blk, const(D, D), const(FF, D), const(FF, D), const(8, D)],
            out_specs=[blk, blk, blk, const(D, D), const(FF, D), const(FF, D), const(8, D)],
        ),
        out_shape=[
            sd((n, SLOTS, D), bf16),
            sd((n, PAD, D), f32),
            sd((n, PAD, D), bf16),
            sd((D, D), f32),
            sd((FF, D), f32),
            sd((FF, D), f32),
            sd((8, D), f32),
        ],
        compiler_params=pltpu.CompilerParams(
            dimension_semantics=("arbitrary", "arbitrary"), vmem_limit_bytes=VLIM
        ),
        cost_estimate=pl.CostEstimate(
            flops=n * 18_000_000_000 // 2, transcendentals=n * PAD * FF * 2, bytes_accessed=n * 15_000_000
        ),
        name="rows_forward_backward",
    )(counts, x, o, li, cot, wo, wi, wb, sp)


def attn_bwd_body(x_ref, q_ref, k_ref, v_ref, e_ref, o_ref, do_ref, acc_ref, w_ref,
                  gi_ref, gw_ref, dq_ref, dkt_ref, dvt_ref):
    n = pl.program_id(0)

    @pl.when(n == 0)
    def _():
        gw_ref[...] = jnp.zeros_like(gw_ref)

    for h in range(2):
        hs = slice(h * HD, (h + 1) * HD)
        dkt = jnp.zeros((HD, CTX), f32)
        dvt = jnp.zeros((HD, CTX), f32)
        for rb in range(NRB):
            rs = slice(rb * RB, (rb + 1) * RB)
            do = do_ref[0, rs, hs]
            dof = do.astype(f32)
            t = jnp.sum(dof * o_ref[0, rs, hs].astype(f32), axis=-1, keepdims=True)
            dp = nt(do, v_ref[0, :, hs])
            e = e_ref[0, h, rs]
            ds = (e.astype(f32) * (dp - t)).astype(bf16)
            dq_ref[rs, hs] = nn(ds, k_ref[0, :, hs]).astype(bf16)
            dvt = dvt + tn(do, e)
            dkt = dkt + tn(q_ref[0, rs, hs], ds)
        dkt_ref[hs] = dkt.astype(bf16)
        dvt_ref[hs] = dvt.astype(bf16)
    xc = x_ref[0, 0:CTX]
    gw_ref[0] += tn(dq_ref[0:CTX], xc) * scaling
    gw_ref[0] += tn(dq_ref[CTX:SLOTS], x_ref[0, CTX:SLOTS]) * scaling
    gw_ref[1] += nn(dkt_ref[...], xc)
    gw_ref[2] += nn(dvt_ref[...], xc)
    gi_ref[0, 0:CTX] = (
        acc_ref[0, 0:CTX]
        + nn(dq_ref[0:CTX], w_ref[0]) * scaling
        + tn(dkt_ref[...], w_ref[1])
        + tn(dvt_ref[...], w_ref[2])
    )
    gi_ref[0, CTX:SLOTS] = acc_ref[0, CTX:SLOTS] + nn(dq_ref[CTX:SLOTS], w_ref[0]) * scaling


def attn_bwd(pair, x, q, k, v, e, o, do, acc, wqkv):
    n = x.shape[0]
    sd = jax.ShapeDtypeStruct
    heads = lambda rows: pl.BlockSpec((1, rows, 2 * HD), lambda i: (i, 0, pair))
    return pl.pallas_call(
        attn_bwd_body,
        grid=(n,),
        in_specs=[
            pl.BlockSpec((1, SLOTS, D), lambda i: (i, 0, 0)),
            heads(PAD),
            heads(CTX),
            heads(CTX),
            pl.BlockSpec((1, 2, PAD, CTX), lambda i: (i, pair, 0, 0)),
            heads(PAD),
            heads(PAD),
            pl.BlockSpec((1, acc.shape[1], D), lambda i: (i, 0, 0)),
            pl.BlockSpec((3, 2 * HD, D), lambda i: (0, pair, 0)),
        ],
        out_specs=[
            pl.BlockSpec((1, SLOTS, D), lambda i: (i, 0, 0)),
            pl.BlockSpec((3, 2 * HD, D), lambda i: (0, 0, 0)),
        ],
        out_shape=[sd((n, SLOTS, D), f32), sd((3, 2 * HD, D), f32)],
        scratch_shapes=[
            pltpu.VMEM((PAD, 2 * HD), bf16),
            pltpu.VMEM((2 * HD, CTX), bf16),
            pltpu.VMEM((2 * HD, CTX), bf16),
        ],
        compiler_params=pltpu.CompilerParams(
            dimension_semantics=("arbitrary",), vmem_limit_bytes=VLIM
        ),
        cost_estimate=pl.CostEstimate(
            flops=n * 9_000_000_000 // 2, transcendentals=0, bytes_accessed=n * 12_000_000
        ),
        name="attention_backward",
    )(x, q, k, v, e, o, do, acc, wqkv)


def to_plain(stacked):
    width = stacked.shape[1]
    groups = stacked.reshape(D, 8, width)
    return jnp.concatenate(
        [
            groups[:, 0],
            groups[:, 1],
            groups[:, 2],
            groups[:, 3],
            groups[:, 4:6].reshape(FF, width),
            groups[:, 6:8].reshape(FF, width),
        ],
        axis=0,
    )


def to_stacked(plain):
    width = plain.shape[1]
    attn = jnp.transpose(plain[0 : 4 * D].reshape(4, D, width), (1, 0, 2))
    inner = plain[4 * D : 4 * D + FF].reshape(D, 2, width)
    outer = plain[4 * D + FF : 4 * D + 2 * FF].reshape(D, 2, width)
    return jnp.concatenate([attn, inner, outer], axis=1).reshape(MROWS, width)


def row_vectors(block_ids, attn_vecs, ffn_vecs):
    pieces = []
    for slot_number in range(4):
        pieces.append(jnp.where((block_ids == slot_number)[:, None], attn_vecs, 0.0))
    for slot_number in range(2):
        pieces.append(jnp.where((block_ids == 4 + slot_number)[:, None], ffn_vecs, 0.0))
    return jnp.concatenate(pieces, axis=1)


def select_right(left_done, block_ids, basis_cols, transposed):
    if transposed:
        every = jnp.einsum("rk,blk->brl", left_done, basis_cols, precision=highest)
    else:
        every = jnp.einsum("rk,bkl->brl", left_done, basis_cols, precision=highest)
    onehot = (block_ids[None, :] == jnp.arange(6, dtype=jnp.int32)[:, None]).astype(jnp.float32)
    return jnp.sum(onehot[:, :, None] * every, axis=0)


def adam_step(grad, moments):
    first_new = beta_one * moments[0] + (1.0 - beta_one) * grad
    second_new = beta_two * moments[1] + (1.0 - beta_two) * grad * grad
    direction = (
        first_new
        / (1.0 - beta_one**STEP)
        / (jnp.sqrt(second_new / (1.0 - beta_two**STEP)) + eps_adam)
    )
    return (jnp.stack([first_new, second_new]), direction)


def on_device(
    features,
    cotangent,
    counts,
    weights,
    small_params,
    moments_old,
    small_moments,
    basis_attn,
    basis_ffn,
    basis_cols,
):
    groups = MROWS // 8
    gathered = lax.all_gather(weights.astype(bf16), ("dp", "fsdp"), axis=0, tiled=True)
    by_slot = gathered.reshape(groups, 8, D).transpose(1, 0, 2)
    wqkv, wo = by_slot[0:3], by_slot[3]
    wi, wb = by_slot[4:6].reshape(FF, D), by_slot[6:8].reshape(FF, D)
    bias1 = small_params[2 * D : 2 * D + FF].reshape(D, 2).T
    sp = jnp.concatenate(
        [
            small_params[: 2 * D].reshape(2, D),
            bias1,
            small_params[2 * D + FF :].reshape(3, D),
            jnp.zeros((1, D), f32),
        ]
    )
    q, k, v, e, o, li = attn_fwd(features, wqkv)
    output, d1, do, go, gi, gb, gs = rows_pass(counts, features, o, li, cotangent, wo, wi, wb, sp)
    part, gw0 = attn_bwd(0, features, q, k, v, e, o, do, d1, wqkv)
    grad_input, gw1 = attn_bwd(1, features, q, k, v, e, o, do, part, wqkv)
    sum_weights = jnp.stack(
        [
            jnp.concatenate([gw0[0], gw1[0]]),
            jnp.concatenate([gw0[1], gw1[1]]),
            jnp.concatenate([gw0[2], gw1[2]]),
            go,
            gi[:D],
            gi[D:],
            gb[:D],
            gb[D:],
        ],
        axis=1,
    ).reshape(MROWS, D)
    sum_small = jnp.concatenate(
        [gs[0], gs[1], gs[2:4].T.reshape(FF), gs[4], gs[5], gs[6]]
    )
    grad_weights = lax.psum_scatter(sum_weights, ("dp", "fsdp"), scatter_dimension=0, tiled=True)
    grad_small = lax.psum(sum_small, ("dp", "fsdp"))
    count_rows = grad_weights.shape[0]
    row_ids = lax.axis_index(("dp", "fsdp")) * count_rows + jnp.arange(count_rows, dtype=jnp.int32)
    within = row_ids % 8
    group_ids = row_ids // 8
    block_ids = jnp.where(within < 4, within, 4 + (within - 4) // 2)
    inner_ids = jnp.where(within < 4, group_ids, 2 * group_ids + within % 2)
    attn_pick = jnp.minimum(block_ids, 3)
    ffn_pick = jnp.clip(block_ids - 4, 0, 1)
    attn_inner = jnp.minimum(inner_ids, D - 1)
    full_grad = to_plain(
        lax.all_gather(
            grad_weights.astype(jnp.bfloat16), ("dp", "fsdp"), axis=0, tiled=True
        ).astype(grad_weights.dtype)
    )
    left_fwd = row_vectors(
        block_ids, basis_attn[attn_pick, :, attn_inner], basis_ffn[ffn_pick, :, inner_ids]
    )
    rotated = select_right(
        jnp.dot(left_fwd, full_grad, precision=highest), block_ids, basis_cols, False
    )
    moments_new, direction = adam_step(rotated, moments_old)
    full_direction = to_plain(
        lax.all_gather(direction.astype(jnp.bfloat16), ("dp", "fsdp"), axis=0, tiled=True).astype(
            direction.dtype
        )
    )
    left_back = row_vectors(
        block_ids, basis_attn[attn_pick, attn_inner, :], basis_ffn[ffn_pick, inner_ids, :]
    )
    update = select_right(
        jnp.dot(left_back, full_direction, precision=highest), block_ids, basis_cols, True
    )
    weights_new = weights - rate_mats * update
    small_moments_new, small_direction = adam_step(grad_small, small_moments)
    small_new = small_params - rate_small * small_direction
    return (
        output,
        grad_input,
        grad_weights,
        moments_new,
        weights_new,
        grad_small,
        small_moments_new,
        small_new,
    )


def solution(mesh):
    placed = (
        P(("dp", "fsdp"), None, None),
        P(("dp", "fsdp"), None, None),
        P(("dp", "fsdp")),
        P(("dp", "fsdp"), None),
        P(),
        P(None, ("dp", "fsdp"), None),
        P(),
        P(),
        P(),
        P(),
    )
    return jax.shard_map(
        on_device,
        mesh=mesh,
        in_specs=placed,
        out_specs=(
            P(("dp", "fsdp"), None, None),
            P(("dp", "fsdp"), None, None),
            P(("dp", "fsdp"), None),
            P(None, ("dp", "fsdp"), None),
            P(("dp", "fsdp"), None),
            P(),
            P(),
            P(),
        ),
        check_vma=False,
    )
```

```python
import functools
import jax
import jax.numpy as jnp
from jax import lax
from jax.sharding import PartitionSpec as P
from jax.experimental import pallas as pl
from jax.experimental.pallas import tpu as pltpu

D = 512
HEADS = 4
FF = 1024
HD = 128
CTX = 1024
SLOTS = 1128
STEP = 10
PAD = 1152
RB = 384
NRB = PAD // RB
scaling = HD ** (-0.5)
eps_norm = 1e-05
eps_adam = 1e-08
beta_one = 0.9
beta_two = 0.999
rate_mats = 0.1
rate_small = 0.5
axes = ("dp", "fsdp")
bf16 = jnp.bfloat16
f32 = jnp.float32
VLIM = 58 * 1024 * 1024


def nt(a, b):
    return lax.dot_general(a, b, (((1,), (1,)), ((), ())), preferred_element_type=f32)


def nn(a, b):
    return lax.dot_general(a, b, (((1,), (0,)), ((), ())), preferred_element_type=f32)


def tn(a, b):
    return lax.dot_general(a, b, (((0,), (0,)), ((), ())), preferred_element_type=f32)


def attn_fwd_body(xc_ref, xr_ref, w_ref, q_ref, k_ref, v_ref, e_ref, o_ref, li_ref, ve_ref):
    rb = pl.program_id(1)

    @pl.when(rb == 0)
    def _():
        xc = xc_ref[0]
        k_ref[0] = nt(xc, w_ref[:, 1].reshape(D, D)).astype(bf16)
        v_ref[0] = nt(xc, w_ref[:, 2].reshape(D, D)).astype(bf16)
        for h in range(HEADS):
            ve_ref[h, :, 0:HD] = v_ref[0, :, h * HD : (h + 1) * HD]
            ve_ref[h, :, HD : 2 * HD] = jnp.ones((CTX, HD), bf16)

    rows = rb * RB + lax.broadcasted_iota(jnp.int32, (RB, 1), 0)
    xr = jnp.where(rows < SLOTS, xr_ref[0].astype(f32), 0.0).astype(bf16)
    q_ref[0] = (nt(xr, w_ref[:, 0].reshape(D, D)) * scaling).astype(bf16)
    for h in range(HEADS):
        hs = slice(h * HD, (h + 1) * HD)
        s = nt(q_ref[0, :, hs], k_ref[0, :, hs])
        m = jnp.max(s, axis=-1, keepdims=True)
        e_ref[0, h] = jnp.exp(s - m).astype(bf16)
        ov = nn(e_ref[0, h], ve_ref[h])
        li = 1.0 / ov[:, HD:]
        li_ref[0, :, hs] = li
        o_ref[0, :, hs] = (ov[:, :HD] * li).astype(bf16)


def attn_fwd(hood, x, wqkv, earlier=()):
    n = x.shape[0]
    sd = jax.ShapeDtypeStruct
    body = attn_fwd_body
    if earlier:
        body = lambda *refs: attn_fwd_body(*refs[:3], *refs[9:])
    return pl.pallas_call(
        body,
        grid=(1, NRB),
        in_specs=[
            pl.BlockSpec((1, CTX, D), lambda i, r: (hood, 0, 0)),
            pl.BlockSpec((1, RB, D), lambda i, r: (hood, r, 0)),
            pl.BlockSpec(wqkv.shape, lambda i, r: (0, 0, 0, 0)),
        ]
        + [pl.BlockSpec(memory_space=pl.ANY)] * len(earlier),
        out_specs=[
            pl.BlockSpec((1, RB, D), lambda i, r: (hood, r, 0)),
            pl.BlockSpec((1, CTX, D), lambda i, r: (hood, 0, 0)),
            pl.BlockSpec((1, CTX, D), lambda i, r: (hood, 0, 0)),
            pl.BlockSpec((1, HEADS, RB, CTX), lambda i, r: (hood, 0, r, 0)),
            pl.BlockSpec((1, RB, D), lambda i, r: (hood, r, 0)),
            pl.BlockSpec((1, RB, D), lambda i, r: (hood, r, 0)),
        ],
        out_shape=[
            sd((n, PAD, D), bf16),
            sd((n, CTX, D), bf16),
            sd((n, CTX, D), bf16),
            sd((n, HEADS, PAD, CTX), bf16),
            sd((n, PAD, D), bf16),
            sd((n, PAD, D), f32),
        ],
        scratch_shapes=[pltpu.VMEM((HEADS, CTX, 2 * HD), bf16)],
        input_output_aliases={3 + i: i for i in range(len(earlier))},
        compiler_params=pltpu.CompilerParams(
            dimension_semantics=("arbitrary", "arbitrary"), vmem_limit_bytes=VLIM
        ),
        cost_estimate=pl.CostEstimate(
            flops=7_000_000_000, transcendentals=HEADS * PAD * CTX, bytes_accessed=20_000_000
        ),
        name="attention_forward",
    )(x, x, wqkv, *earlier)


def lane_mean(v):
    return jnp.sum(v, axis=-1, keepdims=True) * (1.0 / D)


def rows_body(cnt_ref, x_ref, o_ref, li_ref, c_ref, w_ref, sp_ref,
              out_ref, d1_ref, do_ref, go_out, gi_out, gb_out, gs_ref, go_ref, gi_ref, gb_ref):
    n, rb = pl.program_id(0), pl.program_id(1)
    first = jnp.logical_and(n == 0, rb == 0)
    last = jnp.logical_and(n == pl.num_programs(0) - 1, rb == NRB - 1)

    @pl.when(first)
    def _():
        go_ref[...] = jnp.zeros_like(go_ref)
        gi_ref[...] = jnp.zeros_like(gi_ref)
        gb_ref[...] = jnp.zeros_like(gb_ref)
        gs_ref[...] = jnp.zeros_like(gs_ref)

    per = w_ref.shape[1] // 5
    wo = w_ref[:, 0:per].reshape(D, D)
    wi = w_ref[:, per : 3 * per].reshape(FF, D)
    wb = w_ref[:, 3 * per :].reshape(FF, D)
    rows = rb * RB + lax.broadcasted_iota(jnp.int32, (RB, 1), 0)
    valid = rows < SLOTS
    live = rows < CTX + cnt_ref[n]
    gain1, shift1 = sp_ref[0:1], sp_ref[1:2]
    bias2, gain2, shift2 = sp_ref[4:5], sp_ref[5:6], sp_ref[6:7]
    bias1 = jnp.concatenate([sp_ref[2:3], sp_ref[3:4]], axis=1)
    o = o_ref[0]
    r1 = jnp.where(valid, x_ref[0].astype(f32), 0.0) + nt(o, wo)
    c1 = r1 - lane_mean(r1)
    is1 = lax.rsqrt(lane_mean(c1 * c1) + eps_norm)
    xh1 = c1 * is1
    h = xh1 * gain1 + shift1
    hb = h.astype(bf16)
    u = nt(hb, wi) + bias1
    au = jnp.abs(u)
    ex = jnp.exp(-0.5 * u * u)
    t = 1.0 / (1.0 + 0.23164189 * au)
    poly = t * (0.127414796 + t * (-0.142248368 + t * (0.7107068705 + t * (-0.7265760135 + t * 0.5307027145))))
    tail = poly * ex
    phi = jnp.where(u >= 0.0, 1.0 - tail, tail)
    gb = (u * phi).astype(bf16)
    dgelu = phi + u * ex * 0.3989422804014327
    r2 = h + nn(gb, wb) + bias2
    c2 = r2 - lane_mean(r2)
    is2 = lax.rsqrt(lane_mean(c2 * c2) + eps_norm)
    xh2 = c2 * is2
    out_ref[0] = jnp.where(live, xh2 * gain2 + shift2, 0.0).astype(bf16)
    dy = jnp.where(live, c_ref[0].astype(f32), 0.0)
    gs_ref[5:6] += jnp.sum(dy * xh2, axis=0, keepdims=True)
    gs_ref[6:7] += jnp.sum(dy, axis=0, keepdims=True)
    e2 = dy * gain2
    d2 = (e2 - lane_mean(e2) - xh2 * lane_mean(e2 * xh2)) * is2
    df = d2.astype(bf16)
    gs_ref[4:5] += jnp.sum(df.astype(f32), axis=0, keepdims=True)
    gb_ref[...] += tn(gb, df)
    du = (nt(df, wb) * dgelu).astype(bf16)
    dub = jnp.sum(du.astype(f32), axis=0, keepdims=True)
    gs_ref[2:3] += dub[:, :D]
    gs_ref[3:4] += dub[:, D:]
    gi_ref[...] += tn(du, hb)
    dh = d2 + nn(du, wi)
    gs_ref[0:1] += jnp.sum(dh * xh1, axis=0, keepdims=True)
    gs_ref[1:2] += jnp.sum(dh, axis=0, keepdims=True)
    e1 = dh * gain1
    d1 = (e1 - lane_mean(e1) - xh1 * lane_mean(e1 * xh1)) * is1
    d1_ref[0] = d1
    da = d1.astype(bf16)
    go_ref[...] += tn(da, o)
    do_ref[0] = (nn(da, wo) * li_ref[0]).astype(bf16)

    @pl.when(last)
    def _():
        go_out[...] = go_ref[...].astype(bf16)
        gi_out[...] = gi_ref[...].astype(bf16)
        gb_out[...] = gb_ref[...].astype(bf16)


def rows_pass(counts, x, o, li, cot, rest, sp):
    n = x.shape[0]
    sd = jax.ShapeDtypeStruct
    blk = pl.BlockSpec((1, RB, D), lambda i, r, c: (i, r, 0))
    const = lambda *s: pl.BlockSpec(s, lambda i, r, c: (0,) * len(s))
    return pl.pallas_call(
        rows_body,
        grid_spec=pltpu.PrefetchScalarGridSpec(
            num_scalar_prefetch=1,
            grid=(n, NRB),
            in_specs=[blk, blk, blk, blk, const(*rest.shape), const(8, D)],
            out_specs=[blk, blk, blk, const(D, D), const(FF, D), const(FF, D), const(8, D)],
            scratch_shapes=[pltpu.VMEM((D, D), f32), pltpu.VMEM((FF, D), f32), pltpu.VMEM((FF, D), f32)],
        ),
        out_shape=[
            sd((n, SLOTS, D), bf16),
            sd((n, SLOTS, D), f32),
            sd((n, PAD, D), bf16),
            sd((D, D), bf16),
            sd((FF, D), bf16),
            sd((FF, D), bf16),
            sd((8, D), f32),
        ],
        compiler_params=pltpu.CompilerParams(
            dimension_semantics=("arbitrary", "arbitrary"), vmem_limit_bytes=VLIM
        ),
        cost_estimate=pl.CostEstimate(
            flops=n * 18_000_000_000 // 2, transcendentals=n * PAD * FF * 2, bytes_accessed=n * 15_000_000
        ),
        name="rows_forward_backward",
    )(counts, x, o, li, cot, rest, sp)


def attn_bwd_body(x_ref, q_ref, k_ref, v_ref, e_ref, o_ref, do_ref, acc_ref, w_ref,
                  gi_ref, gw_out, dq_ref, dkt_ref, dvt_ref, gw_ref):
    n = pl.program_id(0)

    @pl.when(n == 0)
    def _():
        gw_ref[...] = jnp.zeros_like(gw_ref)

    for h in range(2):
        hs = slice(h * HD, (h + 1) * HD)
        dkt = jnp.zeros((HD, CTX), f32)
        dvt = jnp.zeros((HD, CTX), f32)
        for rb in range(NRB):
            rs = slice(rb * RB, (rb + 1) * RB)
            do = do_ref[0, rs, hs]
            dof = do.astype(f32)
            t = jnp.sum(dof * o_ref[0, rs, hs].astype(f32), axis=-1, keepdims=True)
            dp = nt(do, v_ref[0, :, hs])
            e = e_ref[0, h, rs]
            ds = (e.astype(f32) * (dp - t)).astype(bf16)
            dq_ref[rs, hs] = nn(ds, k_ref[0, :, hs]).astype(bf16)
            dvt = dvt + tn(do, e)
            dkt = dkt + tn(q_ref[0, rs, hs], ds)
        dkt_ref[hs] = dkt.astype(bf16)
        dvt_ref[hs] = dvt.astype(bf16)
    xc = x_ref[0, 0:CTX]
    wq, wk, wv = (w_ref[:, i].reshape(2 * HD, D) for i in range(3))
    gw_ref[0] += (tn(dq_ref[0:CTX], xc) + tn(dq_ref[CTX:SLOTS], x_ref[0, CTX:SLOTS])) * scaling
    gw_ref[1] += nn(dkt_ref[...], xc)
    gw_ref[2] += nn(dvt_ref[...], xc)
    gi_ref[0, 0:CTX] = (
        acc_ref[0, 0:CTX]
        + nn(dq_ref[0:CTX], wq) * scaling
        + tn(dkt_ref[...], wk)
        + tn(dvt_ref[...], wv)
    )
    gi_ref[0, CTX:SLOTS] = acc_ref[0, CTX:SLOTS] + nn(dq_ref[CTX:SLOTS], wq) * scaling

    @pl.when(n == pl.num_programs(0) - 1)
    def _():
        gw_out[...] = gw_ref[...].astype(bf16)


def attn_bwd(pair, x, q, k, v, e, o, do, acc, wqkv):
    n = x.shape[0]
    sd = jax.ShapeDtypeStruct
    ways = wqkv.shape[0]
    if ways > 1:
        wspec = pl.BlockSpec((ways // 2,) + wqkv.shape[1:], lambda i: (pair, 0, 0, 0))
    else:
        wspec = pl.BlockSpec((1, 3, 2 * HD, D), lambda i: (0, 0, pair, 0))
    heads = lambda rows: pl.BlockSpec((1, rows, 2 * HD), lambda i: (i, 0, pair))
    whole = pl.BlockSpec((1, SLOTS, D), lambda i: (i, 0, 0))
    return pl.pallas_call(
        attn_bwd_body,
        grid=(n,),
        in_specs=[
            whole,
            heads(PAD),
            heads(CTX),
            heads(CTX),
            pl.BlockSpec((1, 2, PAD, CTX), lambda i: (i, pair, 0, 0)),
            heads(PAD),
            heads(PAD),
            whole,
            wspec,
        ],
        out_specs=[whole, pl.BlockSpec((3, 2 * HD, D), lambda i: (0, 0, 0))],
        out_shape=[sd((n, SLOTS, D), f32), sd((3, 2 * HD, D), bf16)],
        scratch_shapes=[
            pltpu.VMEM((PAD, 2 * HD), bf16),
            pltpu.VMEM((2 * HD, CTX), bf16),
            pltpu.VMEM((2 * HD, CTX), bf16),
            pltpu.VMEM((3, 2 * HD, D), f32),
        ],
        input_output_aliases={7: 0},
        compiler_params=pltpu.CompilerParams(
            dimension_semantics=("arbitrary",), vmem_limit_bytes=VLIM
        ),
        cost_estimate=pl.CostEstimate(
            flops=9_000_000_000, transcendentals=0, bytes_accessed=24_000_000
        ),
        name="attention_backward",
    )(x, q, k, v, e, o, do, acc, wqkv)


def adam_direction(first_new, second_new):
    return (first_new * (1.0 / (1.0 - beta_one**STEP))) / (
        jnp.sqrt(second_new * (1.0 / (1.0 - beta_two**STEP))) + eps_adam
    )


def rotate_body(g_ref, a_ref, b_ref, m_ref, r_ref, u_ref):
    rows, per = g_ref.shape[0], m_ref.shape[2] // 3
    mine = slice(0, per) if rows == D else slice(per, 3 * per)
    r = nn(tn(a_ref[...], g_ref[...]).astype(bf16), b_ref[...])
    r_ref[...] = r.astype(bf16)
    first_new = beta_one * m_ref[:, 0, mine].reshape(rows, D).astype(f32) + (1.0 - beta_one) * r
    second_new = beta_two * m_ref[:, 1, mine].reshape(rows, D).astype(f32) + (1.0 - beta_two) * r * r
    step = adam_direction(first_new, second_new).astype(bf16)
    u_ref[...] = nn(a_ref[...], nt(step, b_ref[...]).astype(bf16)).astype(bf16)


def rotated_step(grad, rows_basis, cols_basis, moments):
    rows = grad.shape[0]
    sd = jax.ShapeDtypeStruct
    return pl.pallas_call(
        rotate_body,
        out_shape=[sd((rows, D), bf16), sd((rows, D), bf16)],
        compiler_params=pltpu.CompilerParams(vmem_limit_bytes=VLIM),
        cost_estimate=pl.CostEstimate(
            flops=4 * rows * D * (rows + D), transcendentals=rows * D, bytes_accessed=2 * rows * (rows + 5 * D)
        ),
        name="rotated_step",
    )(grad, rows_basis, cols_basis, moments)


class Net:
    def __init__(self, mesh):
        self.count = mesh.size
        self.bits = self.count.bit_length() - 1
        self.inner_bits = self.bits - 2
        self.inner = 1 << self.inner_bits
        self.me = lax.axis_index(axes)
        self.local = self.me & (self.inner - 1)
        self.plane = self.me >> self.inner_bits
        stages = [(0, 1)]
        while stages[-1][0] + stages[-1][1] < self.inner_bits:
            low = stages[-1][0] + stages[-1][1]
            stages.append((low, min(2, self.inner_bits - low)))
        self.stages = stages
        self.top = (self.inner_bits, 2)

    def swap(self, value, offset, targets=None):
        pairs = [(i, i ^ offset) for i in range(self.count)]
        if targets is not None:
            pairs = [(i, j) for i, j in pairs if (j >> self.inner_bits) in targets]
        return lax.ppermute(value, axes, pairs)

    def digit(self, stage):
        return (self.me >> stage[0]) & ((1 << stage[1]) - 1)

    def collect(self, value, stage):
        return [value] + [self.swap(value, rel << stage[0]) for rel in range(1, 1 << stage[1])]

    def widen(self, value, stage):
        return interleave(self.collect(value, stage))

    def gather(self, value, stages):
        for stage in reversed(stages[1:]):
            value = self.widen(value, stage)
        return place(self.me, self.collect(value, stages[0]))

    def cut(self, pick, stage):
        mine = self.digit(stage)
        return [pick(mine ^ rel) for rel in range(1 << stage[1])]

    def trade(self, terms, stage, targets=None):
        return terms[:1] + [
            self.swap(term, rel << stage[0], targets) for rel, term in enumerate(terms) if rel
        ]

    def exchange(self, pick, stage, targets=None):
        return self.trade(self.cut(pick, stage), stage, targets)


def after(value, *earlier):
    return lax.optimization_barrier((value, earlier))[0]


def interleave(parts):
    value = jnp.stack(parts, axis=1)
    return value.reshape((-1,) + value.shape[2:])


def total(parts):
    parts = [p.astype(f32) for p in parts]
    while len(parts) > 1:
        parts = [a + b for a, b in zip(parts[0::2], parts[1::2])]
    return parts[0]


def take_at(value, index, axis):
    return lax.dynamic_index_in_dim(value, index, axis, keepdims=False)


def split_high(value):
    high = lax.reduce_precision(value, 8, 7)
    return jnp.concatenate([high.astype(bf16), (value - high).astype(bf16)])


def join_high(pair):
    half = pair.shape[0] // 2
    return pair[:half].astype(f32) + pair[half:].astype(f32)


def reduce_cut(net, value, stage, extra=None):
    value = value.reshape(-1, 1 << stage[1], value.shape[1], D)

    def pick(d):
        part = take_at(value, d, 1).reshape(-1, D)
        return part if extra is None else jnp.concatenate([part, extra])

    return net.cut(pick, stage)


def reduce_sum(parts, rows, extra=0):
    kept = parts[0].shape[0] - extra
    summed = total([p[:kept] for p in parts]).astype(bf16).reshape(-1, rows, D)
    return (summed, split_high(total([join_high(p[kept:]) for p in parts]))) if extra else summed


def place_body(me_ref, *refs):
    *parts, out = refs
    me = me_ref[0] & (out.shape[0] - 1)

    def move(j, carry):
        for c, part in enumerate(parts):
            out[(j * len(parts) + c) ^ me] = part[j]
        return carry

    lax.fori_loop(0, parts[0].shape[0], move, 0)


def place(me, parts):
    size = len(parts) * parts[0].shape[0]
    shape = jax.ShapeDtypeStruct((size,) + parts[0].shape[1:], parts[0].dtype)
    return pl.pallas_call(
        place_body,
        in_specs=[pl.BlockSpec(memory_space=pltpu.SMEM)]
        + [pl.BlockSpec(memory_space=pltpu.VMEM)] * len(parts),
        out_specs=pl.BlockSpec(memory_space=pltpu.VMEM),
        out_shape=shape,
        compiler_params=pltpu.CompilerParams(vmem_limit_bytes=24 * 1024 * 1024),
        cost_estimate=pl.CostEstimate(flops=0, transcendentals=0, bytes_accessed=4 * shape.size),
        name="place",
    )(me.reshape(1), *parts)


def by_index(parts, index):
    return [
        functools.reduce(
            lambda rest, r: jnp.where(index == (b ^ r), parts[r], rest), range(1, len(parts)), parts[0]
        )
        for b in range(len(parts))
    ]


def on_device(mesh, features, cotangent, counts, weights, small_params, moments_old, small_moments,
              basis_attn, basis_ffn, basis_cols):
    net = Net(mesh)
    per = weights.shape[0] // 8
    everyone = net.stages + [net.top]

    def by_matrix(stacked):
        groups = stacked.reshape(per, 8, D)
        return (
            jnp.transpose(groups[:, 0:4], (1, 0, 2)),
            groups[:, 4:6].reshape(2 * per, D),
            groups[:, 6:8].reshape(2 * per, D),
        )

    def stacked(attn, inner, outer):
        return jnp.concatenate(
            [jnp.stack(attn, axis=1), inner.reshape(per, 2, D), outer.reshape(per, 2, D)], axis=1
        ).reshape(8 * per, D)

    inner = net.inner
    n_attn, n_ffn = D // inner, FF // inner
    ffn_of = lambda plane: jnp.clip(plane - 1, 0, 1)
    stages, top = net.stages, net.top

    own_attn, own_in, own_out = by_matrix(weights.astype(bf16))
    first = own_attn[None, 0:3]
    rest = jnp.concatenate([own_attn[3], own_in, own_out])[None]
    olds = [by_matrix(moments_old[i].astype(bf16)) for i in range(2)]
    old_attn = jnp.stack([m[0] for m in olds], axis=1)
    old_ffn = jnp.stack([jnp.stack([m[1], m[2]]) for m in olds], axis=1)
    old_terms = net.cut(
        lambda d: jnp.concatenate([take_at(old_attn, d, 0), take_at(old_ffn, ffn_of(d), 0)], axis=1), top
    )
    mine = ffn_of(net.plane)
    bases = (
        take_at(basis_attn, net.plane, 0).astype(bf16),
        take_at(basis_cols, net.plane, 0).astype(bf16),
        take_at(basis_ffn, mine, 0).astype(bf16),
        take_at(basis_cols, 4 + mine, 0).astype(bf16),
    )
    sp = jnp.concatenate([small_params.reshape(7, D), jnp.zeros((1, D), f32)])

    order = list(reversed(everyone))
    first_parts = net.collect(first, order[0])
    for i, stage in enumerate(order[1:]):
        first = interleave(first_parts)
        rest = after(rest, first)
        if i == 0:
            rest_parts = net.collect(rest, order[0])
        first_parts = net.collect(first, stage)
        if i:
            rest = interleave(after(rest_parts, first))
            rest_parts = net.collect(rest, order[i])
    wqkv = place(net.me, first_parts)
    if per % 16:
        wqkv = jnp.transpose(wqkv, (1, 0, 2, 3)).reshape(1, 3, D, D)

    wqkv, bases, old_terms, _ = lax.optimization_barrier((wqkv, bases, old_terms, rest))
    kept = attn_fwd(0, features, wqkv)
    rest = interleave(after(rest_parts, kept[4]))
    rest_parts = net.collect(rest, order[-1])
    old_parts = net.trade(after(old_terms, rest), top)
    kept = attn_fwd(1, features, after(wqkv, rest, old_terms), kept)
    rest_parts, old_parts = after((rest_parts, old_parts), kept[4])
    olds = jnp.stack(old_parts)
    for stage in reversed(stages[2:]):
        olds = net.widen(olds, stage)
    rest = place(net.me, rest_parts)
    if per % 16:
        rest = jnp.concatenate(
            [rest[:, lo * per : hi * per].reshape(-1, D) for lo, hi in ((0, 1), (1, 3), (3, 5))]
        )[None]
    old_parts = net.collect(olds, stages[1])
    q, k, v, e, o, li = kept
    output, d1, do, go, gi, gb, gs = rows_pass(
        counts, features, o, li, cotangent, after(rest, olds), sp
    )

    early = jnp.concatenate(
        [go.reshape(inner, -1, D), gi.reshape(inner, -1, D), gb.reshape(inner, -1, D)], axis=1
    )
    small = split_high(gs)
    n_small, n_early = small.shape[0], early.shape[1]
    terms = reduce_cut(net, early, stages[0], small)
    early_parts = net.trade(terms, stages[0])
    olds = interleave(after(old_parts, output))
    old_parts = net.collect(olds, stages[0])
    back = functools.partial(attn_bwd, x=features, q=q, k=k, v=v, e=e, o=o, do=do)
    acc, gw0 = back(0, acc=d1, wqkv=after(wqkv, terms, olds))
    early_parts, old_parts = after((early_parts, old_parts), gw0)
    early, small = reduce_sum(early_parts, n_early, n_small)
    for stage in stages[2:]:
        early, small = reduce_sum(net.trade(reduce_cut(net, early, stage, small), stage), n_early, n_small)
    terms = reduce_cut(net, early, stages[1], small)
    early_parts = net.trade(terms, stages[1])
    olds = place(net.me, old_parts)
    grad_input, gw1 = back(1, acc=acc, wqkv=after(wqkv, terms, olds))
    if per % 16:
        olds = jnp.transpose(olds, (1, 0, 2, 3))
        olds = jnp.concatenate(
            [olds[:, :, 0:per].reshape(2, D, D), olds[:, :, per:].reshape(2, FF, D)], axis=1
        )[None]

    late = jnp.concatenate([gw0, gw1], axis=1).reshape(3, inner, n_attn, D)
    late = jnp.transpose(late, (1, 0, 2, 3)).reshape(inner, 3 * n_attn, D)
    terms = reduce_cut(net, late, stages[0])
    late_parts = net.trade(terms, stages[0])

    early, small = reduce_sum(after(early_parts, terms), n_early, n_small)
    early = early.reshape(n_early, D)
    outs = jnp.stack(
        [
            early[n_attn : n_attn + n_ffn],
            early[n_attn + n_ffn :],
            jnp.concatenate([early[:n_attn], jnp.zeros((n_ffn - n_attn, D), bf16)]),
        ]
    )
    top_terms = net.cut(lambda d: jnp.concatenate([take_at(outs, jnp.maximum(d, 1) - 1, 0), small]), top)
    late = reduce_sum(late_parts, 3 * n_attn)
    for stage in stages[2:]:
        late = reduce_sum(net.trade(reduce_cut(net, late, stage), stage), 3 * n_attn)
    terms = reduce_cut(net, late, stages[1])
    late_parts = net.trade(terms, stages[1])
    top_parts = net.trade(after(top_terms, terms), top)

    late = reduce_sum(late_parts, 3 * n_attn).reshape(3, n_attn, D)
    terms = net.cut(lambda d: take_at(late, jnp.minimum(d, 2), 0), top)
    late_parts = net.trade(terms, top, (0, 1, 2))
    top_parts = after(top_parts, terms)
    ffn = total([p[:n_ffn] for p in top_parts]).astype(bf16)
    gs = total([join_high(p[n_ffn:]) for p in top_parts])
    grad_small = gs[0:7].reshape(-1)
    small_first = beta_one * small_moments[0] + (1.0 - beta_one) * grad_small
    small_second = beta_two * small_moments[1] + (1.0 - beta_two) * grad_small * grad_small
    small_new = small_params - rate_small * adam_direction(small_first, small_second)

    ffn_parts = net.collect(ffn[None], stages[-1])
    attn = total(late_parts).astype(bf16)
    attn = jnp.where(net.plane == 3, ffn[:n_attn], attn)[None]
    for stage in reversed(stages[1:]):
        attn_parts = net.collect(attn, stage)
        ffn = interleave(after(ffn_parts, attn))
        ffn_parts = net.collect(ffn, stages[stages.index(stage) - 1])
        attn = interleave(attn_parts)
    attn_parts = net.collect(attn, stages[0])
    ffn = place(net.me, ffn_parts).reshape(FF, D)
    attn = place(net.me, attn_parts).reshape(D, D)

    r_attn, u_attn = rotated_step(attn, bases[0], bases[1], olds)
    back = take_at(jnp.stack([attn, r_attn, u_attn]).reshape(3, 4, inner, per, D), net.local, 2)
    terms = net.cut(lambda d: take_at(back, d, 1), top)
    back = net.trade(terms, top)
    r_ffn, u_ffn = rotated_step(ffn, bases[2], bases[3], olds)
    back_ffn = take_at(jnp.stack([ffn, r_ffn, u_ffn]).reshape(3, 4, inner, 2 * per, D), net.local, 2)
    back_ffn = net.exchange(lambda d: take_at(back_ffn, d, 1), top)

    back_ffn = by_index(back_ffn, net.plane)
    back = by_index(back, net.plane)
    grad_weights, rotated, update = (
        stacked([part[i] for part in back], back_ffn[1][i], back_ffn[2][i]).astype(f32) for i in range(3)
    )
    moments_new = jnp.stack(
        [
            beta_one * moments_old[0] + (1.0 - beta_one) * rotated,
            beta_two * moments_old[1] + (1.0 - beta_two) * rotated * rotated,
        ]
    )
    weights_new = weights - rate_mats * update
    return (
        output,
        grad_input,
        grad_weights,
        moments_new,
        weights_new,
        grad_small,
        jnp.stack([small_first, small_second]),
        small_new,
    )


def solution(mesh):
    rows = P(("dp", "fsdp"), None)
    blocks = P(("dp", "fsdp"), None, None)
    pair = P(None, ("dp", "fsdp"), None)
    return jax.shard_map(
        lambda *arrays: on_device(mesh, *arrays),
        mesh=mesh,
        in_specs=(blocks, blocks, P(("dp", "fsdp")), rows, P(), pair, P(), P(), P(), P()),
        out_specs=(blocks, blocks, rows, pair, rows, P(), P(), P()),
        check_vma=False,
    )
```

```python
import functools
import jax
import jax.numpy as jnp
from jax import lax
from jax.sharding import PartitionSpec as P
from jax.experimental import pallas as pl
from jax.experimental.pallas import tpu as pltpu

D = 512
HEADS = 4
FF = 1024
HD = 128
CTX = 1024
SLOTS = 1128
STEP = 10
PAD = 1152
RB = 384
NRB = PAD // RB
scaling = HD ** (-0.5)
eps_norm = 1e-05
eps_adam = 1e-08
beta_one = 0.9
beta_two = 0.999
rate_mats = 0.1
rate_small = 0.5
axes = ("dp", "fsdp")
bf16 = jnp.bfloat16
f32 = jnp.float32
VLIM_FWD = 58 * 1024 * 1024
VLIM_ROWS = 58 * 1024 * 1024
VLIM_BWD = 58 * 1024 * 1024
VLIM_STEP = 24 * 1024 * 1024


def nt(a, b):
    return lax.dot_general(a, b, (((1,), (1,)), ((), ())), preferred_element_type=f32)


def nn(a, b):
    return lax.dot_general(a, b, (((1,), (0,)), ((), ())), preferred_element_type=f32)


def tn(a, b):
    return lax.dot_general(a, b, (((0,), (0,)), ((), ())), preferred_element_type=f32)


def put_in_order(me, parts, out):
    def move(j, carry):
        for c, part in enumerate(parts):
            out[(j * len(parts) + c) ^ me] = part[j]
        return carry

    lax.fori_loop(0, parts[0].shape[0], move, 0)


def attn_fwd_body(xc_ref, xr_ref, w_ref, q_ref, k_ref, v_ref, e_ref, o_ref, li_ref, ve_ref):
    rb = pl.program_id(1)

    @pl.when(rb == 0)
    def _():
        xc = xc_ref[0]
        k_ref[0] = nt(xc, w_ref[:, 1].reshape(D, D)).astype(bf16)
        v_ref[0] = nt(xc, w_ref[:, 2].reshape(D, D)).astype(bf16)
        for h in range(HEADS):
            ve_ref[h, :, 0:HD] = v_ref[0, :, h * HD : (h + 1) * HD]
            ve_ref[h, :, HD : 2 * HD] = jnp.ones((CTX, HD), bf16)

    rows = rb * RB + lax.broadcasted_iota(jnp.int32, (RB, 1), 0)
    xr = jnp.where(rows < SLOTS, xr_ref[0].astype(f32), 0.0).astype(bf16)
    q_ref[0] = (nt(xr, w_ref[:, 0].reshape(D, D)) * scaling).astype(bf16)
    for h in range(HEADS):
        hs = slice(h * HD, (h + 1) * HD)
        s = nt(q_ref[0, :, hs], k_ref[0, :, hs])
        m = jnp.max(s, axis=-1, keepdims=True)
        e_ref[0, h] = jnp.exp(s - m).astype(bf16)
        ov = nn(e_ref[0, h], ve_ref[h])
        li = 1.0 / ov[:, HD:]
        lane = lax.broadcasted_iota(jnp.int32, (RB, HD), 1) // (HD // HEADS)
        scales = li if h == 0 else jnp.where(lane == h, li, scales)
        o_ref[0, :, hs] = (ov[:, :HD] * li).astype(bf16)
    li_ref[0] = scales


def attn_fwd(hood, x, wqkv, earlier=(), me=None):
    n = x.shape[0]
    sd = jax.ShapeDtypeStruct
    everything = lambda shape: pl.BlockSpec(shape, lambda i, r: (0,) * len(shape))
    if me is None:
        weights, wshape = [wqkv], wqkv.shape
    else:
        weights, wshape = list(wqkv), (2 * wqkv[0].shape[0],) + wqkv[0].shape[1:]
    n_w, n_e = len(weights), len(earlier)

    def body(*refs):
        if me is not None:
            me_ref, *refs = refs
            parts, placed = refs[2 : 2 + n_w], refs[-2]

            @pl.when(pl.program_id(1) == 0)
            def _():
                put_in_order(me_ref[0], parts, placed)

            refs = refs[:-2] + refs[-1:]
        else:
            placed = refs[2]
        attn_fwd_body(*refs[:2], placed, *refs[2 + n_w + n_e :])

    return pl.pallas_call(
        body,
        grid=(1, NRB),
        in_specs=([] if me is None else [pl.BlockSpec(memory_space=pltpu.SMEM)])
        + [
            pl.BlockSpec((1, CTX, D), lambda i, r: (hood, 0, 0)),
            pl.BlockSpec((1, RB, D), lambda i, r: (hood, r, 0)),
        ]
        + [everything(w.shape) for w in weights]
        + [pl.BlockSpec(memory_space=pl.ANY)] * n_e,
        out_specs=[
            pl.BlockSpec((1, RB, D), lambda i, r: (hood, r, 0)),
            pl.BlockSpec((1, CTX, D), lambda i, r: (hood, 0, 0)),
            pl.BlockSpec((1, CTX, D), lambda i, r: (hood, 0, 0)),
            pl.BlockSpec((1, HEADS, RB, CTX), lambda i, r: (hood, 0, r, 0)),
            pl.BlockSpec((1, RB, D), lambda i, r: (hood, r, 0)),
            pl.BlockSpec((1, RB, HD), lambda i, r: (hood, r, 0)),
        ]
        + ([] if me is None else [everything(wshape)]),
        out_shape=[
            sd((n, PAD, D), bf16),
            sd((n, CTX, D), bf16),
            sd((n, CTX, D), bf16),
            sd((n, HEADS, PAD, CTX), bf16),
            sd((n, PAD, D), bf16),
            sd((n, PAD, HD), f32),
        ]
        + ([] if me is None else [sd(wshape, bf16)]),
        scratch_shapes=[pltpu.VMEM((HEADS, CTX, 2 * HD), bf16)],
        input_output_aliases={2 + n_w + (me is not None) + i: i for i in range(n_e)},
        compiler_params=pltpu.CompilerParams(
            dimension_semantics=("arbitrary", "arbitrary"), vmem_limit_bytes=VLIM_FWD
        ),
        cost_estimate=pl.CostEstimate(
            flops=7_000_000_000, transcendentals=HEADS * PAD * CTX, bytes_accessed=20_000_000
        ),
        name="attention_forward",
    )(*([] if me is None else [me.reshape(1)]), x, x, *weights, *earlier)


def lane_mean(v):
    return jnp.sum(v, axis=-1, keepdims=True) * (1.0 / D)


NSUB = 1


def rows_body(ways, cnt_ref, x_ref, o_ref, li_ref, c_ref, *refs):
    parts, (sp_ref,
            out_ref, d1_ref, do_ref, go_out, gi_out, gb_out, gs_ref, go_ref, gi_ref, gb_ref,
            gbs, dus, dfs, hbs, das, osc, *placed) = refs[:ways], refs[ways:]
    w_ref = placed[0] if placed else parts[0]
    n, rb = pl.program_id(0), pl.program_id(1)
    first = jnp.logical_and(n == 0, rb == 0)

    @pl.when(first)
    def _():
        go_ref[...] = jnp.zeros_like(go_ref)
        gi_ref[...] = jnp.zeros_like(gi_ref)
        gb_ref[...] = jnp.zeros_like(gb_ref)
        gs_ref[...] = jnp.zeros_like(gs_ref)
        if placed:
            put_in_order(cnt_ref[cnt_ref.shape[0] - 1], parts, w_ref)

    per = w_ref.shape[1] // 5
    wo = w_ref[:, 0:per].reshape(D, D)
    wi = w_ref[:, per : 3 * per].reshape(FF, D)
    wb = w_ref[:, 3 * per :].reshape(FF, D)
    gain1, shift1 = sp_ref[0:1], sp_ref[1:2]
    bias2, gain2, shift2 = sp_ref[4:5], sp_ref[5:6], sp_ref[6:7]
    bias1 = jnp.concatenate([sp_ref[2:3], sp_ref[3:4]], axis=1)
    size = RB // NSUB
    sums = []

    def chain(part):
        rs = slice(part * size, (part + 1) * size)
        here = pl.ds(pl.multiple_of(rb * RB, RB) + part * size, size)
        osc[here] = o_ref[0, rs]
        rows = rb * RB + part * size + lax.broadcasted_iota(jnp.int32, (size, 1), 0)
        valid = rows < SLOTS
        live = rows < CTX + cnt_ref[n]
        at = nt(o_ref[0, rs], wo)
        yield
        r1 = jnp.where(valid, x_ref[0, rs].astype(f32), 0.0) + at
        c1 = r1 - lane_mean(r1)
        is1 = lax.rsqrt(lane_mean(c1 * c1) + eps_norm)
        xh1 = c1 * is1
        h = xh1 * gain1 + shift1
        hb = h.astype(bf16)
        hbs[here] = hb
        yield
        u = nt(hb, wi)
        yield
        u = u + bias1
        ex = jnp.exp2((-0.7213475204444817 * u) * u)
        t = 1.0 / (1.0 + 0.23164189 * jnp.abs(u))
        poly = t * (0.127414796 + t * (-0.142248368 + t * (0.7107068705 + t * (-0.7265760135 + t * 0.5307027145))))
        tail = poly * ex
        phi = jnp.where(u >= 0.0, 1.0 - tail, tail)
        gb = (u * phi).astype(bf16)
        gbs[here] = gb
        dgelu = phi + u * ex * 0.3989422804014327
        yield
        r2 = nn(gb, wb)
        yield
        r2 = h + r2 + bias2
        c2 = r2 - lane_mean(r2)
        is2 = lax.rsqrt(lane_mean(c2 * c2) + eps_norm)
        xh2 = c2 * is2
        out_ref[0, rs] = jnp.where(live, xh2 * gain2 + shift2, 0.0).astype(bf16)
        dy = jnp.where(live, c_ref[0, rs].astype(f32), 0.0)
        s5 = jnp.sum(dy * xh2, axis=0, keepdims=True)
        s6 = jnp.sum(dy, axis=0, keepdims=True)
        e2 = dy * gain2
        d2 = (e2 - lane_mean(e2) - xh2 * lane_mean(e2 * xh2)) * is2
        df = d2.astype(bf16)
        dfs[here] = df
        s4 = jnp.sum(df.astype(f32), axis=0, keepdims=True)
        yield
        dg = nt(df, wb)
        yield
        du = (dg * dgelu).astype(bf16)
        dus[here] = du
        s2 = jnp.sum(du.astype(f32), axis=0, keepdims=True)
        yield
        dh = nn(du, wi)
        yield
        dh = d2 + dh
        s0 = jnp.sum(dh * xh1, axis=0, keepdims=True)
        s1 = jnp.sum(dh, axis=0, keepdims=True)
        e1 = dh * gain1
        d1 = (e1 - lane_mean(e1) - xh1 * lane_mean(e1 * xh1)) * is1
        d1_ref[0, rs] = d1
        da = d1.astype(bf16)
        das[here] = da
        sums.append((s0, s1, s2[:, :D], s2[:, D:], s4, s5, s6))
        yield
        dm = nn(da, wo)
        yield
        for h in range(HEADS):
            hs = slice(h * HD, (h + 1) * HD)
            li = li_ref[0, rs, h * (HD // HEADS) : h * (HD // HEADS) + 1]
            do_ref[0, rs, hs] = (dm[:, hs] * li).astype(bf16)

    chains = [chain(i) for i in range(NSUB)]
    for i, c in enumerate(chains):
        for _ in range(len(chains) - 1 - i):
            next(c)
    done = 0
    while done < len(chains):
        done = 0
        for c in chains:
            try:
                next(c)
            except StopIteration:
                done += 1
    for i in range(7):
        total_i = sums[0][i]
        for s in sums[1:]:
            total_i = total_i + s[i]
        gs_ref[i : i + 1] += total_i

    @pl.when(rb == NRB - 1)
    def _():
        for target, whole, left, right in (
            (gb_ref, gb_out, gbs, dfs), (gi_ref, gi_out, dus, hbs), (go_ref, go_out, das, osc)
        ):
            grad = target[...] + tn(left[...], right[...])
            target[...] = grad
            whole[...] = grad.astype(bf16)


def rows_pass(counts, x, o, li, cot, rest, sp, me=None):
    n = x.shape[0]
    if me is None:
        rest, placed = [rest], []
    else:
        rest, placed = list(rest), [pltpu.VMEM((2 * rest[0].shape[0],) + rest[0].shape[1:], bf16)]
        counts = jnp.concatenate([counts, me.reshape(1)])
    sd = jax.ShapeDtypeStruct
    blk = pl.BlockSpec((1, RB, D), lambda i, r, c: (i, r, 0))
    const = lambda *s: pl.BlockSpec(s, lambda i, r, c: (0,) * len(s))
    return pl.pallas_call(
        functools.partial(rows_body, len(rest)),
        grid_spec=pltpu.PrefetchScalarGridSpec(
            num_scalar_prefetch=1,
            grid=(n, NRB),
            in_specs=[
                blk,
                blk,
                pl.BlockSpec((1, RB, HD), lambda i, r, c: (i, r, 0)),
                blk,
            ]
            + [const(*w.shape) for w in rest]
            + [const(8, D)],
            out_specs=[blk, blk, blk, const(D, D), const(FF, D), const(FF, D), const(8, D)],
            scratch_shapes=[
                pltpu.VMEM((D, D), f32),
                pltpu.VMEM((FF, D), f32),
                pltpu.VMEM((FF, D), f32),
                pltpu.VMEM((PAD, FF), bf16),
                pltpu.VMEM((PAD, FF), bf16),
                pltpu.VMEM((PAD, D), bf16),
                pltpu.VMEM((PAD, D), bf16),
                pltpu.VMEM((PAD, D), bf16),
                pltpu.VMEM((PAD, D), bf16),
            ]
            + placed,
        ),
        out_shape=[
            sd((n, SLOTS, D), bf16),
            sd((n, SLOTS, D), f32),
            sd((n, PAD, D), bf16),
            sd((D, D), bf16),
            sd((FF, D), bf16),
            sd((FF, D), bf16),
            sd((8, D), f32),
        ],
        compiler_params=pltpu.CompilerParams(
            dimension_semantics=("arbitrary", "arbitrary"), vmem_limit_bytes=VLIM_ROWS
        ),
        cost_estimate=pl.CostEstimate(
            flops=n * 18_000_000_000 // 2, transcendentals=n * PAD * FF * 2, bytes_accessed=n * 15_000_000
        ),
        name="rows_forward_backward",
    )(counts, x, o, li, cot, *rest, sp)


def attn_bwd_body(x_ref, q_ref, k_ref, v_ref, e_ref, o_ref, do_ref, acc_ref, w_ref,
                  gi_ref, gw_out, dq_ref, dkt_ref, dvt_ref, gw_ref):
    n = pl.program_id(0)

    @pl.when(n == 0)
    def _():
        gw_ref[...] = jnp.zeros_like(gw_ref)

    for h in range(2):
        hs = slice(h * HD, (h + 1) * HD)
        dkt = jnp.zeros((HD, CTX), f32)
        dvt = jnp.zeros((HD, CTX), f32)
        for rb in range(NRB):
            rs = slice(rb * RB, (rb + 1) * RB)
            do = do_ref[0, rs, hs]
            dof = do.astype(f32)
            t = jnp.sum(dof * o_ref[0, rs, hs].astype(f32), axis=-1, keepdims=True)
            dp = nt(do, v_ref[0, :, hs])
            e = e_ref[0, h, rs]
            ds = (e.astype(f32) * (dp - t)).astype(bf16)
            dq_ref[rs, hs] = nn(ds, k_ref[0, :, hs]).astype(bf16)
            dvt = dvt + tn(do, e)
            dkt = dkt + tn(q_ref[0, rs, hs], ds)
        dkt_ref[hs] = dkt.astype(bf16)
        dvt_ref[hs] = dvt.astype(bf16)
    xc = x_ref[0, 0:CTX]
    wq, wk, wv = (w_ref[:, i].reshape(2 * HD, D) for i in range(3))
    gw_ref[0] += (tn(dq_ref[0:CTX], xc) + tn(dq_ref[CTX:SLOTS], x_ref[0, CTX:SLOTS])) * scaling
    gw_ref[1] += nn(dkt_ref[...], xc)
    gw_ref[2] += nn(dvt_ref[...], xc)
    gi_ref[0, 0:CTX] = (
        acc_ref[0, 0:CTX]
        + nn(dq_ref[0:CTX], wq) * scaling
        + tn(dkt_ref[...], wk)
        + tn(dvt_ref[...], wv)
    )
    gi_ref[0, CTX:SLOTS] = acc_ref[0, CTX:SLOTS] + nn(dq_ref[CTX:SLOTS], wq) * scaling

    @pl.when(n == pl.num_programs(0) - 1)
    def _():
        gw_out[...] = gw_ref[...].astype(bf16)


def attn_bwd(pair, x, q, k, v, e, o, do, acc, wqkv):
    n = x.shape[0]
    sd = jax.ShapeDtypeStruct
    ways = wqkv.shape[0]
    if ways > 1:
        wspec = pl.BlockSpec((ways // 2,) + wqkv.shape[1:], lambda i: (pair, 0, 0, 0))
    else:
        wspec = pl.BlockSpec((1, 3, 2 * HD, D), lambda i: (0, 0, pair, 0))
    heads = lambda rows: pl.BlockSpec((1, rows, 2 * HD), lambda i: (i, 0, pair))
    whole = pl.BlockSpec((1, SLOTS, D), lambda i: (i, 0, 0))
    return pl.pallas_call(
        attn_bwd_body,
        grid=(n,),
        in_specs=[
            whole,
            heads(PAD),
            heads(CTX),
            heads(CTX),
            pl.BlockSpec((1, 2, PAD, CTX), lambda i: (i, pair, 0, 0)),
            heads(PAD),
            heads(PAD),
            whole,
            wspec,
        ],
        out_specs=[whole, pl.BlockSpec((3, 2 * HD, D), lambda i: (0, 0, 0))],
        out_shape=[sd((n, SLOTS, D), f32), sd((3, 2 * HD, D), bf16)],
        scratch_shapes=[
            pltpu.VMEM((PAD, 2 * HD), bf16),
            pltpu.VMEM((2 * HD, CTX), bf16),
            pltpu.VMEM((2 * HD, CTX), bf16),
            pltpu.VMEM((3, 2 * HD, D), f32),
        ],
        input_output_aliases={7: 0},
        compiler_params=pltpu.CompilerParams(
            dimension_semantics=("arbitrary",), vmem_limit_bytes=VLIM_BWD
        ),
        cost_estimate=pl.CostEstimate(
            flops=9_000_000_000, transcendentals=0, bytes_accessed=24_000_000
        ),
        name="attention_backward",
    )(x, q, k, v, e, o, do, acc, wqkv)


def adam_direction(first_new, second_new):
    return (first_new * (1.0 / (1.0 - beta_one**STEP))) / (
        jnp.sqrt(second_new * (1.0 / (1.0 - beta_two**STEP))) + eps_adam
    )


def rotate(grad, rows_basis, cols_basis, first_old, second_old):
    r = nn(tn(rows_basis, grad).astype(bf16), cols_basis)
    first_new = beta_one * first_old.astype(f32) + (1.0 - beta_one) * r
    second_new = beta_two * second_old.astype(f32) + (1.0 - beta_two) * r * r
    step = adam_direction(first_new, second_new).astype(bf16)
    return r.astype(bf16), nn(rows_basis, nt(step, cols_basis).astype(bf16)).astype(bf16)


def rotate_body(g_ref, a_ref, b_ref, m_ref, r_ref, u_ref):
    r_ref[...], u_ref[...] = rotate(g_ref[...], a_ref[...], b_ref[...], m_ref[0], m_ref[1])


def rotated_step(grad, rows_basis, cols_basis, moments):
    rows = grad.shape[0]
    sd = jax.ShapeDtypeStruct
    return pl.pallas_call(
        rotate_body,
        out_shape=[sd((rows, D), bf16), sd((rows, D), bf16)],
        compiler_params=pltpu.CompilerParams(vmem_limit_bytes=VLIM_STEP),
        cost_estimate=pl.CostEstimate(
            flops=4 * rows * D * (rows + D), transcendentals=rows * D, bytes_accessed=2 * rows * (rows + 5 * D)
        ),
        name="rotated_step",
    )(grad, rows_basis, cols_basis, moments)


def rotate_parts_body(me_ref, *refs):
    grads, a_ref, b_ref, olds, outs = refs[:2], refs[2], refs[3], refs[4:6], refs[6:10]
    g_ref, m_ref, r_ref, u_ref = refs[10:]
    me = me_ref[0]
    planes, inner, rows = len(outs), g_ref.shape[0], r_ref.shape[0]
    per = rows // (planes * inner)
    put_in_order(me & (inner - 1), grads, g_ref)
    put_in_order(me, olds, m_ref)
    r_ref[...], u_ref[...] = rotate(
        g_ref[...].reshape(rows, D), a_ref[...], b_ref[...],
        m_ref[:, 0].reshape(rows, D), m_ref[:, 1].reshape(rows, D),
    )
    n = g_ref.shape[1]
    for rel, out in enumerate(outs):
        row = pl.multiple_of((me ^ (rel * inner)) * per, per)
        out[0] = g_ref[row // n, pl.ds(pl.multiple_of(row % n, per), per)]
        out[1] = r_ref[pl.ds(row, per)]
        out[2] = u_ref[pl.ds(row, per)]


def rotated_step_parts(me, grads, rows_basis, cols_basis, olds, block):
    rows = rows_basis.shape[0]
    inner = 2 * grads[0].shape[0]
    count = 2 * olds[0].shape[0]
    per = rows // count
    full = lambda shape: pl.BlockSpec(shape, lambda i: (0,) * len(shape))
    return pl.pallas_call(
        rotate_parts_body,
        grid=(1,),
        in_specs=[pl.BlockSpec(memory_space=pltpu.SMEM)]
        + [full(g.shape) for g in grads]
        + [full(rows_basis.shape), full(cols_basis.shape)]
        + [pl.BlockSpec((count // 2, 2, per, D), lambda i: (0, 0, block, 0))] * 2,
        out_specs=[full((3, per, D))] * (count // inner),
        out_shape=[jax.ShapeDtypeStruct((3, per, D), bf16)] * (count // inner),
        scratch_shapes=[
            pltpu.VMEM((inner, rows // inner, D), bf16),
            pltpu.VMEM((count, 2, per, D), bf16),
            pltpu.VMEM((rows, D), bf16),
            pltpu.VMEM((rows, D), bf16),
        ],
        compiler_params=pltpu.CompilerParams(vmem_limit_bytes=VLIM_STEP),
        cost_estimate=pl.CostEstimate(
            flops=4 * rows * D * (rows + D), transcendentals=rows * D, bytes_accessed=2 * rows * (rows + 5 * D)
        ),
        name="rotated_step",
    )(me.reshape(1), *grads, rows_basis, cols_basis, *olds)


class Net:
    def __init__(self, mesh):
        self.count = mesh.size
        self.bits = self.count.bit_length() - 1
        self.inner_bits = self.bits - 2
        self.inner = 1 << self.inner_bits
        self.me = lax.axis_index(axes)
        self.local = self.me & (self.inner - 1)
        self.plane = self.me >> self.inner_bits
        stages = [(0, 1)]
        while stages[-1][0] + stages[-1][1] < self.inner_bits:
            low = stages[-1][0] + stages[-1][1]
            stages.append((low, min(2, self.inner_bits - low)))
        self.stages = stages
        self.top = (self.inner_bits, 2)

    def swap(self, value, offset, targets=None):
        pairs = [(i, i ^ offset) for i in range(self.count)]
        if targets is not None:
            pairs = [(i, j) for i, j in pairs if (j >> self.inner_bits) in targets]
        return lax.ppermute(value, axes, pairs)

    def digit(self, stage):
        return (self.me >> stage[0]) & ((1 << stage[1]) - 1)

    def collect(self, value, stage):
        return [value] + [self.swap(value, rel << stage[0]) for rel in range(1, 1 << stage[1])]

    def widen(self, value, stage):
        return interleave(self.collect(value, stage))

    def gather(self, value, stages):
        for stage in reversed(stages[1:]):
            value = self.widen(value, stage)
        return place(self.me, self.collect(value, stages[0]))

    def cut(self, pick, stage):
        mine = self.digit(stage)
        return [pick(mine ^ rel) for rel in range(1 << stage[1])]

    def trade(self, terms, stage, targets=None):
        return list(terms[:1]) + [
            self.swap(term, rel << stage[0], targets) for rel, term in enumerate(terms) if rel
        ]

    def exchange(self, pick, stage, targets=None):
        return self.trade(self.cut(pick, stage), stage, targets)


def after(value, *earlier):
    return lax.optimization_barrier((value, earlier))[0]


def interleave(parts):
    value = jnp.stack(parts, axis=1)
    return value.reshape((-1,) + value.shape[2:])


def total(parts):
    parts = [p.astype(f32) for p in parts]
    while len(parts) > 1:
        parts = [a + b for a, b in zip(parts[0::2], parts[1::2])]
    return parts[0]


def take_at(value, index, axis):
    return lax.dynamic_index_in_dim(value, index, axis, keepdims=False)


def split_high(value):
    high = lax.reduce_precision(value, 8, 7)
    return jnp.concatenate([high.astype(bf16), (value - high).astype(bf16)])


def join_high(pair):
    half = pair.shape[0] // 2
    return pair[:half].astype(f32) + pair[half:].astype(f32)


def reduce_cut(net, value, stage, extra=None):
    value = value.reshape(-1, 1 << stage[1], value.shape[1], D)

    def pick(d):
        part = take_at(value, d, 1).reshape(-1, D)
        return part if extra is None else jnp.concatenate([part, extra])

    return net.cut(pick, stage)


def reduce_sum(parts, rows, extra=0):
    kept = parts[0].shape[0] - extra
    summed = total([p[:kept] for p in parts]).astype(bf16).reshape(-1, rows, D)
    return (summed, split_high(total([join_high(p[kept:]) for p in parts]))) if extra else summed


def place_body(me_ref, *refs):
    *parts, out = refs
    put_in_order(me_ref[0] & (out.shape[0] - 1), parts, out)


def place(me, parts):
    size = len(parts) * parts[0].shape[0]
    shape = jax.ShapeDtypeStruct((size,) + parts[0].shape[1:], parts[0].dtype)
    return pl.pallas_call(
        place_body,
        in_specs=[pl.BlockSpec(memory_space=pltpu.SMEM)]
        + [pl.BlockSpec(memory_space=pltpu.VMEM)] * len(parts),
        out_specs=pl.BlockSpec(memory_space=pltpu.VMEM),
        out_shape=shape,
        compiler_params=pltpu.CompilerParams(vmem_limit_bytes=24 * 1024 * 1024),
        cost_estimate=pl.CostEstimate(flops=0, transcendentals=0, bytes_accessed=4 * shape.size),
        name="place",
    )(me.reshape(1), *parts)


def by_index(parts, index):
    return [
        functools.reduce(
            lambda rest, r: jnp.where(index == (b ^ r), parts[r], rest), range(1, len(parts)), parts[0]
        )
        for b in range(len(parts))
    ]


def on_device(mesh, features, cotangent, counts, weights, small_params, moments_old, small_moments,
              basis_attn, basis_ffn, basis_cols):
    net = Net(mesh)
    per = weights.shape[0] // 8
    everyone = net.stages + [net.top]

    def by_matrix(stacked):
        groups = stacked.reshape(per, 8, D)
        return (
            jnp.transpose(groups[:, 0:4], (1, 0, 2)),
            groups[:, 4:6].reshape(2 * per, D),
            groups[:, 6:8].reshape(2 * per, D),
        )

    def stacked(attn, inner, outer):
        return jnp.concatenate(
            [jnp.stack(attn, axis=1), inner.reshape(per, 2, D), outer.reshape(per, 2, D)], axis=1
        ).reshape(8 * per, D)

    inner = net.inner
    n_attn, n_ffn = D // inner, FF // inner
    ffn_of = lambda plane: jnp.clip(plane - 1, 0, 1)
    stages, top = net.stages, net.top

    own_attn, own_in, own_out = by_matrix(weights.astype(bf16))
    first = own_attn[None, 0:3]
    rest = jnp.concatenate([own_attn[3], own_in, own_out])[None]
    olds = [by_matrix(moments_old[i].astype(bf16)) for i in range(2)]
    old_attn = jnp.stack([m[0] for m in olds], axis=1)
    old_ffn = jnp.stack([jnp.stack([m[1], m[2]]) for m in olds], axis=1)
    old_terms = net.cut(
        lambda d: jnp.concatenate([take_at(old_ffn, ffn_of(d), 0), take_at(old_attn, d, 0)], axis=1), top
    )
    mine = ffn_of(net.plane)
    bases = (
        take_at(basis_attn, net.plane, 0).astype(bf16),
        take_at(basis_cols, net.plane, 0).astype(bf16),
        take_at(basis_ffn, mine, 0).astype(bf16),
        take_at(basis_cols, 4 + mine, 0).astype(bf16),
    )
    sp = jnp.concatenate([small_params.reshape(7, D), jnp.zeros((1, D), f32)])

    whole_tiles = per % 16 == 0
    order = list(reversed(everyone))
    first = interleave(net.collect(first, order[0]))
    rest_parts = net.collect(after(rest, first), order[0])
    for i, stage in enumerate(order[1:]):
        first_parts = net.collect(first, stage)
        if i == 0:
            first_parts, bases, old_terms = after((first_parts, bases, old_terms), first)
        if stage is not order[-1]:
            first = interleave(first_parts)
            rest_parts, first = after((rest_parts, first), first_parts)
            rest = interleave(rest_parts)
            rest_parts = net.collect(rest, stage)
    if whole_tiles:
        first_parts = after(first_parts, rest, bases, old_terms)
        *kept, wqkv = attn_fwd(0, features, first_parts, me=net.me)
    else:
        wqkv = jnp.transpose(place(net.me, first_parts), (1, 0, 2, 3)).reshape(1, 3, D, D)
        kept = attn_fwd(0, features, wqkv)
    rest = interleave(after(rest_parts, kept[4]))
    rest_parts = net.collect(rest, order[-1])
    old_parts = net.trade(after(old_terms, rest), top)
    kept = attn_fwd(1, features, after(wqkv, rest), kept)
    rest_parts, old_parts = after((rest_parts, old_parts), kept[4])
    olds = jnp.stack(old_parts)
    for stage in reversed(stages[2:]):
        olds = net.widen(olds, stage)
    old_parts = net.collect(olds, stages[1])
    q, k, v, e, o, li = kept
    if whole_tiles:
        rows_done = rows_pass(counts, features, o, li, cotangent, after(rest_parts, olds), sp, net.me)
    else:
        rest = place(net.me, rest_parts)
        rest = jnp.concatenate(
            [rest[:, lo * per : hi * per].reshape(-1, D) for lo, hi in ((0, 1), (1, 3), (3, 5))]
        )[None]
        rows_done = rows_pass(counts, features, o, li, cotangent, rest, sp)
    output, d1, do, go, gi, gb, gs = rows_done

    early = jnp.concatenate(
        [go.reshape(inner, -1, D), gi.reshape(inner, -1, D), gb.reshape(inner, -1, D)], axis=1
    )
    small = split_high(gs)
    n_small, n_early = small.shape[0], early.shape[1]
    terms = reduce_cut(net, early, stages[0], small)
    early_parts = net.trade(terms, stages[0])
    olds = interleave(after(old_parts, output))
    old_parts = net.collect(olds, stages[0])
    back = functools.partial(attn_bwd, x=features, q=q, k=k, v=v, e=e, o=o, do=do)
    acc, gw0 = back(0, acc=d1, wqkv=after(wqkv, terms, olds))
    early_parts, old_parts = after((early_parts, old_parts), gw0)
    early, small = reduce_sum(early_parts, n_early, n_small)
    for stage in stages[2:]:
        early, small = reduce_sum(net.trade(reduce_cut(net, early, stage, small), stage), n_early, n_small)
    terms = reduce_cut(net, early, stages[1], small)
    early_parts = net.trade(terms, stages[1])
    grad_input, gw1 = back(1, acc=acc, wqkv=after(wqkv, terms))

    late = jnp.concatenate([gw0, gw1], axis=1).reshape(3, inner, n_attn, D)
    late = jnp.transpose(late, (1, 0, 2, 3)).reshape(inner, 3 * n_attn, D)
    terms = reduce_cut(net, late, stages[0])
    late_parts = net.trade(terms, stages[0])

    early, small = reduce_sum(after(early_parts, terms), n_early, n_small)
    early = early.reshape(n_early, D)
    outs = jnp.stack(
        [
            early[n_attn : n_attn + n_ffn],
            early[n_attn + n_ffn :],
            jnp.concatenate([early[:n_attn], jnp.zeros((n_ffn - n_attn, D), bf16)]),
        ]
    )
    top_terms = net.cut(lambda d: jnp.concatenate([take_at(outs, jnp.maximum(d, 1) - 1, 0), small]), top)
    top_parts = net.trade(top_terms, top)
    late = reduce_sum(after(late_parts, top_terms), 3 * n_attn)
    for stage in stages[2:]:
        late = reduce_sum(net.trade(reduce_cut(net, late, stage), stage), 3 * n_attn)
    late_parts = net.trade(reduce_cut(net, late, stages[1]), stages[1])

    late = reduce_sum(late_parts, 3 * n_attn).reshape(3, n_attn, D)
    terms = net.cut(lambda d: take_at(late, jnp.minimum(d, 2), 0), top)
    late_parts = net.trade(terms, top, (0, 1, 2))
    top_parts = after(top_parts, terms)
    ffn = total([p[:n_ffn] for p in top_parts]).astype(bf16)
    ffn_parts = net.collect(ffn[None], stages[-1])
    late_parts, ffn = after((late_parts, ffn), ffn)
    attn = total(late_parts).astype(bf16)
    attn = jnp.where(net.plane == 3, ffn[:n_attn], attn)[None]
    for stage in reversed(stages[1:]):
        attn_parts = net.collect(attn, stage)
        ffn = interleave(after(ffn_parts, attn))
        ffn_parts = net.collect(ffn, stages[stages.index(stage) - 1])
        attn = interleave(after(attn_parts, ffn))
    attn_parts = net.collect(attn, stages[0])

    if whole_tiles:
        back_attn = rotated_step_parts(net.me, attn_parts, bases[0], bases[1], old_parts, 2)
        back_ffn = rotated_step_parts(net.me, ffn_parts, bases[2], bases[3], old_parts, 0)
    else:
        olds = jnp.transpose(place(net.me, old_parts), (1, 0, 2, 3))
        attn = place(net.me, attn_parts).reshape(D, D)
        ffn = place(net.me, ffn_parts).reshape(FF, D)
        both = rotated_step(attn, bases[0], bases[1], olds[:, :, 2 * per :].reshape(2, D, D))
        back_attn = take_at(jnp.stack([attn, *both]).reshape(3, 4, inner, per, D), net.local, 2)
        back_attn = net.cut(lambda d: take_at(back_attn, d, 1), top)
        both = rotated_step(ffn, bases[2], bases[3], olds[:, :, : 2 * per].reshape(2, FF, D))
        back_ffn = take_at(jnp.stack([ffn, *both]).reshape(3, 4, inner, 2 * per, D), net.local, 2)
        back_ffn = net.cut(lambda d: take_at(back_ffn, d, 1), top)
    back_attn = by_index(net.trade(back_attn, top), net.plane)
    back_ffn = by_index(net.trade(back_ffn, top), net.plane)
    gs = total([join_high(p[n_ffn:]) for p in top_parts])
    grad_small = gs[0:7].reshape(-1)
    small_first = beta_one * small_moments[0] + (1.0 - beta_one) * grad_small
    small_second = beta_two * small_moments[1] + (1.0 - beta_two) * grad_small * grad_small
    small_new = small_params - rate_small * adam_direction(small_first, small_second)
    grad_weights, rotated, update = (
        stacked([part[i] for part in back_attn], back_ffn[1][i], back_ffn[2][i]).astype(f32) for i in range(3)
    )
    moments_new = jnp.stack(
        [
            beta_one * moments_old[0] + (1.0 - beta_one) * rotated,
            beta_two * moments_old[1] + (1.0 - beta_two) * rotated * rotated,
        ]
    )
    weights_new = weights - rate_mats * update
    return (
        output,
        grad_input,
        grad_weights,
        moments_new,
        weights_new,
        grad_small,
        jnp.stack([small_first, small_second]),
        small_new,
    )


def solution(mesh):
    rows = P(("dp", "fsdp"), None)
    blocks = P(("dp", "fsdp"), None, None)
    pair = P(None, ("dp", "fsdp"), None)
    return jax.shard_map(
        lambda *arrays: on_device(mesh, *arrays),
        mesh=mesh,
        in_specs=(blocks, blocks, P(("dp", "fsdp")), rows, P(), pair, P(), P(), P(), P()),
        out_specs=(blocks, blocks, rows, pair, rows, P(), P(), P()),
        check_vma=False,
    )
```

```python
import functools
import jax
import jax.numpy as jnp
from jax import lax
from jax.sharding import PartitionSpec as P
from jax.experimental import pallas as pl
from jax.experimental.pallas import tpu as pltpu

D = 512
HEADS = 4
FF = 1024
HD = 128
CTX = 1024
SLOTS = 1128
STEP = 10
PAD = 1152
RB = 384
NRB = PAD // RB
RBL = 576
SUB = 128
NRBL = PAD // RBL
scaling = HD ** (-0.5)
eps_norm = 1e-05
eps_adam = 1e-08
beta_one = 0.9
beta_two = 0.999
rate_mats = 0.1
rate_small = 0.5
axes = ("dp", "fsdp")
bf16 = jnp.bfloat16
f32 = jnp.float32
VLIM_FWD = 58 * 1024 * 1024
VLIM_ROWS = 46 * 1024 * 1024
VLIM_BWD = 46 * 1024 * 1024
VLIM_STEP = 24 * 1024 * 1024


def nt(a, b):
    return lax.dot_general(a, b, (((1,), (1,)), ((), ())), preferred_element_type=f32)


def nn(a, b):
    return lax.dot_general(a, b, (((1,), (0,)), ((), ())), preferred_element_type=f32)


def tn(a, b):
    return lax.dot_general(a, b, (((0,), (0,)), ((), ())), preferred_element_type=f32)


def put_in_order(me, parts, out):
    def move(j, carry):
        for c, part in enumerate(parts):
            out[(j * len(parts) + c) ^ me] = part[j]
        return carry

    lax.fori_loop(0, parts[0].shape[0], move, 0)


def attn_fwd_body(ways, *refs):
    me_ref, xc_ref, xr_ref, *refs = refs
    parts, (q_ref, k_ref, v_ref, e_ref, o_ref, li_ref, w_ref, ve_ref) = refs[:ways], refs[ways:]
    n, rb = pl.program_id(0), pl.program_id(1)

    @pl.when(jnp.logical_and(n == 0, rb == 0))
    def _():
        put_in_order(me_ref[0] & (w_ref.shape[0] - 1), parts, w_ref)

    @pl.when(rb == 0)
    def _():
        xc = xc_ref[0]
        k_ref[0] = nt(xc, w_ref[:, 1].reshape(D, D)).astype(bf16)
        v_ref[0] = nt(xc, w_ref[:, 2].reshape(D, D)).astype(bf16)
        for h in range(HEADS):
            ve_ref[h, :, 0:HD] = v_ref[0, :, h * HD : (h + 1) * HD]
            ve_ref[h, :, HD : 2 * HD] = jnp.ones((CTX, HD), bf16)

    rows = rb * RB + lax.broadcasted_iota(jnp.int32, (RB, 1), 0)
    xr = jnp.where(rows < SLOTS, xr_ref[0].astype(f32), 0.0).astype(bf16)
    q_ref[0] = (nt(xr, w_ref[:, 0].reshape(D, D)) * scaling).astype(bf16)
    lane = lax.broadcasted_iota(jnp.int32, (SUB, HD), 1) // (HD // HEADS)
    for r in range(0, RB, SUB):
        rs = slice(r, r + SUB)
        for h in range(HEADS):
            hs = slice(h * HD, (h + 1) * HD)
            s = nt(q_ref[0, rs, hs], k_ref[0, :, hs])
            m = jnp.max(s, axis=-1, keepdims=True)
            e = jnp.exp(s - m).astype(bf16)
            e_ref[0, h, rs] = e
            ov = nn(e, ve_ref[h])
            li = 1.0 / ov[:, HD:]
            scales = li if h == 0 else jnp.where(lane == h, li, scales)
            o_ref[0, rs, hs] = (ov[:, :HD] * li).astype(bf16)
        li_ref[0, rs] = scales


def attn_fwd(x, parts, me):
    n = x.shape[0]
    sd = jax.ShapeDtypeStruct
    everything = lambda shape: pl.BlockSpec(shape, lambda i, r: (0,) * len(shape))
    wshape = (len(parts) * parts[0].shape[0],) + parts[0].shape[1:]
    block = lambda w: pl.BlockSpec((1, RB, w), lambda i, r: (i, r, 0))
    context = pl.BlockSpec((1, CTX, D), lambda i, r: (i, 0, 0))
    return pl.pallas_call(
        functools.partial(attn_fwd_body, len(parts)),
        grid=(n, NRB),
        in_specs=[pl.BlockSpec(memory_space=pltpu.SMEM), context, block(D)]
        + [everything(w.shape) for w in parts],
        out_specs=[
            block(D),
            context,
            context,
            pl.BlockSpec((1, HEADS, RB, CTX), lambda i, r: (i, 0, r, 0)),
            block(D),
            block(HD),
            everything(wshape),
        ],
        out_shape=[
            sd((n, PAD, D), bf16),
            sd((n, CTX, D), bf16),
            sd((n, CTX, D), bf16),
            sd((n, HEADS, PAD, CTX), bf16),
            sd((n, PAD, D), bf16),
            sd((n, PAD, HD), f32),
            sd(wshape, bf16),
        ],
        scratch_shapes=[pltpu.VMEM((HEADS, CTX, 2 * HD), bf16)],
        compiler_params=pltpu.CompilerParams(
            dimension_semantics=("arbitrary", "arbitrary"), vmem_limit_bytes=VLIM_FWD
        ),
        cost_estimate=pl.CostEstimate(
            flops=14_000_000_000, transcendentals=n * HEADS * PAD * CTX, bytes_accessed=40_000_000
        ),
        name="attention_forward",
    )(me.reshape(1), x, x, *parts)


def lane_mean(v):
    return jnp.sum(v, axis=-1, keepdims=True) * (1.0 / D)


NSUB = 1


def rows_body(ways, cnt_ref, x_ref, o_ref, li_ref, c_ref, *refs):
    parts, (sp_ref,
            out_ref, d1_ref, do_ref, keep_ref, send_ref, gs_ref, go_ref, gi_ref, gb_ref,
            gbs, dus, dfs, hbs, das, osc, *placed) = refs[:ways], refs[ways:]
    w_ref = placed[0] if placed else parts[0]
    me = cnt_ref[cnt_ref.shape[0] - 1]
    pieces, small = 2 * keep_ref.shape[0], 2 * gs_ref.shape[0]
    n, rb = pl.program_id(0), pl.program_id(1)
    first = jnp.logical_and(n == 0, rb == 0)
    last = jnp.logical_and(n == pl.num_programs(0) - 1, rb == NRBL - 1)

    @pl.when(first)
    def _():
        go_ref[...] = jnp.zeros_like(go_ref)
        gi_ref[...] = jnp.zeros_like(gi_ref)
        gb_ref[...] = jnp.zeros_like(gb_ref)
        gs_ref[...] = jnp.zeros_like(gs_ref)
        if placed:
            put_in_order(me, parts, w_ref)

    per = w_ref.shape[1] // 5
    wo = w_ref[:, 0:per].reshape(D, D)
    wi = w_ref[:, per : 3 * per].reshape(FF, D)
    wb = w_ref[:, 3 * per :].reshape(FF, D)
    gain1, shift1 = sp_ref[0:1], sp_ref[1:2]
    bias2, gain2, shift2 = sp_ref[4:5], sp_ref[5:6], sp_ref[6:7]
    bias1 = jnp.concatenate([sp_ref[2:3], sp_ref[3:4]], axis=1)
    size = RBL // NSUB
    sums = []

    def chain(part):
        rs = slice(part * size, (part + 1) * size)
        here = pl.ds(pl.multiple_of(rb * RBL, RBL) + part * size, size)
        osc[here] = o_ref[0, rs]
        rows = rb * RBL + part * size + lax.broadcasted_iota(jnp.int32, (size, 1), 0)
        valid = rows < SLOTS
        live = rows < CTX + cnt_ref[n]
        at = nt(o_ref[0, rs], wo)
        yield
        r1 = jnp.where(valid, x_ref[0, rs].astype(f32), 0.0) + at
        c1 = r1 - lane_mean(r1)
        is1 = lax.rsqrt(lane_mean(c1 * c1) + eps_norm)
        xh1 = c1 * is1
        h = xh1 * gain1 + shift1
        hb = h.astype(bf16)
        hbs[here] = hb
        yield
        u = nt(hb, wi)
        yield
        u = u + bias1
        ex = jnp.exp2((-0.7213475204444817 * u) * u)
        t = 1.0 / (1.0 + 0.23164189 * jnp.abs(u))
        poly = t * (0.127414796 + t * (-0.142248368 + t * (0.7107068705 + t * (-0.7265760135 + t * 0.5307027145))))
        tail = poly * ex
        phi = jnp.where(u >= 0.0, 1.0 - tail, tail)
        gb = (u * phi).astype(bf16)
        gbs[here] = gb
        dgelu = phi + u * ex * 0.3989422804014327
        yield
        r2 = nn(gb, wb)
        yield
        r2 = h + r2 + bias2
        c2 = r2 - lane_mean(r2)
        is2 = lax.rsqrt(lane_mean(c2 * c2) + eps_norm)
        xh2 = c2 * is2
        out_ref[0, rs] = jnp.where(live, xh2 * gain2 + shift2, 0.0).astype(bf16)
        dy = jnp.where(live, c_ref[0, rs].astype(f32), 0.0)
        s5 = jnp.sum(dy * xh2, axis=0, keepdims=True)
        s6 = jnp.sum(dy, axis=0, keepdims=True)
        e2 = dy * gain2
        d2 = (e2 - lane_mean(e2) - xh2 * lane_mean(e2 * xh2)) * is2
        df = d2.astype(bf16)
        dfs[here] = df
        s4 = jnp.sum(df.astype(f32), axis=0, keepdims=True)
        yield
        dg = nt(df, wb)
        yield
        du = (dg * dgelu).astype(bf16)
        dus[here] = du
        s2 = jnp.sum(du.astype(f32), axis=0, keepdims=True)
        yield
        dh = nn(du, wi)
        yield
        dh = d2 + dh
        s0 = jnp.sum(dh * xh1, axis=0, keepdims=True)
        s1 = jnp.sum(dh, axis=0, keepdims=True)
        e1 = dh * gain1
        d1 = (e1 - lane_mean(e1) - xh1 * lane_mean(e1 * xh1)) * is1
        d1_ref[0, rs] = d1
        da = d1.astype(bf16)
        das[here] = da
        sums.append((s0, s1, s2[:, :D], s2[:, D:], s4, s5, s6))
        yield
        dm = nn(da, wo)
        yield
        for h in range(HEADS):
            hs = slice(h * HD, (h + 1) * HD)
            li = li_ref[0, rs, h * (HD // HEADS) : h * (HD // HEADS) + 1]
            do_ref[0, rs, hs] = (dm[:, hs] * li).astype(bf16)

    chains = [chain(i) for i in range(NSUB)]
    for i, c in enumerate(chains):
        for _ in range(len(chains) - 1 - i):
            next(c)
    done = 0
    while done < len(chains):
        done = 0
        for c in chains:
            try:
                next(c)
            except StopIteration:
                done += 1
    for i in range(7):
        total_i = sums[0][i]
        for s in sums[1:]:
            total_i = total_i + s[i]
        gs_ref[i : i + 1] += total_i

    @pl.when(rb == NRBL - 1)
    def _():
        for target, left, right in ((gi_ref, dus, hbs), (gb_ref, gbs, dfs), (go_ref, das, osc)):
            target[...] += tn(left[...], right[...])

    def write(core):
        for p in range(pieces):
            out = keep_ref if p % 2 == core else send_ref
            if p < 2:
                high = gs_ref[...].astype(bf16)
                out[0, : small // 2] = high
                out[0, small // 2 : small] = (gs_ref[...] - high.astype(f32)).astype(bf16)
            else:
                out[p // 2, :small] = jnp.zeros((small, D), bf16)
            at = small
            for target in (gi_ref, gb_ref, go_ref):
                size = target.shape[0] // pieces
                out[p // 2, at : at + size] = target[p * size : (p + 1) * size].astype(bf16)
                at += size

    for core in range(2):
        pl.when(jnp.logical_and(last, me % 2 == core))(functools.partial(write, core))


def rows_pass(counts, x, o, li, cot, rest, sp, me, pieces):
    n = x.shape[0]
    placed = []
    if len(rest) > 1:
        placed = [pltpu.VMEM((2 * rest[0].shape[0],) + rest[0].shape[1:], bf16)]
    counts = jnp.concatenate([counts, me.reshape(1)])
    cut = (pieces // 2, 16 + (D + 2 * FF) // pieces, D)
    sd = jax.ShapeDtypeStruct
    blk = pl.BlockSpec((1, RBL, D), lambda i, r, c: (i, r, 0))
    const = lambda *s: pl.BlockSpec(s, lambda i, r, c: (0,) * len(s))
    return pl.pallas_call(
        functools.partial(rows_body, len(rest)),
        grid_spec=pltpu.PrefetchScalarGridSpec(
            num_scalar_prefetch=1,
            grid=(n, NRBL),
            in_specs=[
                blk,
                blk,
                pl.BlockSpec((1, RBL, HD), lambda i, r, c: (i, r, 0)),
                blk,
            ]
            + [const(*w.shape) for w in rest]
            + [const(8, D)],
            out_specs=[blk, blk, blk, const(*cut), const(*cut)],
            scratch_shapes=[
                pltpu.VMEM((8, D), f32),
                pltpu.VMEM((D, D), f32),
                pltpu.VMEM((FF, D), f32),
                pltpu.VMEM((FF, D), f32),
                pltpu.VMEM((PAD, FF), bf16),
                pltpu.VMEM((PAD, FF), bf16),
                pltpu.VMEM((PAD, D), bf16),
                pltpu.VMEM((PAD, D), bf16),
                pltpu.VMEM((PAD, D), bf16),
                pltpu.VMEM((PAD, D), bf16),
            ]
            + placed,
        ),
        out_shape=[
            sd((n, SLOTS, D), bf16),
            sd((n, SLOTS, D), f32),
            sd((n, PAD, D), bf16),
            sd(cut, bf16),
            sd(cut, bf16),
        ],
        compiler_params=pltpu.CompilerParams(
            dimension_semantics=("arbitrary", "arbitrary"), vmem_limit_bytes=VLIM_ROWS
        ),
        cost_estimate=pl.CostEstimate(
            flops=n * 18_000_000_000 // 2, transcendentals=n * PAD * FF * 2, bytes_accessed=n * 15_000_000
        ),
        name="rows_forward_backward",
    )(counts, x, o, li, cot, *rest, sp)


def attn_bwd_body(cut, *refs):
    x_ref, q_ref, k_ref, v_ref, e_ref, o_ref, do_ref, acc_ref, w_ref, *refs = refs
    (me_ref, other_ref), refs = (refs[:2], refs[2:]) if cut else ((None, None), refs)
    gi_ref, *outs = refs[:-4]
    dkt_ref, dvt_ref, gw_ref, xs_ref = refs[-4:]
    n, rb = pl.program_id(0), pl.program_id(1)

    @pl.when(jnp.logical_and(n == 0, rb == 0))
    def _():
        gw_ref[...] = jnp.zeros_like(gw_ref)

    @pl.when(rb == 0)
    def _():
        dkt_ref[...] = jnp.zeros_like(dkt_ref)
        dvt_ref[...] = jnp.zeros_like(dvt_ref)

    rows = rb * RBL + lax.broadcasted_iota(jnp.int32, (RBL, 1), 0)
    x = jnp.where(rows < SLOTS, x_ref[0].astype(f32), 0.0).astype(bf16)
    here = pl.ds(pl.multiple_of(rb * RBL, RBL), RBL)
    xs_ref[here] = x
    dqs = []
    for h in range(2):
        hs = slice(h * HD, (h + 1) * HD)
        do = do_ref[0, :, hs]
        t = jnp.sum(do.astype(f32) * o_ref[0, :, hs].astype(f32), axis=-1, keepdims=True)
        dp = nt(do, v_ref[0, :, hs])
        e = e_ref[0, h]
        ds = (e.astype(f32) * (dp - t)).astype(bf16)
        dqs.append(nn(ds, k_ref[0, :, hs]).astype(bf16))
        dvt_ref[hs] += tn(do, e)
        dkt_ref[hs] += tn(q_ref[0, :, hs], ds)
    dq = jnp.concatenate(dqs, axis=1)
    wq, wk, wv = (w_ref[:, i].reshape(2 * HD, D) for i in range(3))
    gw_ref[0] += tn(dq, x) * scaling
    gi_ref[0, here] = acc_ref[0] + nn(dq, wq) * scaling

    @pl.when(rb == NRBL - 1)
    def _():
        dkt, dvt = dkt_ref[...].astype(bf16), dvt_ref[...].astype(bf16)
        xc = xs_ref[0:CTX]
        gw_ref[1] += nn(dkt, xc)
        gw_ref[2] += nn(dvt, xc)
        gi_ref[0, 0:CTX] += tn(dkt, wk) + tn(dvt, wv)

    last = jnp.logical_and(n == pl.num_programs(0) - 1, rb == NRBL - 1)
    if not cut:

        @pl.when(last)
        def _():
            outs[0][...] = gw_ref[...]

        return

    def write(core):
        pieces, size = 2 * outs[0].shape[0], outs[0].shape[2]
        for p in range(pieces):
            out = outs[0] if p % 2 == core else outs[1]
            half, row = divmod(p * size, 2 * HD)
            for i in range(3):
                out[p // 2, i] = (gw_ref if half else other_ref)[i, row : row + size].astype(bf16)

    for core in range(2):
        pl.when(jnp.logical_and(last, me_ref[0] % 2 == core))(functools.partial(write, core))


def attn_bwd(pair, x, q, k, v, e, o, do, acc, wqkv, cut=()):
    n = x.shape[0]
    sd = jax.ShapeDtypeStruct
    ways = wqkv.shape[0]
    if ways > 1:
        wspec = pl.BlockSpec((ways // 2,) + wqkv.shape[1:], lambda i, r: (pair, 0, 0, 0))
    else:
        wspec = pl.BlockSpec((1, 3, 2 * HD, D), lambda i, r: (0, 0, pair, 0))
    heads = pl.BlockSpec((1, RBL, 2 * HD), lambda i, r: (i, r, pair))
    context = pl.BlockSpec((1, CTX, 2 * HD), lambda i, r: (i, 0, pair))
    rows = pl.BlockSpec((1, RBL, D), lambda i, r: (i, r, 0))
    grads = lambda shape: pl.BlockSpec(shape, lambda i, r: (0,) * len(shape))
    outs = [sd((cut[2] // 2, 3, D // cut[2], D), bf16)] * 2 if cut else [sd((3, 2 * HD, D), f32)]
    return pl.pallas_call(
        functools.partial(attn_bwd_body, bool(cut)),
        grid=(n, NRBL),
        in_specs=[
            rows,
            heads,
            context,
            context,
            pl.BlockSpec((1, 2, RBL, CTX), lambda i, r: (i, pair, r, 0)),
            heads,
            heads,
            rows,
            wspec,
        ]
        + ([pl.BlockSpec(memory_space=pltpu.SMEM), grads((3, 2 * HD, D))] if cut else []),
        out_specs=[pl.BlockSpec((1, PAD, D), lambda i, r: (i, 0, 0))] + [grads(g.shape) for g in outs],
        out_shape=[sd((n, SLOTS, D), f32)] + outs,
        scratch_shapes=[
            pltpu.VMEM((2 * HD, CTX), f32),
            pltpu.VMEM((2 * HD, CTX), f32),
            pltpu.VMEM((3, 2 * HD, D), f32),
            pltpu.VMEM((PAD, D), bf16),
        ],
        input_output_aliases={7: 0},
        compiler_params=pltpu.CompilerParams(
            dimension_semantics=("arbitrary", "arbitrary"), vmem_limit_bytes=VLIM_BWD
        ),
        cost_estimate=pl.CostEstimate(
            flops=9_000_000_000, transcendentals=0, bytes_accessed=24_000_000
        ),
        name="attention_backward",
    )(x, q, k, v, e, o, do, acc, wqkv, *([cut[0].reshape(1), cut[1]] if cut else []))


def adam_direction(first_new, second_new):
    return (first_new * (1.0 / (1.0 - beta_one**STEP))) / (
        jnp.sqrt(second_new * (1.0 / (1.0 - beta_two**STEP))) + eps_adam
    )


def rotate(grad, rows_basis, cols_basis, first_old, second_old):
    r = nn(tn(rows_basis, grad).astype(bf16), cols_basis)
    first_new = beta_one * first_old.astype(f32) + (1.0 - beta_one) * r
    second_new = beta_two * second_old.astype(f32) + (1.0 - beta_two) * r * r
    step = adam_direction(first_new, second_new).astype(bf16)
    return r.astype(bf16), nn(rows_basis, nt(step, cols_basis).astype(bf16)).astype(bf16)


def rotate_body(g_ref, a_ref, b_ref, m_ref, r_ref, u_ref):
    r_ref[...], u_ref[...] = rotate(g_ref[...], a_ref[...], b_ref[...], m_ref[0], m_ref[1])


def rotated_step(grad, rows_basis, cols_basis, moments):
    rows = grad.shape[0]
    sd = jax.ShapeDtypeStruct
    return pl.pallas_call(
        rotate_body,
        out_shape=[sd((rows, D), bf16), sd((rows, D), bf16)],
        compiler_params=pltpu.CompilerParams(vmem_limit_bytes=VLIM_STEP),
        cost_estimate=pl.CostEstimate(
            flops=4 * rows * D * (rows + D), transcendentals=rows * D, bytes_accessed=2 * rows * (rows + 5 * D)
        ),
        name="rotated_step",
    )(grad, rows_basis, cols_basis, moments)


def rotate_parts_body(me_ref, *refs):
    grads, a_ref, b_ref, olds, outs = refs[:2], refs[2], refs[3], refs[4:6], refs[6:10]
    g_ref, m_ref, r_ref, u_ref = refs[10:]
    me = me_ref[0]
    planes, inner, rows = len(outs), g_ref.shape[0], r_ref.shape[0]
    per = rows // (planes * inner)
    put_in_order(me & (inner - 1), grads, g_ref)
    put_in_order(me, olds, m_ref)
    r_ref[...], u_ref[...] = rotate(
        g_ref[...].reshape(rows, D), a_ref[...], b_ref[...],
        m_ref[:, 0].reshape(rows, D), m_ref[:, 1].reshape(rows, D),
    )
    n = g_ref.shape[1]
    for rel, out in enumerate(outs):
        row = pl.multiple_of((me ^ (rel * inner)) * per, per)
        out[0] = g_ref[row // n, pl.ds(pl.multiple_of(row % n, per), per)]
        out[1] = r_ref[pl.ds(row, per)]
        out[2] = u_ref[pl.ds(row, per)]


def rotated_step_parts(me, grads, rows_basis, cols_basis, olds, block):
    rows = rows_basis.shape[0]
    inner = 2 * grads[0].shape[0]
    count = 2 * olds[0].shape[0]
    per = rows // count
    full = lambda shape: pl.BlockSpec(shape, lambda i: (0,) * len(shape))
    return pl.pallas_call(
        rotate_parts_body,
        grid=(1,),
        in_specs=[pl.BlockSpec(memory_space=pltpu.SMEM)]
        + [full(g.shape) for g in grads]
        + [full(rows_basis.shape), full(cols_basis.shape)]
        + [pl.BlockSpec((count // 2, 2, per, D), lambda i: (0, 0, block, 0))] * 2,
        out_specs=[full((3, per, D))] * (count // inner),
        out_shape=[jax.ShapeDtypeStruct((3, per, D), bf16)] * (count // inner),
        scratch_shapes=[
            pltpu.VMEM((inner, rows // inner, D), bf16),
            pltpu.VMEM((count, 2, per, D), bf16),
            pltpu.VMEM((rows, D), bf16),
            pltpu.VMEM((rows, D), bf16),
        ],
        compiler_params=pltpu.CompilerParams(vmem_limit_bytes=VLIM_STEP),
        cost_estimate=pl.CostEstimate(
            flops=4 * rows * D * (rows + D), transcendentals=rows * D, bytes_accessed=2 * rows * (rows + 5 * D)
        ),
        name="rotated_step",
    )(me.reshape(1), *grads, rows_basis, cols_basis, *olds)


class Net:
    def __init__(self, mesh):
        self.count = mesh.size
        self.bits = self.count.bit_length() - 1
        self.inner_bits = self.bits - 2
        self.inner = 1 << self.inner_bits
        self.me = lax.axis_index(axes)
        self.local = self.me & (self.inner - 1)
        self.plane = self.me >> self.inner_bits
        stages = [(0, 1)]
        while stages[-1][0] + stages[-1][1] < self.inner_bits:
            low = stages[-1][0] + stages[-1][1]
            stages.append((low, min(2, self.inner_bits - low)))
        self.stages = stages
        self.top = (self.inner_bits, 2)

    def swap(self, value, offset, targets=(0, 1, 2, 3), sources=(0, 1, 2, 3)):
        pairs = [(i, i ^ offset) for i in range(self.count)]
        pairs = [
            (i, j) for i, j in pairs
            if (i >> self.inner_bits) in sources and (j >> self.inner_bits) in targets
        ]
        return lax.ppermute(value, axes, pairs)

    def digit(self, stage):
        return (self.me >> stage[0]) & ((1 << stage[1]) - 1)

    def collect(self, value, stage):
        return [value] + [self.swap(value, rel << stage[0]) for rel in range(1, 1 << stage[1])]

    def widen(self, value, stage):
        return interleave(self.collect(value, stage))

    def cut(self, pick, stage):
        mine = self.digit(stage)
        return [pick(mine ^ rel) for rel in range(1 << stage[1])]

    def trade(self, terms, stage, targets=(0, 1, 2, 3), sources=(0, 1, 2, 3)):
        return list(terms[:1]) + [
            self.swap(term, rel << stage[0], targets, sources) for rel, term in enumerate(terms) if rel
        ]


def after(value, *earlier):
    return lax.optimization_barrier((value, earlier))[0]


def interleave(parts):
    value = jnp.stack(parts, axis=1)
    return value.reshape((-1,) + value.shape[2:])


def total(parts):
    parts = [p.astype(f32) for p in parts]
    while len(parts) > 1:
        parts = [a + b for a, b in zip(parts[0::2], parts[1::2])]
    return parts[0]


def take_at(value, index, axis):
    return lax.dynamic_index_in_dim(value, index, axis, keepdims=False)


def join_high(pair):
    half = pair.shape[0] // 2
    return pair[:half].astype(f32) + pair[half:].astype(f32)


def sum_cut_body(low, bits, small, me_ref, *refs):
    size = 1 << bits
    parts, terms = refs[:-size], refs[-size:]
    digit = (me_ref[0] >> low) & (size - 1)
    if small:
        whole = total([join_high(p[0, :small]) for p in parts])
        high = whole.astype(bf16)
        pair = jnp.concatenate([high, (whole - high.astype(f32)).astype(bf16)])
    for rel, term in enumerate(terms):
        for j in range(term.shape[0]):
            piece = j * size + (digit ^ rel)
            if small:
                term[j, :small] = pair
                term[j, small:] = total([p[piece, small:] for p in parts]).astype(bf16)
            else:
                term[j] = total([p[piece] for p in parts]).astype(bf16)


def sum_top_body(low, small, me_ref, *refs):
    parts, terms = refs[:-4], refs[-4:]
    plane = (me_ref[0] >> low) & 3
    for rel, term in enumerate(terms):
        goal = plane ^ rel
        if not small:
            piece = jnp.minimum(goal, 2)
            term[...] = total([p[0, piece] for p in parts]).astype(bf16)
            continue
        rows = term.shape[0] - small
        whole = total([join_high(p[0, :small]) for p in parts])
        high = whole.astype(bf16)
        term[:small] = jnp.concatenate([high, (whole - high.astype(f32)).astype(bf16)])

        def give(k):
            count = min(rows, parts[0].shape[1] - small - k * rows)
            begin = small + k * rows
            term[small : small + count] = total([p[0, begin : begin + count] for p in parts]).astype(bf16)
            if count < rows:
                term[small + count :] = jnp.zeros((rows - count, D), bf16)

        for k in range(3):
            pl.when(jnp.maximum(goal, 1) == k + 1)(functools.partial(give, k))


def deal(body, me, parts, term, count):
    shape = jax.ShapeDtypeStruct(term, bf16)
    full = lambda dims: pl.BlockSpec(dims, lambda i: (0,) * len(dims))
    return pl.pallas_call(
        body,
        grid=(1,),
        in_specs=[pl.BlockSpec(memory_space=pltpu.SMEM)] + [full(p.shape) for p in parts],
        out_specs=[full(term)] * count,
        out_shape=[shape] * count,
        compiler_params=pltpu.CompilerParams(vmem_limit_bytes=VLIM_STEP),
        cost_estimate=pl.CostEstimate(
            flops=0, transcendentals=0, bytes_accessed=4 * len(parts) * parts[0].size
        ),
        name="sum_and_deal",
    )(me.reshape(1), *parts)


def sum_cut(net, parts, stage, small=0):
    size = 1 << stage[1]
    shape = parts[0].shape
    body = functools.partial(sum_cut_body, *stage, small)
    return deal(body, net.me, parts, (shape[0] // size,) + shape[1:], size)


def sum_top(net, parts, rows, small=0):
    body = functools.partial(sum_top_body, net.top[0], small)
    return deal(body, net.me, parts, (small + rows, D), 4)


def place_body(me_ref, *refs):
    *parts, out = refs
    put_in_order(me_ref[0] & (out.shape[0] - 1), parts, out)


def place(me, parts):
    size = len(parts) * parts[0].shape[0]
    shape = jax.ShapeDtypeStruct((size,) + parts[0].shape[1:], parts[0].dtype)
    return pl.pallas_call(
        place_body,
        in_specs=[pl.BlockSpec(memory_space=pltpu.SMEM)]
        + [pl.BlockSpec(memory_space=pltpu.VMEM)] * len(parts),
        out_specs=pl.BlockSpec(memory_space=pltpu.VMEM),
        out_shape=shape,
        compiler_params=pltpu.CompilerParams(vmem_limit_bytes=24 * 1024 * 1024),
        cost_estimate=pl.CostEstimate(flops=0, transcendentals=0, bytes_accessed=4 * shape.size),
        name="place",
    )(me.reshape(1), *parts)


def by_index(parts, index):
    return [
        functools.reduce(
            lambda rest, r: jnp.where(index == (b ^ r), parts[r], rest), range(1, len(parts)), parts[0]
        )
        for b in range(len(parts))
    ]


def on_device(mesh, features, cotangent, counts, weights, small_params, moments_old, small_moments,
              basis_attn, basis_ffn, basis_cols):
    net = Net(mesh)
    per = weights.shape[0] // 8
    everyone = net.stages + [net.top]

    def by_matrix(stacked):
        groups = stacked.reshape(per, 8, D)
        return (
            jnp.transpose(groups[:, 0:4], (1, 0, 2)),
            groups[:, 4:6].reshape(2 * per, D),
            groups[:, 6:8].reshape(2 * per, D),
        )

    def stacked(attn, inner, outer):
        return jnp.concatenate(
            [jnp.stack(attn, axis=1), inner.reshape(per, 2, D), outer.reshape(per, 2, D)], axis=1
        ).reshape(8 * per, D)

    inner = net.inner
    n_attn, n_ffn = D // inner, FF // inner
    ffn_of = lambda plane: jnp.clip(plane - 1, 0, 1)
    stages, top = net.stages, net.top

    own_attn, own_in, own_out = by_matrix(weights.astype(bf16))
    first = own_attn[None, 0:3]
    rest = jnp.concatenate([own_attn[3], own_in, own_out])[None]
    olds = [by_matrix(moments_old[i].astype(bf16)) for i in range(2)]
    old_attn = jnp.stack([m[0] for m in olds], axis=1)
    old_ffn = jnp.stack([jnp.stack([m[1], m[2]]) for m in olds], axis=1)
    old_terms = net.cut(
        lambda d: jnp.concatenate([take_at(old_ffn, ffn_of(d), 0), take_at(old_attn, d, 0)], axis=1), top
    )
    mine = ffn_of(net.plane)
    bases = (
        take_at(basis_attn, net.plane, 0).astype(bf16),
        take_at(basis_cols, net.plane, 0).astype(bf16),
        take_at(basis_ffn, mine, 0).astype(bf16),
        take_at(basis_cols, 4 + mine, 0).astype(bf16),
    )
    sp = jnp.concatenate([small_params.reshape(7, D), jnp.zeros((1, D), f32)])

    whole_tiles = per % 16 == 0
    order = list(reversed(everyone))
    first = interleave(net.collect(first, order[0]))
    rest_parts = net.collect(after(rest, first), order[0])
    for i, stage in enumerate(order[1:]):
        first_parts = net.collect(first, stage)
        if i == 0:
            first_parts, bases, old_terms = after((first_parts, bases, old_terms), first)
        if stage is not order[-1]:
            first = interleave(first_parts)
            rest_parts, first = after((rest_parts, first), first_parts)
            rest = interleave(rest_parts)
            rest_parts = net.collect(rest, stage)
    if not whole_tiles:
        first_parts = [jnp.transpose(place(net.me, first_parts), (1, 0, 2, 3)).reshape(1, 3, D, D)]
    first_parts = after(first_parts, rest, bases, old_terms)
    old_parts = net.trade(after(old_terms, rest), top)
    q, k, v, e, o, li, wqkv = attn_fwd(features, first_parts, net.me)
    rest_parts, old_parts = after((rest_parts, old_parts), o)
    rest, olds = interleave(rest_parts), jnp.stack(old_parts)
    for stage in reversed(stages[2:]):
        olds = net.widen(olds, stage)
    rest_parts = net.collect(after(rest, olds), order[-1])
    old_parts = net.collect(olds, stages[1])
    if not whole_tiles:
        rest = place(net.me, rest_parts)
        rest_parts = [
            jnp.concatenate(
                [rest[:, lo * per : hi * per].reshape(-1, D) for lo, hi in ((0, 1), (1, 3), (3, 5))]
            )[None]
        ]
    output, d1, do, *terms = rows_pass(
        counts, features, o, li, cotangent, after(rest_parts, olds), sp, net.me, inner
    )

    n_small = 16
    terms, old_parts = after((terms, old_parts), output)
    early_parts = net.trade(terms, stages[0])
    olds = interleave(old_parts)
    early_parts = after(early_parts, olds)
    for stage in stages[2:]:
        early_parts = net.trade(sum_cut(net, early_parts, stage, n_small), stage)
    terms = sum_cut(net, early_parts, stages[1], n_small)
    early_parts = net.trade(terms, stages[1])
    old_parts = net.collect(olds, stages[0])
    back = functools.partial(attn_bwd, x=features, q=q, k=k, v=v, e=e, o=o, do=do)
    acc, gw0 = back(0, acc=d1, wqkv=after(wqkv, terms, olds))
    early_parts, old_parts = after((early_parts, old_parts), gw0)
    top_terms = sum_top(net, early_parts, n_ffn, n_small)
    top_parts = net.trade(top_terms, top)
    grad_input, *terms = back(1, acc=acc, wqkv=after(wqkv, top_terms, old_parts), cut=(net.me, gw0, inner))

    terms, top_parts = lax.optimization_barrier((terms, top_parts))
    late_parts = net.trade(terms, stages[0])
    ffn = total([p[n_small:] for p in top_parts]).astype(bf16)
    ffn_parts = net.collect(ffn[None], stages[-1])
    late_parts = after(late_parts, ffn)
    for stage in stages[2:]:
        late_parts = net.trade(sum_cut(net, late_parts, stage), stage)
    terms = sum_cut(net, late_parts, stages[1])
    late_parts = net.trade(terms, stages[1])
    gs = total([join_high(p[:n_small]) for p in after(top_parts, terms)])
    grad_small = gs[0:7].reshape(-1)
    small_first = beta_one * small_moments[0] + (1.0 - beta_one) * grad_small
    small_second = beta_two * small_moments[1] + (1.0 - beta_two) * grad_small * grad_small
    small_new = small_params - rate_small * adam_direction(small_first, small_second)
    small_moments_new = jnp.stack([small_first, small_second])
    late_parts, ffn_parts, small_new, small_moments_new = lax.optimization_barrier(
        (late_parts, ffn_parts, small_new, small_moments_new)
    )
    terms = sum_top(net, late_parts, n_attn)
    late_parts = net.trade(terms, top, (0, 1, 2))
    ffn_parts = after(ffn_parts, terms)
    for stage in reversed(stages[:-1]):
        ffn_parts = net.collect(interleave(ffn_parts), stage)

    if whole_tiles:
        back_ffn = rotated_step_parts(net.me, ffn_parts, bases[2], bases[3], old_parts, 0)
    else:
        olds = jnp.transpose(place(net.me, old_parts), (1, 0, 2, 3))
        full = place(net.me, ffn_parts).reshape(FF, D)
        both = rotated_step(full, bases[2], bases[3], olds[:, :, : 2 * per].reshape(2, FF, D))
        back_ffn = take_at(jnp.stack([full, *both]).reshape(3, 4, inner, 2 * per, D), net.local, 2)
        back_ffn = net.cut(lambda d: take_at(back_ffn, d, 1), top)
    late_parts = after(late_parts, back_ffn)
    attn = total(late_parts).astype(bf16)
    attn = jnp.where(net.plane == 3, ffn[:n_attn], attn)[None]
    for stage in reversed(stages[1:]):
        attn = net.widen(attn, stage)
    attn_parts = net.collect(attn, stages[0])
    back_ffn = net.trade(back_ffn, top, sources=(1, 2))
    if whole_tiles:
        back_attn = rotated_step_parts(net.me, attn_parts, bases[0], bases[1], old_parts, 2)
    else:
        full = place(net.me, attn_parts).reshape(D, D)
        both = rotated_step(full, bases[0], bases[1], olds[:, :, 2 * per :].reshape(2, D, D))
        back_attn = take_at(jnp.stack([full, *both]).reshape(3, 4, inner, per, D), net.local, 2)
        back_attn = net.cut(lambda d: take_at(back_attn, d, 1), top)
    back_ffn = after(back_ffn, back_attn)
    back_attn = net.trade(back_attn, top)
    back_attn = by_index(back_attn, net.plane)
    back_ffn = by_index(back_ffn, net.plane)
    grad_weights, rotated, update = (
        stacked([part[i] for part in back_attn], back_ffn[1][i], back_ffn[2][i]).astype(f32) for i in range(3)
    )
    moments_new = jnp.stack(
        [
            beta_one * moments_old[0] + (1.0 - beta_one) * rotated,
            beta_two * moments_old[1] + (1.0 - beta_two) * rotated * rotated,
        ]
    )
    weights_new = weights - rate_mats * update
    return (
        output,
        grad_input,
        grad_weights,
        moments_new,
        weights_new,
        grad_small,
        small_moments_new,
        small_new,
    )


def solution(mesh):
    rows = P(("dp", "fsdp"), None)
    blocks = P(("dp", "fsdp"), None, None)
    pair = P(None, ("dp", "fsdp"), None)
    return jax.shard_map(
        lambda *arrays: on_device(mesh, *arrays),
        mesh=mesh,
        in_specs=(blocks, blocks, P(("dp", "fsdp")), rows, P(), pair, P(), P(), P(), P()),
        out_specs=(blocks, blocks, rows, pair, rows, P(), P(), P()),
        check_vma=False,
    )
```

```python
import functools
import jax
import jax.numpy as jnp
from jax import lax
from jax.sharding import PartitionSpec as P
from jax.experimental import pallas as pl
from jax.experimental.pallas import tpu as pltpu

D = 512
HEADS = 4
FF = 1024
HD = 128
CTX = 1024
SLOTS = 1128
STEP = 10
PAD = 1152
RB = 384
NRB = PAD // RB
RBL = 576
SUB = 128
NRBL = PAD // RBL
scaling = HD ** (-0.5)
eps_norm = 1e-05
eps_adam = 1e-08
beta_one = 0.9
beta_two = 0.999
rate_mats = 0.1
rate_small = 0.5
axes = ("dp", "fsdp")
bf16 = jnp.bfloat16
f32 = jnp.float32
VLIM_FWD = 58 * 1024 * 1024
VLIM_ROWS = 46 * 1024 * 1024
VLIM_BWD = 46 * 1024 * 1024
VLIM_STEP = 24 * 1024 * 1024


def nt(a, b):
    return lax.dot_general(a, b, (((1,), (1,)), ((), ())), preferred_element_type=f32)


def nn(a, b):
    return lax.dot_general(a, b, (((1,), (0,)), ((), ())), preferred_element_type=f32)


def tn(a, b):
    return lax.dot_general(a, b, (((0,), (0,)), ((), ())), preferred_element_type=f32)


def put_in_order(me, parts, out):
    def move(j, carry):
        for c, part in enumerate(parts):
            out[(j * len(parts) + c) ^ me] = part[j]
        return carry

    lax.fori_loop(0, parts[0].shape[0], move, 0)


def attn_fwd_body(ways, *refs):
    me_ref, xc_ref, xr_ref, *refs = refs
    parts, (q_ref, k_ref, v_ref, e_ref, o_ref, li_ref, w_ref, ve_ref) = refs[:ways], refs[ways:]
    n, rb = pl.program_id(0), pl.program_id(1)

    @pl.when(jnp.logical_and(n == 0, rb == 0))
    def _():
        put_in_order(me_ref[0] & (w_ref.shape[0] - 1), parts, w_ref)

    @pl.when(rb == 0)
    def _():
        xc = xc_ref[0]
        k_ref[0] = nt(xc, w_ref[:, 1].reshape(D, D)).astype(bf16)
        v_ref[0] = nt(xc, w_ref[:, 2].reshape(D, D)).astype(bf16)
        for h in range(HEADS):
            ve_ref[h, :, 0:HD] = v_ref[0, :, h * HD : (h + 1) * HD]
            ve_ref[h, :, HD : 2 * HD] = jnp.ones((CTX, HD), bf16)

    rows = rb * RB + lax.broadcasted_iota(jnp.int32, (RB, 1), 0)
    xr = jnp.where(rows < SLOTS, xr_ref[0].astype(f32), 0.0).astype(bf16)
    q_ref[0] = (nt(xr, w_ref[:, 0].reshape(D, D)) * scaling).astype(bf16)
    lane = lax.broadcasted_iota(jnp.int32, (SUB, HD), 1) // (HD // HEADS)
    for r in range(0, RB, SUB):
        rs = slice(r, r + SUB)
        for h in range(HEADS):
            hs = slice(h * HD, (h + 1) * HD)
            s = nt(q_ref[0, rs, hs], k_ref[0, :, hs])
            m = jnp.max(s, axis=-1, keepdims=True)
            e = jnp.exp(s - m).astype(bf16)
            e_ref[0, h, rs] = e
            ov = nn(e, ve_ref[h])
            li = 1.0 / ov[:, HD:]
            scales = li if h == 0 else jnp.where(lane == h, li, scales)
            o_ref[0, rs, hs] = (ov[:, :HD] * li).astype(bf16)
        li_ref[0, rs] = scales


def attn_fwd(x, parts, me):
    n = x.shape[0]
    sd = jax.ShapeDtypeStruct
    everything = lambda shape: pl.BlockSpec(shape, lambda i, r: (0,) * len(shape))
    wshape = (len(parts) * parts[0].shape[0],) + parts[0].shape[1:]
    block = lambda w: pl.BlockSpec((1, RB, w), lambda i, r: (i, r, 0))
    context = pl.BlockSpec((1, CTX, D), lambda i, r: (i, 0, 0))
    return pl.pallas_call(
        functools.partial(attn_fwd_body, len(parts)),
        grid=(n, NRB),
        in_specs=[pl.BlockSpec(memory_space=pltpu.SMEM), context, block(D)]
        + [everything(w.shape) for w in parts],
        out_specs=[
            block(D),
            context,
            context,
            pl.BlockSpec((1, HEADS, RB, CTX), lambda i, r: (i, 0, r, 0)),
            block(D),
            block(HD),
            everything(wshape),
        ],
        out_shape=[
            sd((n, PAD, D), bf16),
            sd((n, CTX, D), bf16),
            sd((n, CTX, D), bf16),
            sd((n, HEADS, PAD, CTX), bf16),
            sd((n, PAD, D), bf16),
            sd((n, PAD, HD), f32),
            sd(wshape, bf16),
        ],
        scratch_shapes=[pltpu.VMEM((HEADS, CTX, 2 * HD), bf16)],
        compiler_params=pltpu.CompilerParams(
            dimension_semantics=("arbitrary", "arbitrary"), vmem_limit_bytes=VLIM_FWD
        ),
        cost_estimate=pl.CostEstimate(
            flops=14_000_000_000, transcendentals=n * HEADS * PAD * CTX, bytes_accessed=40_000_000
        ),
        name="attention_forward",
    )(me.reshape(1), x, x, *parts)


def lane_mean(v):
    return jnp.sum(v, axis=-1, keepdims=True) * (1.0 / D)


NSUB = 1


def rows_body(ways, cnt_ref, x_ref, o_ref, li_ref, c_ref, *refs):
    parts, (sp_ref,
            out_ref, d1_ref, do_ref, keep_ref, send_ref, gs_ref, go_ref, gi_ref, gb_ref,
            gbs, dus, dfs, hbs, das, osc, *placed) = refs[:ways], refs[ways:]
    w_ref = placed[0] if placed else parts[0]
    me = cnt_ref[cnt_ref.shape[0] - 1]
    pieces, small = 2 * keep_ref.shape[0], 2 * gs_ref.shape[0]
    n, rb = pl.program_id(0), pl.program_id(1)
    first = jnp.logical_and(n == 0, rb == 0)
    last = jnp.logical_and(n == pl.num_programs(0) - 1, rb == NRBL - 1)

    @pl.when(first)
    def _():
        go_ref[...] = jnp.zeros_like(go_ref)
        gi_ref[...] = jnp.zeros_like(gi_ref)
        gb_ref[...] = jnp.zeros_like(gb_ref)
        gs_ref[...] = jnp.zeros_like(gs_ref)
        if placed:
            put_in_order(me, parts, w_ref)

    per = w_ref.shape[1] // 5
    wo = w_ref[:, 0:per].reshape(D, D)
    wi = w_ref[:, per : 3 * per].reshape(FF, D)
    wb = w_ref[:, 3 * per :].reshape(FF, D)
    gain1, shift1 = sp_ref[0:1], sp_ref[1:2]
    bias2, gain2, shift2 = sp_ref[4:5], sp_ref[5:6], sp_ref[6:7]
    bias1 = jnp.concatenate([sp_ref[2:3], sp_ref[3:4]], axis=1)
    size = RBL // NSUB
    sums = []

    def chain(part):
        rs = slice(part * size, (part + 1) * size)
        here = pl.ds(pl.multiple_of(rb * RBL, RBL) + part * size, size)
        osc[here] = o_ref[0, rs]
        rows = rb * RBL + part * size + lax.broadcasted_iota(jnp.int32, (size, 1), 0)
        valid = rows < SLOTS
        live = rows < CTX + cnt_ref[n]
        at = nt(o_ref[0, rs], wo)
        yield
        r1 = jnp.where(valid, x_ref[0, rs].astype(f32), 0.0) + at
        c1 = r1 - lane_mean(r1)
        is1 = lax.rsqrt(lane_mean(c1 * c1) + eps_norm)
        xh1 = c1 * is1
        h = xh1 * gain1 + shift1
        hb = h.astype(bf16)
        hbs[here] = hb
        yield
        u = nt(hb, wi)
        yield
        u = u + bias1
        ex = jnp.exp2((-0.7213475204444817 * u) * u)
        t = 1.0 / (1.0 + 0.23164189 * jnp.abs(u))
        poly = t * (0.127414796 + t * (-0.142248368 + t * (0.7107068705 + t * (-0.7265760135 + t * 0.5307027145))))
        tail = poly * ex
        phi = jnp.where(u >= 0.0, 1.0 - tail, tail)
        gb = (u * phi).astype(bf16)
        gbs[here] = gb
        dgelu = phi + u * ex * 0.3989422804014327
        yield
        r2 = nn(gb, wb)
        yield
        r2 = h + r2 + bias2
        c2 = r2 - lane_mean(r2)
        is2 = lax.rsqrt(lane_mean(c2 * c2) + eps_norm)
        xh2 = c2 * is2
        out_ref[0, rs] = jnp.where(live, xh2 * gain2 + shift2, 0.0).astype(bf16)
        dy = jnp.where(live, c_ref[0, rs].astype(f32), 0.0)
        s5 = jnp.sum(dy * xh2, axis=0, keepdims=True)
        s6 = jnp.sum(dy, axis=0, keepdims=True)
        e2 = dy * gain2
        d2 = (e2 - lane_mean(e2) - xh2 * lane_mean(e2 * xh2)) * is2
        df = d2.astype(bf16)
        dfs[here] = df
        s4 = jnp.sum(df.astype(f32), axis=0, keepdims=True)
        yield
        dg = nt(df, wb)
        yield
        du = (dg * dgelu).astype(bf16)
        dus[here] = du
        s2 = jnp.sum(du.astype(f32), axis=0, keepdims=True)
        yield
        dh = nn(du, wi)
        yield
        dh = d2 + dh
        s0 = jnp.sum(dh * xh1, axis=0, keepdims=True)
        s1 = jnp.sum(dh, axis=0, keepdims=True)
        e1 = dh * gain1
        d1 = (e1 - lane_mean(e1) - xh1 * lane_mean(e1 * xh1)) * is1
        d1_ref[0, rs] = d1
        da = d1.astype(bf16)
        das[here] = da
        sums.append((s0, s1, s2[:, :D], s2[:, D:], s4, s5, s6))
        yield
        dm = nn(da, wo)
        yield
        for h in range(HEADS):
            hs = slice(h * HD, (h + 1) * HD)
            li = li_ref[0, rs, h * (HD // HEADS) : h * (HD // HEADS) + 1]
            do_ref[0, rs, hs] = (dm[:, hs] * li).astype(bf16)

    chains = [chain(i) for i in range(NSUB)]
    for i, c in enumerate(chains):
        for _ in range(len(chains) - 1 - i):
            next(c)
    done = 0
    while done < len(chains):
        done = 0
        for c in chains:
            try:
                next(c)
            except StopIteration:
                done += 1
    for i in range(7):
        total_i = sums[0][i]
        for s in sums[1:]:
            total_i = total_i + s[i]
        gs_ref[i : i + 1] += total_i

    @pl.when(rb == NRBL - 1)
    def _():
        for target, left, right in ((gi_ref, dus, hbs), (gb_ref, gbs, dfs), (go_ref, das, osc)):
            target[...] += tn(left[...], right[...])

    def write(core):
        for p in range(pieces):
            out = keep_ref if p % 2 == core else send_ref
            if p < 2:
                high = gs_ref[...].astype(bf16)
                out[0, : small // 2] = high
                out[0, small // 2 : small] = (gs_ref[...] - high.astype(f32)).astype(bf16)
            else:
                out[p // 2, :small] = jnp.zeros((small, D), bf16)
            at = small
            for target in (gi_ref, gb_ref, go_ref):
                size = target.shape[0] // pieces
                out[p // 2, at : at + size] = target[p * size : (p + 1) * size].astype(bf16)
                at += size

    for core in range(2):
        pl.when(jnp.logical_and(last, me % 2 == core))(functools.partial(write, core))


def rows_pass(counts, x, o, li, cot, rest, sp, pieces):
    n = x.shape[0]
    placed = []
    if len(rest) > 1:
        placed = [pltpu.VMEM((2 * rest[0].shape[0],) + rest[0].shape[1:], bf16)]
    cut = (pieces // 2, 16 + (D + 2 * FF) // pieces, D)
    sd = jax.ShapeDtypeStruct
    blk = pl.BlockSpec((1, RBL, D), lambda i, r, c: (i, r, 0))
    const = lambda *s: pl.BlockSpec(s, lambda i, r, c: (0,) * len(s))
    return pl.pallas_call(
        functools.partial(rows_body, len(rest)),
        grid_spec=pltpu.PrefetchScalarGridSpec(
            num_scalar_prefetch=1,
            grid=(n, NRBL),
            in_specs=[
                blk,
                blk,
                pl.BlockSpec((1, RBL, HD), lambda i, r, c: (i, r, 0)),
                blk,
            ]
            + [const(*w.shape) for w in rest]
            + [const(8, D)],
            out_specs=[blk, blk, blk, const(*cut), const(*cut)],
            scratch_shapes=[
                pltpu.VMEM((8, D), f32),
                pltpu.VMEM((D, D), f32),
                pltpu.VMEM((FF, D), f32),
                pltpu.VMEM((FF, D), f32),
                pltpu.VMEM((PAD, FF), bf16),
                pltpu.VMEM((PAD, FF), bf16),
                pltpu.VMEM((PAD, D), bf16),
                pltpu.VMEM((PAD, D), bf16),
                pltpu.VMEM((PAD, D), bf16),
                pltpu.VMEM((PAD, D), bf16),
            ]
            + placed,
        ),
        out_shape=[
            sd((n, SLOTS, D), bf16),
            sd((n, SLOTS, D), f32),
            sd((n, PAD, D), bf16),
            sd(cut, bf16),
            sd(cut, bf16),
        ],
        compiler_params=pltpu.CompilerParams(
            dimension_semantics=("arbitrary", "arbitrary"), vmem_limit_bytes=VLIM_ROWS
        ),
        cost_estimate=pl.CostEstimate(
            flops=n * 18_000_000_000 // 2, transcendentals=n * PAD * FF * 2, bytes_accessed=n * 15_000_000
        ),
        name="rows_forward_backward",
    )(counts, x, o, li, cot, *rest, sp)


def attn_bwd_body(cut, *refs):
    x_ref, q_ref, k_ref, v_ref, e_ref, o_ref, do_ref, acc_ref, w_ref, *refs = refs
    (me_ref, other_ref), refs = (refs[:2], refs[2:]) if cut else ((None, None), refs)
    gi_ref, *outs = refs[:-4]
    dkt_ref, dvt_ref, gw_ref, xs_ref = refs[-4:]
    n, rb = pl.program_id(0), pl.program_id(1)

    @pl.when(jnp.logical_and(n == 0, rb == 0))
    def _():
        gw_ref[...] = jnp.zeros_like(gw_ref)

    @pl.when(rb == 0)
    def _():
        dkt_ref[...] = jnp.zeros_like(dkt_ref)
        dvt_ref[...] = jnp.zeros_like(dvt_ref)

    rows = rb * RBL + lax.broadcasted_iota(jnp.int32, (RBL, 1), 0)
    x = jnp.where(rows < SLOTS, x_ref[0].astype(f32), 0.0).astype(bf16)
    here = pl.ds(pl.multiple_of(rb * RBL, RBL), RBL)
    xs_ref[here] = x
    dqs = []
    for h in range(2):
        hs = slice(h * HD, (h + 1) * HD)
        do = do_ref[0, :, hs]
        t = jnp.sum(do.astype(f32) * o_ref[0, :, hs].astype(f32), axis=-1, keepdims=True)
        dp = nt(do, v_ref[0, :, hs])
        e = e_ref[0, h]
        ds = (e.astype(f32) * (dp - t)).astype(bf16)
        dqs.append(nn(ds, k_ref[0, :, hs]).astype(bf16))
        dvt_ref[hs] += tn(do, e)
        dkt_ref[hs] += tn(q_ref[0, :, hs], ds)
    dq = jnp.concatenate(dqs, axis=1)
    wq, wk, wv = (w_ref[:, i].reshape(2 * HD, D) for i in range(3))
    gw_ref[0] += tn(dq, x) * scaling
    gi_ref[0, here] = acc_ref[0] + nn(dq, wq) * scaling

    @pl.when(rb == NRBL - 1)
    def _():
        dkt, dvt = dkt_ref[...].astype(bf16), dvt_ref[...].astype(bf16)
        xc = xs_ref[0:CTX]
        gw_ref[1] += nn(dkt, xc)
        gw_ref[2] += nn(dvt, xc)
        gi_ref[0, 0:CTX] += tn(dkt, wk) + tn(dvt, wv)

    last = jnp.logical_and(n == pl.num_programs(0) - 1, rb == NRBL - 1)
    if not cut:

        @pl.when(last)
        def _():
            outs[0][...] = gw_ref[...]

        return

    def write(core):
        pieces, size = 2 * outs[0].shape[0], outs[0].shape[2]
        for p in range(pieces):
            out = outs[0] if p % 2 == core else outs[1]
            half, row = divmod(p * size, 2 * HD)
            for i in range(3):
                out[p // 2, i] = (gw_ref if half else other_ref)[i, row : row + size].astype(bf16)

    for core in range(2):
        pl.when(jnp.logical_and(last, me_ref[0] % 2 == core))(functools.partial(write, core))


def attn_bwd(pair, x, q, k, v, e, o, do, acc, wqkv, cut=()):
    n = x.shape[0]
    sd = jax.ShapeDtypeStruct
    ways = wqkv.shape[0]
    if ways > 1:
        wspec = pl.BlockSpec((ways // 2,) + wqkv.shape[1:], lambda i, r: (pair, 0, 0, 0))
    else:
        wspec = pl.BlockSpec((1, 3, 2 * HD, D), lambda i, r: (0, 0, pair, 0))
    heads = pl.BlockSpec((1, RBL, 2 * HD), lambda i, r: (i, r, pair))
    context = pl.BlockSpec((1, CTX, 2 * HD), lambda i, r: (i, 0, pair))
    rows = pl.BlockSpec((1, RBL, D), lambda i, r: (i, r, 0))
    grads = lambda shape: pl.BlockSpec(shape, lambda i, r: (0,) * len(shape))
    outs = [sd((cut[2] // 2, 3, D // cut[2], D), bf16)] * 2 if cut else [sd((3, 2 * HD, D), f32)]
    return pl.pallas_call(
        functools.partial(attn_bwd_body, bool(cut)),
        grid=(n, NRBL),
        in_specs=[
            rows,
            heads,
            context,
            context,
            pl.BlockSpec((1, 2, RBL, CTX), lambda i, r: (i, pair, r, 0)),
            heads,
            heads,
            rows,
            wspec,
        ]
        + ([pl.BlockSpec(memory_space=pltpu.SMEM), grads((3, 2 * HD, D))] if cut else []),
        out_specs=[pl.BlockSpec((1, PAD, D), lambda i, r: (i, 0, 0))] + [grads(g.shape) for g in outs],
        out_shape=[sd((n, SLOTS, D), f32)] + outs,
        scratch_shapes=[
            pltpu.VMEM((2 * HD, CTX), f32),
            pltpu.VMEM((2 * HD, CTX), f32),
            pltpu.VMEM((3, 2 * HD, D), f32),
            pltpu.VMEM((PAD, D), bf16),
        ],
        input_output_aliases={7: 0},
        compiler_params=pltpu.CompilerParams(
            dimension_semantics=("arbitrary", "arbitrary"), vmem_limit_bytes=VLIM_BWD
        ),
        cost_estimate=pl.CostEstimate(
            flops=9_000_000_000, transcendentals=0, bytes_accessed=24_000_000
        ),
        name="attention_backward",
    )(x, q, k, v, e, o, do, acc, wqkv, *([cut[0].reshape(1), cut[1]] if cut else []))


def adam_direction(first_new, second_new):
    return (first_new * (1.0 / (1.0 - beta_one**STEP))) / (
        jnp.sqrt(second_new * (1.0 / (1.0 - beta_two**STEP))) + eps_adam
    )


def rotate(grad, rows_basis, cols_basis, first_old, second_old):
    r = nn(tn(rows_basis, grad).astype(bf16), cols_basis)
    first_new = beta_one * first_old.astype(f32) + (1.0 - beta_one) * r
    second_new = beta_two * second_old.astype(f32) + (1.0 - beta_two) * r * r
    step = adam_direction(first_new, second_new).astype(bf16)
    return r.astype(bf16), nn(rows_basis, nt(step, cols_basis).astype(bf16)).astype(bf16)


def rotate_body(g_ref, a_ref, b_ref, m_ref, r_ref, u_ref):
    r_ref[...], u_ref[...] = rotate(g_ref[...], a_ref[...], b_ref[...], m_ref[0], m_ref[1])


def rotated_step(grad, rows_basis, cols_basis, moments):
    rows = grad.shape[0]
    sd = jax.ShapeDtypeStruct
    return pl.pallas_call(
        rotate_body,
        out_shape=[sd((rows, D), bf16), sd((rows, D), bf16)],
        compiler_params=pltpu.CompilerParams(vmem_limit_bytes=VLIM_STEP),
        cost_estimate=pl.CostEstimate(
            flops=4 * rows * D * (rows + D), transcendentals=rows * D, bytes_accessed=2 * rows * (rows + 5 * D)
        ),
        name="rotated_step",
    )(grad, rows_basis, cols_basis, moments)


def rotate_parts_body(me_ref, *refs):
    grads, a_ref, b_ref, olds, outs = refs[:2], refs[2], refs[3], refs[4:6], refs[6:10]
    g_ref, m_ref, r_ref, u_ref = refs[10:]
    me = me_ref[0]
    planes, inner, rows = len(outs), g_ref.shape[0], r_ref.shape[0]
    per = rows // (planes * inner)
    put_in_order(me & (inner - 1), grads, g_ref)
    put_in_order(me, olds, m_ref)
    r_ref[...], u_ref[...] = rotate(
        g_ref[...].reshape(rows, D), a_ref[...], b_ref[...],
        m_ref[:, 0].reshape(rows, D), m_ref[:, 1].reshape(rows, D),
    )
    n = g_ref.shape[1]
    for rel, out in enumerate(outs):
        row = pl.multiple_of((me ^ (rel * inner)) * per, per)
        out[0] = g_ref[row // n, pl.ds(pl.multiple_of(row % n, per), per)]
        out[1] = r_ref[pl.ds(row, per)]
        out[2] = u_ref[pl.ds(row, per)]


def rotated_step_parts(me, grads, rows_basis, cols_basis, olds, block):
    rows = rows_basis.shape[0]
    inner = 2 * grads[0].shape[0]
    count = 2 * olds[0].shape[0]
    per = rows // count
    full = lambda shape: pl.BlockSpec(shape, lambda i: (0,) * len(shape))
    return pl.pallas_call(
        rotate_parts_body,
        grid=(1,),
        in_specs=[pl.BlockSpec(memory_space=pltpu.SMEM)]
        + [full(g.shape) for g in grads]
        + [full(rows_basis.shape), full(cols_basis.shape)]
        + [pl.BlockSpec((count // 2, 2, per, D), lambda i: (0, 0, block, 0))] * 2,
        out_specs=[full((3, per, D))] * (count // inner),
        out_shape=[jax.ShapeDtypeStruct((3, per, D), bf16)] * (count // inner),
        scratch_shapes=[
            pltpu.VMEM((inner, rows // inner, D), bf16),
            pltpu.VMEM((count, 2, per, D), bf16),
            pltpu.VMEM((rows, D), bf16),
            pltpu.VMEM((rows, D), bf16),
        ],
        compiler_params=pltpu.CompilerParams(vmem_limit_bytes=VLIM_STEP),
        cost_estimate=pl.CostEstimate(
            flops=4 * rows * D * (rows + D), transcendentals=rows * D, bytes_accessed=2 * rows * (rows + 5 * D)
        ),
        name="rotated_step",
    )(me.reshape(1), *grads, rows_basis, cols_basis, *(pltpu.with_memory_space_constraint(v, pltpu.HBM) for v in olds))


class Net:
    def __init__(self, mesh):
        self.count = mesh.size
        self.bits = self.count.bit_length() - 1
        self.inner_bits = self.bits - 2
        self.inner = 1 << self.inner_bits
        self.me = lax.axis_index(axes)
        self.local = self.me & (self.inner - 1)
        self.plane = self.me >> self.inner_bits
        stages = [(0, 1)]
        while stages[-1][0] + stages[-1][1] < self.inner_bits:
            low = stages[-1][0] + stages[-1][1]
            stages.append((low, min(2, self.inner_bits - low)))
        self.stages = stages
        self.top = (self.inner_bits, 2)

    def swap(self, value, offset, targets=(0, 1, 2, 3), sources=(0, 1, 2, 3)):
        pairs = [(i, i ^ offset) for i in range(self.count)]
        pairs = [
            (i, j) for i, j in pairs
            if (i >> self.inner_bits) in sources and (j >> self.inner_bits) in targets
        ]
        return lax.ppermute(value, axes, pairs)

    def digit(self, stage):
        return (self.me >> stage[0]) & ((1 << stage[1]) - 1)

    def collect(self, value, stage):
        return [value] + [self.swap(value, rel << stage[0]) for rel in range(1, 1 << stage[1])]

    def widen(self, value, stage):
        return interleave(self.collect(value, stage))

    def cut(self, pick, stage):
        mine = self.digit(stage)
        return [pick(mine ^ rel) for rel in range(1 << stage[1])]

    def trade(self, terms, stage, targets=(0, 1, 2, 3), sources=(0, 1, 2, 3)):
        return list(terms[:1]) + [
            self.swap(term, rel << stage[0], targets, sources) for rel, term in enumerate(terms) if rel
        ]


def after(value, *earlier):
    return lax.optimization_barrier((value, earlier))[0]


def interleave(parts):
    value = jnp.stack(parts, axis=1)
    return value.reshape((-1,) + value.shape[2:])


def total(parts):
    parts = [p.astype(f32) for p in parts]
    while len(parts) > 1:
        parts = [a + b for a, b in zip(parts[0::2], parts[1::2])]
    return parts[0]


def take_at(value, index, axis):
    return lax.dynamic_index_in_dim(value, index, axis, keepdims=False)


def join_high(pair):
    half = pair.shape[0] // 2
    return pair[:half].astype(f32) + pair[half:].astype(f32)


def sum_cut_body(low, bits, small, me_ref, *refs):
    size = 1 << bits
    parts, terms = refs[:-size], refs[-size:]
    digit = (me_ref[0] >> low) & (size - 1)
    if small:
        whole = total([join_high(p[0, :small]) for p in parts])
        high = whole.astype(bf16)
        pair = jnp.concatenate([high, (whole - high.astype(f32)).astype(bf16)])
    for rel, term in enumerate(terms):
        for j in range(term.shape[0]):
            piece = j * size + (digit ^ rel)
            if small:
                term[j, :small] = pair
                term[j, small:] = total([p[piece, small:] for p in parts]).astype(bf16)
            else:
                term[j] = total([p[piece] for p in parts]).astype(bf16)


def sum_top_body(low, small, me_ref, *refs):
    parts, terms = refs[:-4], refs[-4:]
    plane = (me_ref[0] >> low) & 3
    for rel, term in enumerate(terms):
        goal = plane ^ rel
        if not small:
            piece = jnp.minimum(goal, 2)
            term[...] = total([p[0, piece] for p in parts]).astype(bf16)
            continue
        rows = term.shape[0] - small
        whole = total([join_high(p[0, :small]) for p in parts])
        high = whole.astype(bf16)
        term[:small] = jnp.concatenate([high, (whole - high.astype(f32)).astype(bf16)])

        def give(k):
            count = min(rows, parts[0].shape[1] - small - k * rows)
            begin = small + k * rows
            term[small : small + count] = total([p[0, begin : begin + count] for p in parts]).astype(bf16)
            if count < rows:
                term[small + count :] = jnp.zeros((rows - count, D), bf16)

        for k in range(3):
            pl.when(jnp.maximum(goal, 1) == k + 1)(functools.partial(give, k))


def deal(body, me, parts, term, count):
    full = lambda dims: pl.BlockSpec(dims, lambda i: (0,) * len(dims))
    return pl.pallas_call(
        body,
        grid=(1,),
        in_specs=[pl.BlockSpec(memory_space=pltpu.SMEM)] + [full(p.shape) for p in parts],
        out_specs=[full(term)] * count,
        out_shape=[pltpu.HBM(term, bf16)] * count,
        compiler_params=pltpu.CompilerParams(vmem_limit_bytes=VLIM_STEP),
        cost_estimate=pl.CostEstimate(
            flops=0, transcendentals=0, bytes_accessed=4 * len(parts) * parts[0].size
        ),
        name="sum_and_deal",
    )(me.reshape(1), *parts)


def sum_cut(net, parts, stage, small=0):
    size = 1 << stage[1]
    shape = parts[0].shape
    body = functools.partial(sum_cut_body, *stage, small)
    return deal(body, net.me, parts, (shape[0] // size,) + shape[1:], size)


def sum_top(net, parts, rows, small=0):
    body = functools.partial(sum_top_body, net.top[0], small)
    return deal(body, net.me, parts, (small + rows, D), 4)


def place_body(me_ref, *refs):
    *parts, out = refs
    put_in_order(me_ref[0] & (out.shape[0] - 1), parts, out)


def place(me, parts):
    size = len(parts) * parts[0].shape[0]
    shape = jax.ShapeDtypeStruct((size,) + parts[0].shape[1:], parts[0].dtype)
    return pl.pallas_call(
        place_body,
        in_specs=[pl.BlockSpec(memory_space=pltpu.SMEM)]
        + [pl.BlockSpec(memory_space=pltpu.VMEM)] * len(parts),
        out_specs=pl.BlockSpec(memory_space=pltpu.VMEM),
        out_shape=shape,
        compiler_params=pltpu.CompilerParams(vmem_limit_bytes=24 * 1024 * 1024),
        cost_estimate=pl.CostEstimate(flops=0, transcendentals=0, bytes_accessed=4 * shape.size),
        name="place",
    )(me.reshape(1), *parts)


def finish_body(low, me_ref, *refs):
    attn, ffn = refs[:4], refs[4:8]
    moments_ref, weights_ref, grad_ref, new_ref, out_ref = refs[8:]
    plane = (me_ref[0] >> low) & 3
    per = attn[0].shape[1]
    rows = 8 * per

    def choose(parts, plain, kind):
        value = parts[0][kind].astype(f32)
        for rel in range(1, 4):
            value = jnp.where(plane == (plain ^ rel), parts[rel][kind].astype(f32), value)
        return value.astype(bf16)

    row = lax.broadcasted_iota(jnp.int32, (rows, rows), 0)
    source = lax.broadcasted_iota(jnp.int32, (rows, rows), 1)
    group, slot = row // 8, row % 8
    wanted = jnp.where(
        slot < 4, slot * per + group, (4 + 2 * ((slot - 4) // 2)) * per + 2 * group + slot % 2
    )
    order = jnp.where(source == wanted, 1.0, 0.0).astype(bf16)

    def plain(kind):
        parts = [choose(attn, b, kind) for b in range(4)] + [choose(ffn, f, kind) for f in (1, 2)]
        return nn(order, jnp.concatenate(parts))

    grad_ref[...] = plain(0)
    turned = plain(1)
    new_ref[0] = beta_one * moments_ref[0] + (1.0 - beta_one) * turned
    new_ref[1] = beta_two * moments_ref[1] + (1.0 - beta_two) * turned * turned
    out_ref[...] = weights_ref[...] - rate_mats * plain(2)


def finish(net, attn, ffn, moments, weights):
    full = lambda shape: pl.BlockSpec(shape, lambda i: (0,) * len(shape))
    arrays = [*attn, *ffn, moments, weights]
    outs = [weights, moments, weights]
    return pl.pallas_call(
        functools.partial(finish_body, net.top[0]),
        grid=(1,),
        in_specs=[pl.BlockSpec(memory_space=pltpu.SMEM)] + [full(v.shape) for v in arrays],
        out_specs=[full(v.shape) for v in outs],
        out_shape=[jax.ShapeDtypeStruct(v.shape, f32) for v in outs],
        compiler_params=pltpu.CompilerParams(vmem_limit_bytes=VLIM_STEP),
        cost_estimate=pl.CostEstimate(flops=50_000_000, transcendentals=0, bytes_accessed=3_000_000),
        name="finish",
    )(net.me.reshape(1), *arrays)


def by_index(parts, index):
    return [
        functools.reduce(
            lambda rest, r: jnp.where(index == (b ^ r), parts[r], rest), range(1, len(parts)), parts[0]
        )
        for b in range(len(parts))
    ]


def on_device(mesh, features, cotangent, counts, weights, small_params, moments_old, small_moments,
              basis_attn, basis_ffn, basis_cols):
    net = Net(mesh)
    per = weights.shape[0] // 8
    everyone = net.stages + [net.top]

    def by_matrix(stacked):
        groups = stacked.reshape(per, 8, D)
        return (
            jnp.transpose(groups[:, 0:4], (1, 0, 2)),
            groups[:, 4:6].reshape(2 * per, D),
            groups[:, 6:8].reshape(2 * per, D),
        )

    def stacked(attn, inner, outer):
        return jnp.concatenate(
            [jnp.stack(attn, axis=1), inner.reshape(per, 2, D), outer.reshape(per, 2, D)], axis=1
        ).reshape(8 * per, D)

    inner = net.inner
    n_attn, n_ffn = D // inner, FF // inner
    ffn_of = lambda plane: jnp.clip(plane - 1, 0, 1)
    stages, top = net.stages, net.top

    own_attn, own_in, own_out = by_matrix(weights.astype(bf16))
    first = own_attn[None, 0:3]
    rest = jnp.concatenate([own_attn[3], own_in, own_out])[None]
    olds = [by_matrix(moments_old[i].astype(bf16)) for i in range(2)]
    old_attn = jnp.stack([m[0] for m in olds], axis=1)
    old_ffn = jnp.stack([jnp.stack([m[1], m[2]]) for m in olds], axis=1)
    old_terms = net.cut(
        lambda d: jnp.concatenate([take_at(old_ffn, ffn_of(d), 0), take_at(old_attn, d, 0)], axis=1), top
    )
    mine = ffn_of(net.plane)
    bases = (
        take_at(basis_attn, net.plane, 0).astype(bf16),
        take_at(basis_cols, net.plane, 0).astype(bf16),
        take_at(basis_cols, 4 + mine, 0).astype(bf16),
    )
    sp = jnp.concatenate([small_params.reshape(7, D), jnp.zeros((1, D), f32)])
    counts_me = jnp.concatenate([counts, net.me.reshape(1)])

    whole_tiles = per % 16 == 0
    order = list(reversed(everyone))
    first = interleave(net.collect(first, order[0]))
    rest_parts = net.collect(after(rest, first), order[0])
    for i, stage in enumerate(order[1:]):
        first_parts = net.collect(first, stage)
        if i == 0:
            first_parts, bases, old_terms, sp, counts_me = after(
                (first_parts, bases, old_terms, sp, counts_me), first
            )
        if stage is not order[-1]:
            first = interleave(first_parts)
            rest_parts, first = after((rest_parts, first), first_parts)
            rest = interleave(rest_parts)
            rest_parts = net.collect(rest, stage)
    if not whole_tiles:
        first_parts = [jnp.transpose(place(net.me, first_parts), (1, 0, 2, 3)).reshape(1, 3, D, D)]
    first_parts, sp, counts_me = lax.optimization_barrier((first_parts, sp, counts_me, rest, bases, old_terms))[:3]
    old_parts = net.trade(after(old_terms, rest), top)
    q, k, v, e, o, li, wqkv = attn_fwd(features, first_parts, net.me)
    rest_parts, old_parts = after((rest_parts, old_parts), o)
    rest, olds = interleave(rest_parts), jnp.stack(old_parts)
    for stage in reversed(stages[2:]):
        olds = net.widen(olds, stage)
    rest_parts = net.collect(after(rest, olds), order[-1])
    old_parts = net.collect(olds, stages[1])
    if not whole_tiles:
        rest = place(net.me, rest_parts)
        rest_parts = [
            jnp.concatenate(
                [rest[:, lo * per : hi * per].reshape(-1, D) for lo, hi in ((0, 1), (1, 3), (3, 5))]
            )[None]
        ]
    output, d1, do, *terms = rows_pass(
        counts_me, features, o, li, cotangent, after(rest_parts, olds), sp, inner
    )

    n_small = 16
    terms, old_parts = after((terms, old_parts), output)
    early_parts = net.trade(terms, stages[0])
    olds = interleave(old_parts)
    early_parts = after(early_parts, olds)
    for stage in stages[2:]:
        early_parts = net.trade(sum_cut(net, early_parts, stage, n_small), stage)
    terms = sum_cut(net, early_parts, stages[1], n_small)
    early_parts = net.trade(terms, stages[1])
    old_parts = net.collect(olds, stages[0])
    back = functools.partial(attn_bwd, x=features, q=q, k=k, v=v, e=e, o=o, do=do)
    acc, gw0 = back(0, acc=d1, wqkv=after(wqkv, terms, olds))
    early_parts, old_parts = after((early_parts, old_parts), gw0)
    top_terms = sum_top(net, early_parts, n_ffn, n_small)
    top_parts = net.trade(top_terms, top)
    grad_input, *terms = back(1, acc=acc, wqkv=after(wqkv, top_terms, old_parts), cut=(net.me, gw0, inner))

    terms, top_parts = lax.optimization_barrier((terms, top_parts))
    late_parts = net.trade(terms, stages[0])
    ffn = total([p[n_small:] for p in top_parts]).astype(bf16)
    ffn_parts = net.collect(ffn[None], stages[-1])
    late_parts = after(late_parts, ffn)
    for stage in stages[2:]:
        late_parts = net.trade(sum_cut(net, late_parts, stage), stage)
    terms = sum_cut(net, late_parts, stages[1])
    late_parts = net.trade(terms, stages[1])
    a_ffn = take_at(after(basis_ffn, terms), mine, 0).astype(bf16)
    early_part, ffn_parts, a_ffn = lax.optimization_barrier((late_parts[1], ffn_parts, a_ffn))
    wide = interleave(ffn_parts)
    late_parts, wide = lax.optimization_barrier((late_parts[:1] + [early_part] + late_parts[2:], wide))
    terms = sum_top(net, late_parts, n_attn)
    late_parts = net.trade(terms, top, (0, 1, 2))
    wide = after(wide, terms)
    ffn_parts = net.collect(wide, stages[len(stages) - 2])
    for stage in reversed(stages[:-2]):
        ffn_parts = net.collect(interleave(ffn_parts), stage)

    if whole_tiles:
        back_ffn = rotated_step_parts(net.me, ffn_parts, a_ffn, bases[2], old_parts, 0)
    else:
        olds = jnp.transpose(place(net.me, old_parts), (1, 0, 2, 3))
        full = place(net.me, ffn_parts).reshape(FF, D)
        both = rotated_step(full, a_ffn, bases[2], olds[:, :, : 2 * per].reshape(2, FF, D))
        back_ffn = take_at(jnp.stack([full, *both]).reshape(3, 4, inner, 2 * per, D), net.local, 2)
        back_ffn = net.cut(lambda d: take_at(back_ffn, d, 1), top)
    late_parts = after(late_parts, back_ffn)
    attn = total(late_parts).astype(bf16)
    attn = jnp.where(net.plane == 3, ffn[:n_attn], attn)[None]
    gs = total([join_high(p[:n_small]) for p in after(top_parts, attn)])
    grad_small = gs[0:7].reshape(-1)
    small_first = beta_one * small_moments[0] + (1.0 - beta_one) * grad_small
    small_second = beta_two * small_moments[1] + (1.0 - beta_two) * grad_small * grad_small
    small_new = small_params - rate_small * adam_direction(small_first, small_second)
    small_moments_new = jnp.stack([small_first, small_second])
    for stage in reversed(stages[1:]):
        attn_parts = net.collect(attn, stage)
        attn_parts, small_new, small_moments_new = lax.optimization_barrier(
            (attn_parts, small_new, small_moments_new)
        )
        attn = interleave(attn_parts)
    attn_parts = net.collect(attn, stages[0])
    back_ffn = net.trade(back_ffn, top, sources=(1, 2))
    if whole_tiles:
        back_attn = rotated_step_parts(net.me, attn_parts, bases[0], bases[1], old_parts, 2)
    else:
        full = place(net.me, attn_parts).reshape(D, D)
        both = rotated_step(full, bases[0], bases[1], olds[:, :, 2 * per :].reshape(2, D, D))
        back_attn = take_at(jnp.stack([full, *both]).reshape(3, 4, inner, per, D), net.local, 2)
        back_attn = net.cut(lambda d: take_at(back_attn, d, 1), top)
    back_ffn = after(back_ffn, back_attn)
    back_attn = net.trade(back_attn, top)
    if whole_tiles:
        grad_weights, moments_new, weights_new = finish(net, back_attn, back_ffn, moments_old, weights)
    else:
        back_attn = by_index(back_attn, net.plane)
        back_ffn = by_index(back_ffn, net.plane)
        grad_weights, rotated, update = (
            stacked([part[i] for part in back_attn], back_ffn[1][i], back_ffn[2][i]).astype(f32) for i in range(3)
        )
        moments_new = jnp.stack(
            [
                beta_one * moments_old[0] + (1.0 - beta_one) * rotated,
                beta_two * moments_old[1] + (1.0 - beta_two) * rotated * rotated,
            ]
        )
        weights_new = weights - rate_mats * update
    return (
        output,
        grad_input,
        grad_weights,
        moments_new,
        weights_new,
        grad_small,
        small_moments_new,
        small_new,
    )


def solution(mesh):
    rows = P(("dp", "fsdp"), None)
    blocks = P(("dp", "fsdp"), None, None)
    pair = P(None, ("dp", "fsdp"), None)
    return jax.shard_map(
        lambda *arrays: on_device(mesh, *arrays),
        mesh=mesh,
        in_specs=(blocks, blocks, P(("dp", "fsdp")), rows, P(), pair, P(), P(), P(), P()),
        out_specs=(blocks, blocks, rows, pair, rows, P(), P(), P()),
        check_vma=False,
    )
```

```python
import functools
import jax
import jax.numpy as jnp
from jax import lax
from jax.sharding import PartitionSpec as P
from jax.experimental import pallas as pl
from jax.experimental.pallas import tpu as pltpu

D = 512
HEADS = 4
FF = 1024
HD = 128
CTX = 1024
SLOTS = 1128
STEP = 10
PAD = 1152
RB = 384
NRB = PAD // RB
RBL = 576
SUB = 128
NRBL = PAD // RBL
scaling = HD ** (-0.5)
eps_norm = 1e-05
eps_adam = 1e-08
beta_one = 0.9
beta_two = 0.999
rate_mats = 0.1
rate_small = 0.5
axes = ("dp", "fsdp")
bf16 = jnp.bfloat16
f32 = jnp.float32
VLIM_FWD = 58 * 1024 * 1024
VLIM_ROWS = 46 * 1024 * 1024
VLIM_BWD = 46 * 1024 * 1024
VLIM_STEP = 24 * 1024 * 1024


def nt(a, b):
    return lax.dot_general(a, b, (((1,), (1,)), ((), ())), preferred_element_type=f32)


def nn(a, b):
    return lax.dot_general(a, b, (((1,), (0,)), ((), ())), preferred_element_type=f32)


def tn(a, b):
    return lax.dot_general(a, b, (((0,), (0,)), ((), ())), preferred_element_type=f32)


def put_in_order(me, parts, out):
    def move(j, carry):
        for c, part in enumerate(parts):
            out[(j * len(parts) + c) ^ me] = part[j]
        return carry

    lax.fori_loop(0, parts[0].shape[0], move, 0)


def attn_fwd_body(ways, *refs):
    me_ref, xc_ref, xr_ref, *refs = refs
    parts, (q_ref, k_ref, v_ref, e_ref, o_ref, li_ref, w_ref, ve_ref) = refs[:ways], refs[ways:]
    n, rb = pl.program_id(0), pl.program_id(1)

    @pl.when(jnp.logical_and(n == 0, rb == 0))
    def _():
        put_in_order(me_ref[0] & (w_ref.shape[0] - 1), parts, w_ref)

    @pl.when(rb == 0)
    def _():
        xc = xc_ref[0]
        k_ref[0] = nt(xc, w_ref[:, 1].reshape(D, D)).astype(bf16)
        v_ref[0] = nt(xc, w_ref[:, 2].reshape(D, D)).astype(bf16)
        for h in range(HEADS):
            ve_ref[h, :, 0:HD] = v_ref[0, :, h * HD : (h + 1) * HD]
            ve_ref[h, :, HD : 2 * HD] = jnp.ones((CTX, HD), bf16)

    rows = rb * RB + lax.broadcasted_iota(jnp.int32, (RB, 1), 0)
    xr = jnp.where(rows < SLOTS, xr_ref[0].astype(f32), 0.0).astype(bf16)
    q_ref[0] = (nt(xr, w_ref[:, 0].reshape(D, D)) * scaling).astype(bf16)
    lane = lax.broadcasted_iota(jnp.int32, (SUB, HD), 1) // (HD // HEADS)
    for r in range(0, RB, SUB):
        rs = slice(r, r + SUB)
        for h in range(HEADS):
            hs = slice(h * HD, (h + 1) * HD)
            s = nt(q_ref[0, rs, hs], k_ref[0, :, hs])
            m = jnp.max(s, axis=-1, keepdims=True)
            e = jnp.exp(s - m).astype(bf16)
            e_ref[0, h, rs] = e
            ov = nn(e, ve_ref[h])
            li = 1.0 / ov[:, HD:]
            scales = li if h == 0 else jnp.where(lane == h, li, scales)
            o_ref[0, rs, hs] = (ov[:, :HD] * li).astype(bf16)
        li_ref[0, rs] = scales


def attn_fwd(x, parts, me):
    n = x.shape[0]
    sd = jax.ShapeDtypeStruct
    everything = lambda shape: pl.BlockSpec(shape, lambda i, r: (0,) * len(shape))
    wshape = (len(parts) * parts[0].shape[0],) + parts[0].shape[1:]
    block = lambda w: pl.BlockSpec((1, RB, w), lambda i, r: (i, r, 0))
    context = pl.BlockSpec((1, CTX, D), lambda i, r: (i, 0, 0))
    return pl.pallas_call(
        functools.partial(attn_fwd_body, len(parts)),
        grid=(n, NRB),
        in_specs=[pl.BlockSpec(memory_space=pltpu.SMEM), context, block(D)]
        + [everything(w.shape) for w in parts],
        out_specs=[
            block(D),
            context,
            context,
            pl.BlockSpec((1, HEADS, RB, CTX), lambda i, r: (i, 0, r, 0)),
            block(D),
            block(HD),
            everything(wshape),
        ],
        out_shape=[
            sd((n, PAD, D), bf16),
            sd((n, CTX, D), bf16),
            sd((n, CTX, D), bf16),
            sd((n, HEADS, PAD, CTX), bf16),
            sd((n, PAD, D), bf16),
            sd((n, PAD, HD), f32),
            sd(wshape, bf16),
        ],
        scratch_shapes=[pltpu.VMEM((HEADS, CTX, 2 * HD), bf16)],
        compiler_params=pltpu.CompilerParams(
            dimension_semantics=("arbitrary", "arbitrary"), vmem_limit_bytes=VLIM_FWD
        ),
        cost_estimate=pl.CostEstimate(
            flops=14_000_000_000, transcendentals=n * HEADS * PAD * CTX, bytes_accessed=40_000_000
        ),
        name="attention_forward",
    )(me.reshape(1), x, x, *parts)


def lane_mean(v):
    return jnp.sum(v, axis=-1, keepdims=True) * (1.0 / D)


NSUB = 1


def rows_body(ways, cnt_ref, x_ref, o_ref, li_ref, c_ref, *refs):
    parts, (sp_ref,
            out_ref, d1_ref, do_ref, keep_ref, send_ref, gs_ref, go_ref, gi_ref, gb_ref,
            gbs, dus, dfs, hbs, das, osc, *placed) = refs[:ways], refs[ways:]
    w_ref = placed[0] if placed else parts[0]
    me = cnt_ref[cnt_ref.shape[0] - 1]
    pieces, small = 2 * keep_ref.shape[0], 2 * gs_ref.shape[0]
    n, rb = pl.program_id(0), pl.program_id(1)
    first = jnp.logical_and(n == 0, rb == 0)
    last = jnp.logical_and(n == pl.num_programs(0) - 1, rb == NRBL - 1)

    @pl.when(first)
    def _():
        go_ref[...] = jnp.zeros_like(go_ref)
        gi_ref[...] = jnp.zeros_like(gi_ref)
        gb_ref[...] = jnp.zeros_like(gb_ref)
        gs_ref[...] = jnp.zeros_like(gs_ref)
        if placed:
            put_in_order(me, parts, w_ref)

    per = w_ref.shape[1] // 5
    wo = w_ref[:, 0:per].reshape(D, D)
    wi = w_ref[:, per : 3 * per].reshape(FF, D)
    wb = w_ref[:, 3 * per :].reshape(FF, D)
    gain1, shift1 = sp_ref[0:1], sp_ref[1:2]
    bias2, gain2, shift2 = sp_ref[4:5], sp_ref[5:6], sp_ref[6:7]
    bias1 = jnp.concatenate([sp_ref[2:3], sp_ref[3:4]], axis=1)
    size = RBL // NSUB
    sums = []

    def chain(part):
        rs = slice(part * size, (part + 1) * size)
        here = pl.ds(pl.multiple_of(rb * RBL, RBL) + part * size, size)
        osc[here] = o_ref[0, rs]
        rows = rb * RBL + part * size + lax.broadcasted_iota(jnp.int32, (size, 1), 0)
        valid = rows < SLOTS
        live = rows < CTX + cnt_ref[n]
        at = nt(o_ref[0, rs], wo)
        yield
        r1 = jnp.where(valid, x_ref[0, rs].astype(f32), 0.0) + at
        c1 = r1 - lane_mean(r1)
        is1 = lax.rsqrt(lane_mean(c1 * c1) + eps_norm)
        xh1 = c1 * is1
        h = xh1 * gain1 + shift1
        hb = h.astype(bf16)
        hbs[here] = hb
        yield
        u = nt(hb, wi)
        yield
        u = u + bias1
        ex = jnp.exp2((-0.7213475204444817 * u) * u)
        t = 1.0 / (1.0 + 0.23164189 * jnp.abs(u))
        poly = t * (0.127414796 + t * (-0.142248368 + t * (0.7107068705 + t * (-0.7265760135 + t * 0.5307027145))))
        tail = poly * ex
        phi = jnp.where(u >= 0.0, 1.0 - tail, tail)
        gb = (u * phi).astype(bf16)
        gbs[here] = gb
        dgelu = phi + u * ex * 0.3989422804014327
        yield
        r2 = nn(gb, wb)
        yield
        r2 = h + r2 + bias2
        c2 = r2 - lane_mean(r2)
        is2 = lax.rsqrt(lane_mean(c2 * c2) + eps_norm)
        xh2 = c2 * is2
        out_ref[0, rs] = jnp.where(live, xh2 * gain2 + shift2, 0.0).astype(bf16)
        dy = jnp.where(live, c_ref[0, rs].astype(f32), 0.0)
        s5 = jnp.sum(dy * xh2, axis=0, keepdims=True)
        s6 = jnp.sum(dy, axis=0, keepdims=True)
        e2 = dy * gain2
        d2 = (e2 - lane_mean(e2) - xh2 * lane_mean(e2 * xh2)) * is2
        df = d2.astype(bf16)
        dfs[here] = df
        s4 = jnp.sum(df.astype(f32), axis=0, keepdims=True)
        yield
        dg = nt(df, wb)
        yield
        du = (dg * dgelu).astype(bf16)
        dus[here] = du
        s2 = jnp.sum(du.astype(f32), axis=0, keepdims=True)
        yield
        dh = nn(du, wi)
        yield
        dh = d2 + dh
        s0 = jnp.sum(dh * xh1, axis=0, keepdims=True)
        s1 = jnp.sum(dh, axis=0, keepdims=True)
        e1 = dh * gain1
        d1 = (e1 - lane_mean(e1) - xh1 * lane_mean(e1 * xh1)) * is1
        d1_ref[0, rs] = d1
        da = d1.astype(bf16)
        das[here] = da
        sums.append((s0, s1, s2[:, :D], s2[:, D:], s4, s5, s6))
        yield
        dm = nn(da, wo)
        yield
        for h in range(HEADS):
            hs = slice(h * HD, (h + 1) * HD)
            li = li_ref[0, rs, h * (HD // HEADS) : h * (HD // HEADS) + 1]
            do_ref[0, rs, hs] = (dm[:, hs] * li).astype(bf16)

    chains = [chain(i) for i in range(NSUB)]
    for i, c in enumerate(chains):
        for _ in range(len(chains) - 1 - i):
            next(c)
    done = 0
    while done < len(chains):
        done = 0
        for c in chains:
            try:
                next(c)
            except StopIteration:
                done += 1
    for i in range(7):
        total_i = sums[0][i]
        for s in sums[1:]:
            total_i = total_i + s[i]
        gs_ref[i : i + 1] += total_i

    @pl.when(rb == NRBL - 1)
    def _():
        for target, left, right in ((gi_ref, dus, hbs), (gb_ref, gbs, dfs), (go_ref, das, osc)):
            target[...] += tn(left[...], right[...])

    def write(core):
        for p in range(pieces):
            out = keep_ref if p % 2 == core else send_ref
            if p < 2:
                high = gs_ref[...].astype(bf16)
                out[0, : small // 2] = high
                out[0, small // 2 : small] = (gs_ref[...] - high.astype(f32)).astype(bf16)
            else:
                out[p // 2, :small] = jnp.zeros((small, D), bf16)
            at = small
            for target in (gi_ref, gb_ref, go_ref):
                size = target.shape[0] // pieces
                out[p // 2, at : at + size] = target[p * size : (p + 1) * size].astype(bf16)
                at += size

    for core in range(2):
        pl.when(jnp.logical_and(last, me % 2 == core))(functools.partial(write, core))


def rows_pass(counts, x, o, li, cot, rest, sp, pieces):
    n = x.shape[0]
    placed = []
    if len(rest) > 1:
        placed = [pltpu.VMEM((2 * rest[0].shape[0],) + rest[0].shape[1:], bf16)]
    cut = (pieces // 2, 16 + (D + 2 * FF) // pieces, D)
    sd = jax.ShapeDtypeStruct
    blk = pl.BlockSpec((1, RBL, D), lambda i, r, c: (i, r, 0))
    const = lambda *s: pl.BlockSpec(s, lambda i, r, c: (0,) * len(s))
    return pl.pallas_call(
        functools.partial(rows_body, len(rest)),
        grid_spec=pltpu.PrefetchScalarGridSpec(
            num_scalar_prefetch=1,
            grid=(n, NRBL),
            in_specs=[
                blk,
                blk,
                pl.BlockSpec((1, RBL, HD), lambda i, r, c: (i, r, 0)),
                blk,
            ]
            + [const(*w.shape) for w in rest]
            + [const(8, D)],
            out_specs=[blk, blk, blk, const(*cut), const(*cut)],
            scratch_shapes=[
                pltpu.VMEM((8, D), f32),
                pltpu.VMEM((D, D), f32),
                pltpu.VMEM((FF, D), f32),
                pltpu.VMEM((FF, D), f32),
                pltpu.VMEM((PAD, FF), bf16),
                pltpu.VMEM((PAD, FF), bf16),
                pltpu.VMEM((PAD, D), bf16),
                pltpu.VMEM((PAD, D), bf16),
                pltpu.VMEM((PAD, D), bf16),
                pltpu.VMEM((PAD, D), bf16),
            ]
            + placed,
        ),
        out_shape=[
            sd((n, SLOTS, D), bf16),
            sd((n, SLOTS, D), f32),
            sd((n, PAD, D), bf16),
            sd(cut, bf16),
            sd(cut, bf16),
        ],
        compiler_params=pltpu.CompilerParams(
            dimension_semantics=("arbitrary", "arbitrary"), vmem_limit_bytes=VLIM_ROWS
        ),
        cost_estimate=pl.CostEstimate(
            flops=n * 18_000_000_000 // 2, transcendentals=n * PAD * FF * 2, bytes_accessed=n * 15_000_000
        ),
        name="rows_forward_backward",
    )(counts, x, o, li, cot, *rest, sp)


def attn_bwd_body(cut, *refs):
    x_ref, q_ref, k_ref, v_ref, e_ref, o_ref, do_ref, acc_ref, w_ref, *refs = refs
    (me_ref, other_ref), refs = (refs[:2], refs[2:]) if cut else ((None, None), refs)
    gi_ref, *outs = refs[:-4]
    dkt_ref, dvt_ref, gw_ref, xs_ref = refs[-4:]
    n, rb = pl.program_id(0), pl.program_id(1)

    @pl.when(jnp.logical_and(n == 0, rb == 0))
    def _():
        gw_ref[...] = jnp.zeros_like(gw_ref)

    @pl.when(rb == 0)
    def _():
        dkt_ref[...] = jnp.zeros_like(dkt_ref)
        dvt_ref[...] = jnp.zeros_like(dvt_ref)

    rows = rb * RBL + lax.broadcasted_iota(jnp.int32, (RBL, 1), 0)
    x = jnp.where(rows < SLOTS, x_ref[0].astype(f32), 0.0).astype(bf16)
    here = pl.ds(pl.multiple_of(rb * RBL, RBL), RBL)
    xs_ref[here] = x
    dqs = []
    for h in range(2):
        hs = slice(h * HD, (h + 1) * HD)
        do = do_ref[0, :, hs]
        t = jnp.sum(do.astype(f32) * o_ref[0, :, hs].astype(f32), axis=-1, keepdims=True)
        dp = nt(do, v_ref[0, :, hs])
        e = e_ref[0, h]
        ds = (e.astype(f32) * (dp - t)).astype(bf16)
        dqs.append(nn(ds, k_ref[0, :, hs]).astype(bf16))
        dvt_ref[hs] += tn(do, e)
        dkt_ref[hs] += tn(q_ref[0, :, hs], ds)
    dq = jnp.concatenate(dqs, axis=1)
    wq, wk, wv = (w_ref[:, i].reshape(2 * HD, D) for i in range(3))
    gw_ref[0] += tn(dq, x) * scaling
    gi_ref[0, here] = acc_ref[0] + nn(dq, wq) * scaling

    @pl.when(rb == NRBL - 1)
    def _():
        dkt, dvt = dkt_ref[...].astype(bf16), dvt_ref[...].astype(bf16)
        xc = xs_ref[0:CTX]
        gw_ref[1] += nn(dkt, xc)
        gw_ref[2] += nn(dvt, xc)
        gi_ref[0, 0:CTX] += tn(dkt, wk) + tn(dvt, wv)

    last = jnp.logical_and(n == pl.num_programs(0) - 1, rb == NRBL - 1)
    if not cut:

        @pl.when(last)
        def _():
            outs[0][...] = gw_ref[...]

        return

    def write(core):
        pieces, size = 2 * outs[0].shape[0], outs[0].shape[2]
        for p in range(pieces):
            out = outs[0] if p % 2 == core else outs[1]
            half, row = divmod(p * size, 2 * HD)
            for i in range(3):
                out[p // 2, i] = (gw_ref if half else other_ref)[i, row : row + size].astype(bf16)

    for core in range(2):
        pl.when(jnp.logical_and(last, me_ref[0] % 2 == core))(functools.partial(write, core))


def attn_bwd(pair, x, q, k, v, e, o, do, acc, wqkv, cut=()):
    n = x.shape[0]
    sd = jax.ShapeDtypeStruct
    ways = wqkv.shape[0]
    if ways > 1:
        wspec = pl.BlockSpec((ways // 2,) + wqkv.shape[1:], lambda i, r: (pair, 0, 0, 0))
    else:
        wspec = pl.BlockSpec((1, 3, 2 * HD, D), lambda i, r: (0, 0, pair, 0))
    heads = pl.BlockSpec((1, RBL, 2 * HD), lambda i, r: (i, r, pair))
    context = pl.BlockSpec((1, CTX, 2 * HD), lambda i, r: (i, 0, pair))
    rows = pl.BlockSpec((1, RBL, D), lambda i, r: (i, r, 0))
    grads = lambda shape: pl.BlockSpec(shape, lambda i, r: (0,) * len(shape))
    outs = [sd((cut[2] // 2, 3, D // cut[2], D), bf16)] * 2 if cut else [sd((3, 2 * HD, D), f32)]
    return pl.pallas_call(
        functools.partial(attn_bwd_body, bool(cut)),
        grid=(n, NRBL),
        in_specs=[
            rows,
            heads,
            context,
            context,
            pl.BlockSpec((1, 2, RBL, CTX), lambda i, r: (i, pair, r, 0)),
            heads,
            heads,
            rows,
            wspec,
        ]
        + ([pl.BlockSpec(memory_space=pltpu.SMEM), grads((3, 2 * HD, D))] if cut else []),
        out_specs=[pl.BlockSpec((1, PAD, D), lambda i, r: (i, 0, 0))] + [grads(g.shape) for g in outs],
        out_shape=[sd((n, SLOTS, D), f32)] + outs,
        scratch_shapes=[
            pltpu.VMEM((2 * HD, CTX), f32),
            pltpu.VMEM((2 * HD, CTX), f32),
            pltpu.VMEM((3, 2 * HD, D), f32),
            pltpu.VMEM((PAD, D), bf16),
        ],
        input_output_aliases={7: 0},
        compiler_params=pltpu.CompilerParams(
            dimension_semantics=("arbitrary", "arbitrary"), vmem_limit_bytes=VLIM_BWD
        ),
        cost_estimate=pl.CostEstimate(
            flops=9_000_000_000, transcendentals=0, bytes_accessed=24_000_000
        ),
        name="attention_backward",
    )(x, q, k, v, e, o, do, acc, wqkv, *([cut[0].reshape(1), cut[1]] if cut else []))


def adam_direction(first_new, second_new):
    return (first_new * (1.0 / (1.0 - beta_one**STEP))) / (
        jnp.sqrt(second_new * (1.0 / (1.0 - beta_two**STEP))) + eps_adam
    )


def rotate(grad, rows_basis, cols_basis, first_old, second_old):
    r = nn(tn(rows_basis, grad).astype(bf16), cols_basis)
    first_new = beta_one * first_old.astype(f32) + (1.0 - beta_one) * r
    second_new = beta_two * second_old.astype(f32) + (1.0 - beta_two) * r * r
    step = adam_direction(first_new, second_new).astype(bf16)
    return r.astype(bf16), nn(rows_basis, nt(step, cols_basis).astype(bf16)).astype(bf16)


def rotate_body(g_ref, a_ref, b_ref, m_ref, r_ref, u_ref):
    r_ref[...], u_ref[...] = rotate(g_ref[...], a_ref[...], b_ref[...], m_ref[0], m_ref[1])


def rotated_step(grad, rows_basis, cols_basis, moments):
    rows = grad.shape[0]
    sd = jax.ShapeDtypeStruct
    return pl.pallas_call(
        rotate_body,
        out_shape=[sd((rows, D), bf16), sd((rows, D), bf16)],
        compiler_params=pltpu.CompilerParams(vmem_limit_bytes=VLIM_STEP),
        cost_estimate=pl.CostEstimate(
            flops=4 * rows * D * (rows + D), transcendentals=rows * D, bytes_accessed=2 * rows * (rows + 5 * D)
        ),
        name="rotated_step",
    )(grad, rows_basis, cols_basis, moments)


def rotate_parts_body(me_ref, *refs):
    grads, a_ref, b_ref, olds, outs = refs[:2], refs[2], refs[3], refs[4:6], refs[6:10]
    g_ref, m_ref, r_ref, u_ref = refs[10:]
    me = me_ref[0]
    planes, inner, rows = len(outs), g_ref.shape[0], r_ref.shape[0]
    per = rows // (planes * inner)
    put_in_order(me & (inner - 1), grads, g_ref)
    put_in_order(me, olds, m_ref)
    r_ref[...], u_ref[...] = rotate(
        g_ref[...].reshape(rows, D), a_ref[...], b_ref[...],
        m_ref[:, 0].reshape(rows, D), m_ref[:, 1].reshape(rows, D),
    )
    n = g_ref.shape[1]
    for rel, out in enumerate(outs):
        row = pl.multiple_of((me ^ (rel * inner)) * per, per)
        out[0] = g_ref[row // n, pl.ds(pl.multiple_of(row % n, per), per)]
        out[1] = r_ref[pl.ds(row, per)]
        out[2] = u_ref[pl.ds(row, per)]


def rotated_step_parts(me, grads, rows_basis, cols_basis, olds, block):
    rows = rows_basis.shape[0]
    inner = 2 * grads[0].shape[0]
    count = 2 * olds[0].shape[0]
    per = rows // count
    full = lambda shape: pl.BlockSpec(shape, lambda i: (0,) * len(shape))
    return pl.pallas_call(
        rotate_parts_body,
        grid=(1,),
        in_specs=[pl.BlockSpec(memory_space=pltpu.SMEM)]
        + [full(g.shape) for g in grads]
        + [full(rows_basis.shape), full(cols_basis.shape)]
        + [pl.BlockSpec((count // 2, 2, per, D), lambda i: (0, 0, block, 0))] * 2,
        out_specs=[full((3, per, D))] * (count // inner),
        out_shape=[jax.ShapeDtypeStruct((3, per, D), bf16)] * (count // inner),
        scratch_shapes=[
            pltpu.VMEM((inner, rows // inner, D), bf16),
            pltpu.VMEM((count, 2, per, D), bf16),
            pltpu.VMEM((rows, D), bf16),
            pltpu.VMEM((rows, D), bf16),
        ],
        compiler_params=pltpu.CompilerParams(vmem_limit_bytes=VLIM_STEP),
        cost_estimate=pl.CostEstimate(
            flops=4 * rows * D * (rows + D), transcendentals=rows * D, bytes_accessed=2 * rows * (rows + 5 * D)
        ),
        name="rotated_step",
    )(me.reshape(1), *grads, rows_basis, cols_basis, *(pltpu.with_memory_space_constraint(v, pltpu.HBM) for v in olds))


class Net:
    def __init__(self, mesh):
        self.count = mesh.size
        self.bits = self.count.bit_length() - 1
        self.inner_bits = self.bits - 2
        self.inner = 1 << self.inner_bits
        self.me = lax.axis_index(axes)
        self.local = self.me & (self.inner - 1)
        self.plane = self.me >> self.inner_bits
        stages = [(0, 1)]
        while stages[-1][0] + stages[-1][1] < self.inner_bits:
            low = stages[-1][0] + stages[-1][1]
            stages.append((low, min(2, self.inner_bits - low)))
        self.stages = stages
        self.top = (self.inner_bits, 2)

    def swap(self, value, offset, targets=(0, 1, 2, 3), sources=(0, 1, 2, 3)):
        pairs = [(i, i ^ offset) for i in range(self.count)]
        pairs = [
            (i, j) for i, j in pairs
            if (i >> self.inner_bits) in sources and (j >> self.inner_bits) in targets
        ]
        return lax.ppermute(value, axes, pairs)

    def digit(self, stage):
        return (self.me >> stage[0]) & ((1 << stage[1]) - 1)

    def collect(self, value, stage):
        return [value] + [self.swap(value, rel << stage[0]) for rel in range(1, 1 << stage[1])]

    def widen(self, value, stage):
        return interleave(self.collect(value, stage))

    def cut(self, pick, stage):
        mine = self.digit(stage)
        return [pick(mine ^ rel) for rel in range(1 << stage[1])]

    def trade(self, terms, stage, targets=(0, 1, 2, 3), sources=(0, 1, 2, 3)):
        return list(terms[:1]) + [
            self.swap(term, rel << stage[0], targets, sources) for rel, term in enumerate(terms) if rel
        ]


def after(value, *earlier):
    return lax.optimization_barrier((value, earlier))[0]


def interleave(parts):
    value = jnp.stack(parts, axis=1)
    return value.reshape((-1,) + value.shape[2:])


def total(parts):
    parts = [p.astype(f32) for p in parts]
    while len(parts) > 1:
        parts = [a + b for a, b in zip(parts[0::2], parts[1::2])]
    return parts[0]


def take_at(value, index, axis):
    return lax.dynamic_index_in_dim(value, index, axis, keepdims=False)


def join_high(pair):
    half = pair.shape[0] // 2
    return pair[:half].astype(f32) + pair[half:].astype(f32)


def sum_cut_body(low, bits, small, me_ref, *refs):
    size = 1 << bits
    parts, terms = refs[:-size], refs[-size:]
    digit = (me_ref[0] >> low) & (size - 1)
    if small:
        whole = total([join_high(p[0, :small]) for p in parts])
        high = whole.astype(bf16)
        pair = jnp.concatenate([high, (whole - high.astype(f32)).astype(bf16)])
    for rel, term in enumerate(terms):
        for j in range(term.shape[0]):
            piece = j * size + (digit ^ rel)
            if small:
                term[j, :small] = pair
                term[j, small:] = total([p[piece, small:] for p in parts]).astype(bf16)
            else:
                term[j] = total([p[piece] for p in parts]).astype(bf16)


def sum_top_body(low, small, me_ref, *refs):
    parts, terms = refs[:-4], refs[-4:]
    plane = (me_ref[0] >> low) & 3
    for rel, term in enumerate(terms):
        goal = plane ^ rel
        if not small:
            piece = jnp.minimum(goal, 2)
            term[...] = total([p[0, piece] for p in parts]).astype(bf16)
            continue
        rows = term.shape[0] - small
        whole = total([join_high(p[0, :small]) for p in parts])
        high = whole.astype(bf16)
        term[:small] = jnp.concatenate([high, (whole - high.astype(f32)).astype(bf16)])

        def give(k):
            count = min(rows, parts[0].shape[1] - small - k * rows)
            begin = small + k * rows
            term[small : small + count] = total([p[0, begin : begin + count] for p in parts]).astype(bf16)
            if count < rows:
                term[small + count :] = jnp.zeros((rows - count, D), bf16)

        for k in range(3):
            pl.when(jnp.maximum(goal, 1) == k + 1)(functools.partial(give, k))


def deal(body, me, parts, term, count):
    full = lambda dims: pl.BlockSpec(dims, lambda i: (0,) * len(dims))
    return pl.pallas_call(
        body,
        grid=(1,),
        in_specs=[pl.BlockSpec(memory_space=pltpu.SMEM)] + [full(p.shape) for p in parts],
        out_specs=[full(term)] * count,
        out_shape=[pltpu.HBM(term, bf16)] * count,
        compiler_params=pltpu.CompilerParams(vmem_limit_bytes=VLIM_STEP),
        cost_estimate=pl.CostEstimate(
            flops=0, transcendentals=0, bytes_accessed=4 * len(parts) * parts[0].size
        ),
        name="sum_and_deal",
    )(me.reshape(1), *parts)


def sum_cut(net, parts, stage, small=0):
    size = 1 << stage[1]
    shape = parts[0].shape
    body = functools.partial(sum_cut_body, *stage, small)
    return deal(body, net.me, parts, (shape[0] // size,) + shape[1:], size)


def sum_top(net, parts, rows, small=0):
    body = functools.partial(sum_top_body, net.top[0], small)
    return deal(body, net.me, parts, (small + rows, D), 4)


def place_body(me_ref, *refs):
    *parts, out = refs
    put_in_order(me_ref[0] & (out.shape[0] - 1), parts, out)


def place(me, parts):
    size = len(parts) * parts[0].shape[0]
    shape = jax.ShapeDtypeStruct((size,) + parts[0].shape[1:], parts[0].dtype)
    return pl.pallas_call(
        place_body,
        in_specs=[pl.BlockSpec(memory_space=pltpu.SMEM)]
        + [pl.BlockSpec(memory_space=pltpu.VMEM)] * len(parts),
        out_specs=pl.BlockSpec(memory_space=pltpu.VMEM),
        out_shape=shape,
        compiler_params=pltpu.CompilerParams(vmem_limit_bytes=24 * 1024 * 1024),
        cost_estimate=pl.CostEstimate(flops=0, transcendentals=0, bytes_accessed=4 * shape.size),
        name="place",
    )(me.reshape(1), *parts)


def finish_body(low, me_ref, *refs):
    attn, ffn = refs[:4], refs[4:8]
    moments_ref, weights_ref, grad_ref, new_ref, out_ref = refs[8:]
    plane = (me_ref[0] >> low) & 3
    per = attn[0].shape[1]
    rows = 8 * per

    def choose(parts, plain, kind):
        value = parts[0][kind].astype(f32)
        for rel in range(1, 4):
            value = jnp.where(plane == (plain ^ rel), parts[rel][kind].astype(f32), value)
        return value.astype(bf16)

    row = lax.broadcasted_iota(jnp.int32, (rows, rows), 0)
    source = lax.broadcasted_iota(jnp.int32, (rows, rows), 1)
    group, slot = row // 8, row % 8
    wanted = jnp.where(
        slot < 4, slot * per + group, (4 + 2 * ((slot - 4) // 2)) * per + 2 * group + slot % 2
    )
    order = jnp.where(source == wanted, 1.0, 0.0).astype(bf16)

    def plain(kind):
        parts = [choose(attn, b, kind) for b in range(4)] + [choose(ffn, f, kind) for f in (1, 2)]
        return nn(order, jnp.concatenate(parts))

    grad_ref[...] = plain(0)
    turned = plain(1)
    new_ref[0] = beta_one * moments_ref[0] + (1.0 - beta_one) * turned
    new_ref[1] = beta_two * moments_ref[1] + (1.0 - beta_two) * turned * turned
    out_ref[...] = weights_ref[...] - rate_mats * plain(2)


def finish(net, attn, ffn, moments, weights):
    full = lambda shape: pl.BlockSpec(shape, lambda i: (0,) * len(shape))
    arrays = [*attn, *ffn, moments, weights]
    outs = [weights, moments, weights]
    return pl.pallas_call(
        functools.partial(finish_body, net.top[0]),
        grid=(1,),
        in_specs=[pl.BlockSpec(memory_space=pltpu.SMEM)] + [full(v.shape) for v in arrays],
        out_specs=[full(v.shape) for v in outs],
        out_shape=[jax.ShapeDtypeStruct(v.shape, f32) for v in outs],
        compiler_params=pltpu.CompilerParams(vmem_limit_bytes=VLIM_STEP),
        cost_estimate=pl.CostEstimate(flops=50_000_000, transcendentals=0, bytes_accessed=3_000_000),
        name="finish",
    )(net.me.reshape(1), *arrays)


def by_index(parts, index):
    return [
        functools.reduce(
            lambda rest, r: jnp.where(index == (b ^ r), parts[r], rest), range(1, len(parts)), parts[0]
        )
        for b in range(len(parts))
    ]


def on_device(mesh, features, cotangent, counts, weights, small_params, moments_old, small_moments,
              basis_attn, basis_ffn, basis_cols):
    net = Net(mesh)
    per = weights.shape[0] // 8
    everyone = net.stages + [net.top]

    def by_matrix(stacked):
        groups = stacked.reshape(per, 8, D)
        return (
            jnp.transpose(groups[:, 0:4], (1, 0, 2)),
            groups[:, 4:6].reshape(2 * per, D),
            groups[:, 6:8].reshape(2 * per, D),
        )

    def stacked(attn, inner, outer):
        return jnp.concatenate(
            [jnp.stack(attn, axis=1), inner.reshape(per, 2, D), outer.reshape(per, 2, D)], axis=1
        ).reshape(8 * per, D)

    inner = net.inner
    n_attn, n_ffn = D // inner, FF // inner
    ffn_of = lambda plane: jnp.clip(plane - 1, 0, 1)
    stages, top = net.stages, net.top

    own_attn, own_in, own_out = by_matrix(weights.astype(bf16))
    first = own_attn[None, 0:3]
    rest = jnp.concatenate([own_attn[3], own_in, own_out])[None]
    olds = [by_matrix(moments_old[i].astype(bf16)) for i in range(2)]
    old_attn = jnp.stack([m[0] for m in olds], axis=1)
    old_ffn = jnp.stack([jnp.stack([m[1], m[2]]) for m in olds], axis=1)
    old_terms = net.cut(
        lambda d: jnp.concatenate([take_at(old_ffn, ffn_of(d), 0), take_at(old_attn, d, 0)], axis=1), top
    )
    mine = ffn_of(net.plane)
    sp = jnp.concatenate([small_params.reshape(7, D), jnp.zeros((1, D), f32)])
    counts_me = jnp.concatenate([counts, net.me.reshape(1)])

    whole_tiles = per % 16 == 0
    order = list(reversed(everyone))
    first = interleave(net.collect(first, order[0]))
    rest_parts = net.collect(after(rest, first), order[0])
    for i, stage in enumerate(order[1:]):
        first_parts = net.collect(first, stage)
        if stage is not order[-1]:
            first = interleave(first_parts)
            rest_parts, first, old_terms, sp, counts_me = after(
                (rest_parts, first, old_terms, sp, counts_me), first_parts
            )
            rest = interleave(rest_parts)
            rest_parts = net.collect(rest, stage)
    if not whole_tiles:
        first_parts = [jnp.transpose(place(net.me, first_parts), (1, 0, 2, 3)).reshape(1, 3, D, D)]
    first_parts, sp, counts_me = lax.optimization_barrier((first_parts, sp, counts_me, rest, old_terms))[:3]
    old_parts = net.trade(after(old_terms, rest), top)
    q, k, v, e, o, li, wqkv = attn_fwd(features, first_parts, net.me)
    rest_parts, old_parts = after((rest_parts, old_parts), o)
    rest, olds = interleave(rest_parts), jnp.stack(old_parts)
    for stage in reversed(stages[2:]):
        olds = net.widen(olds, stage)
    rest_parts = net.collect(after(rest, olds), order[-1])
    old_parts = net.collect(olds, stages[1])
    if not whole_tiles:
        rest = place(net.me, rest_parts)
        rest_parts = [
            jnp.concatenate(
                [rest[:, lo * per : hi * per].reshape(-1, D) for lo, hi in ((0, 1), (1, 3), (3, 5))]
            )[None]
        ]
    output, d1, do, *terms = rows_pass(
        counts_me, features, o, li, cotangent, after(rest_parts, olds), sp, inner
    )

    n_small = 16
    terms, old_parts = after((terms, old_parts), output)
    early_parts = net.trade(terms, stages[0])
    olds = interleave(old_parts)
    early_parts = after(early_parts, olds)
    for stage in stages[2:]:
        early_parts = net.trade(sum_cut(net, early_parts, stage, n_small), stage)
    terms = sum_cut(net, early_parts, stages[1], n_small)
    early_parts = net.trade(terms, stages[1])
    old_parts = net.collect(olds, stages[0])
    back = functools.partial(attn_bwd, x=features, q=q, k=k, v=v, e=e, o=o, do=do)
    acc, gw0 = back(0, acc=d1, wqkv=after(wqkv, terms, olds))
    early_parts, old_parts = after((early_parts, old_parts), gw0)
    top_terms = sum_top(net, early_parts, n_ffn, n_small)
    top_parts = net.trade(top_terms, top)
    grad_input, *terms = back(1, acc=acc, wqkv=after(wqkv, top_terms, old_parts), cut=(net.me, gw0, inner))

    terms, top_parts = lax.optimization_barrier((terms, top_parts))
    late_parts = net.trade(terms, stages[0])
    ffn = total([p[n_small:] for p in top_parts]).astype(bf16)
    ffn_parts = net.collect(ffn[None], stages[-1])
    late_parts = after(late_parts, ffn)
    for stage in stages[2:]:
        late_parts = net.trade(sum_cut(net, late_parts, stage), stage)
    terms = sum_cut(net, late_parts, stages[1])
    late_parts = net.trade(terms, stages[1])
    a_ffn, b_ffn = after((basis_ffn, basis_cols), terms)
    a_ffn, b_ffn = take_at(a_ffn, mine, 0).astype(bf16), take_at(b_ffn, 4 + mine, 0).astype(bf16)
    early_part, ffn_parts, a_ffn, b_ffn = lax.optimization_barrier((late_parts[1], ffn_parts, a_ffn, b_ffn))
    wide = interleave(ffn_parts)
    late_parts, wide = lax.optimization_barrier((late_parts[:1] + [early_part] + late_parts[2:], wide))
    terms = sum_top(net, late_parts, n_attn)
    late_parts = net.trade(terms, top)
    wide = after(wide, terms)
    ffn_parts = net.collect(wide, stages[len(stages) - 2])
    for stage in reversed(stages[:-2]):
        ffn_parts = net.collect(interleave(ffn_parts), stage)

    if whole_tiles:
        back_ffn = rotated_step_parts(net.me, ffn_parts, a_ffn, b_ffn, old_parts, 0)
    else:
        olds = jnp.transpose(place(net.me, old_parts), (1, 0, 2, 3))
        full = place(net.me, ffn_parts).reshape(FF, D)
        both = rotated_step(full, a_ffn, b_ffn, olds[:, :, : 2 * per].reshape(2, FF, D))
        back_ffn = take_at(jnp.stack([full, *both]).reshape(3, 4, inner, 2 * per, D), net.local, 2)
        back_ffn = net.cut(lambda d: take_at(back_ffn, d, 1), top)
    late_parts = after(late_parts, back_ffn)
    attn = total(late_parts).astype(bf16)
    attn = jnp.where(net.plane == 3, ffn[:n_attn], attn)[None]
    gs = total([join_high(p[:n_small]) for p in after(top_parts, attn)])
    a_attn, b_attn = after((basis_attn, basis_cols), attn)
    a_attn, b_attn = (take_at(basis, net.plane, 0).astype(bf16) for basis in (a_attn, b_attn))
    for stage in reversed(stages[1:]):
        attn_parts = net.collect(attn, stage)
        attn_parts, gs, a_attn, b_attn = lax.optimization_barrier((attn_parts, gs, a_attn, b_attn))
        attn = interleave(attn_parts)
    attn_parts = net.collect(attn, stages[0])
    back_ffn = net.trade(back_ffn, top)
    if whole_tiles:
        back_attn = rotated_step_parts(net.me, attn_parts, a_attn, b_attn, old_parts, 2)
    else:
        full = place(net.me, attn_parts).reshape(D, D)
        both = rotated_step(full, a_attn, b_attn, olds[:, :, 2 * per :].reshape(2, D, D))
        back_attn = take_at(jnp.stack([full, *both]).reshape(3, 4, inner, per, D), net.local, 2)
        back_attn = net.cut(lambda d: take_at(back_attn, d, 1), top)
    back_ffn, gs = after((back_ffn, gs), back_attn)
    back_attn = net.trade(back_attn, top)
    grad_small = gs[0:7].reshape(-1)
    small_first = beta_one * small_moments[0] + (1.0 - beta_one) * grad_small
    small_second = beta_two * small_moments[1] + (1.0 - beta_two) * grad_small * grad_small
    small_new = small_params - rate_small * adam_direction(small_first, small_second)
    small_moments_new = jnp.stack([small_first, small_second])
    back_attn, small_new, small_moments_new = lax.optimization_barrier(
        (back_attn, small_new, small_moments_new)
    )
    if whole_tiles:
        grad_weights, moments_new, weights_new = finish(net, back_attn, back_ffn, moments_old, weights)
    else:
        back_attn = by_index(back_attn, net.plane)
        back_ffn = by_index(back_ffn, net.plane)
        grad_weights, rotated, update = (
            stacked([part[i] for part in back_attn], back_ffn[1][i], back_ffn[2][i]).astype(f32) for i in range(3)
        )
        moments_new = jnp.stack(
            [
                beta_one * moments_old[0] + (1.0 - beta_one) * rotated,
                beta_two * moments_old[1] + (1.0 - beta_two) * rotated * rotated,
            ]
        )
        weights_new = weights - rate_mats * update
    return (
        output,
        grad_input,
        grad_weights,
        moments_new,
        weights_new,
        grad_small,
        small_moments_new,
        small_new,
    )


def solution(mesh):
    rows = P(("dp", "fsdp"), None)
    blocks = P(("dp", "fsdp"), None, None)
    pair = P(None, ("dp", "fsdp"), None)
    return jax.shard_map(
        lambda *arrays: on_device(mesh, *arrays),
        mesh=mesh,
        in_specs=(blocks, blocks, P(("dp", "fsdp")), rows, P(), pair, P(), P(), P(), P()),
        out_specs=(blocks, blocks, rows, pair, rows, P(), P(), P()),
        check_vma=False,
    )
```

```python
import functools
import jax
import jax.numpy as jnp
from jax import lax
from jax.sharding import PartitionSpec as P
from jax.experimental import pallas as pl
from jax.experimental.pallas import tpu as pltpu

D = 512
HEADS = 4
FF = 1024
HD = 128
CTX = 1024
SLOTS = 1128
STEP = 10
PAD = 1152
RB = 576
NRB = PAD // RB
RBL = 576
SUB = 144
NRBL = PAD // RBL
scaling = HD ** (-0.5)
eps_norm = 1e-05
eps_adam = 1e-08
beta_one = 0.9
beta_two = 0.999
rate_mats = 0.1
rate_small = 0.5
axes = ("dp", "fsdp")
bf16 = jnp.bfloat16
f32 = jnp.float32
VLIM_FWD = 52 * 1024 * 1024
VLIM_ROWS = 46 * 1024 * 1024
VLIM_BWD = 46 * 1024 * 1024
VLIM_STEP = 20 * 1024 * 1024


def nt(a, b):
    return lax.dot_general(a, b, (((1,), (1,)), ((), ())), preferred_element_type=f32)


def nn(a, b):
    return lax.dot_general(a, b, (((1,), (0,)), ((), ())), preferred_element_type=f32)


def tn(a, b):
    return lax.dot_general(a, b, (((0,), (0,)), ((), ())), preferred_element_type=f32)


def put_in_order(me, parts, out):
    def move(j, carry):
        for c, part in enumerate(parts):
            out[(j * len(parts) + c) ^ me] = part[j]
        return carry

    lax.fori_loop(0, parts[0].shape[0], move, 0)


def attn_fwd_body(ways, *refs):
    me_ref, xc_ref, xr_ref, *refs = refs
    parts, (q_ref, k_ref, v_ref, e_ref, o_ref, li_ref, w_ref, ve_ref) = refs[:ways], refs[ways:]
    n, rb = pl.program_id(0), pl.program_id(1)

    @pl.when(jnp.logical_and(n == 0, rb == 0))
    def _():
        put_in_order(me_ref[0] & (w_ref.shape[0] - 1), parts, w_ref)

    @pl.when(rb == 0)
    def _():
        xc = xc_ref[0]
        k_ref[0] = nt(xc, w_ref[:, 1].reshape(D, D)).astype(bf16)
        v_ref[0] = nt(xc, w_ref[:, 2].reshape(D, D)).astype(bf16)
        for h in range(HEADS):
            ve_ref[h, :, 0:HD] = v_ref[0, :, h * HD : (h + 1) * HD]
            ve_ref[h, :, HD : 2 * HD] = jnp.ones((CTX, HD), bf16)

    rows = rb * RB + lax.broadcasted_iota(jnp.int32, (RB, 1), 0)
    xr = jnp.where(rows < SLOTS, xr_ref[0].astype(f32), 0.0).astype(bf16)
    q_ref[0] = (nt(xr, w_ref[:, 0].reshape(D, D)) * scaling).astype(bf16)
    lane = lax.broadcasted_iota(jnp.int32, (SUB, HD), 1) // (HD // HEADS)
    for r in range(0, RB, SUB):
        rs = slice(r, r + SUB)
        for h in range(HEADS):
            hs = slice(h * HD, (h + 1) * HD)
            s = nt(q_ref[0, rs, hs], k_ref[0, :, hs])
            m = jnp.max(s, axis=-1, keepdims=True)
            e = jnp.exp(s - m).astype(bf16)
            e_ref[0, h, rs] = e
            ov = nn(e, ve_ref[h])
            li = 1.0 / ov[:, HD:]
            scales = li if h == 0 else jnp.where(lane == h, li, scales)
            o_ref[0, rs, hs] = (ov[:, :HD] * li).astype(bf16)
        li_ref[0, rs] = scales


def attn_fwd(x, parts, me):
    n = x.shape[0]
    sd = jax.ShapeDtypeStruct
    everything = lambda shape: pl.BlockSpec(shape, lambda i, r: (0,) * len(shape))
    wshape = (len(parts) * parts[0].shape[0],) + parts[0].shape[1:]
    block = lambda w: pl.BlockSpec((1, RB, w), lambda i, r: (i, r, 0))
    context = pl.BlockSpec((1, CTX, D), lambda i, r: (i, 0, 0))
    return pl.pallas_call(
        functools.partial(attn_fwd_body, len(parts)),
        grid=(n, NRB),
        in_specs=[pl.BlockSpec(memory_space=pltpu.SMEM), context, block(D)]
        + [everything(w.shape) for w in parts],
        out_specs=[
            block(D),
            context,
            context,
            pl.BlockSpec((1, HEADS, RB, CTX), lambda i, r: (i, 0, r, 0)),
            block(D),
            block(HD),
            everything(wshape),
        ],
        out_shape=[
            sd((n, PAD, D), bf16),
            sd((n, CTX, D), bf16),
            sd((n, CTX, D), bf16),
            sd((n, HEADS, PAD, CTX), bf16),
            sd((n, PAD, D), bf16),
            sd((n, PAD, HD), f32),
            sd(wshape, bf16),
        ],
        scratch_shapes=[pltpu.VMEM((HEADS, CTX, 2 * HD), bf16)],
        compiler_params=pltpu.CompilerParams(
            dimension_semantics=("arbitrary", "arbitrary"), vmem_limit_bytes=VLIM_FWD
        ),
        cost_estimate=pl.CostEstimate(
            flops=14_000_000_000, transcendentals=n * HEADS * PAD * CTX, bytes_accessed=40_000_000
        ),
        name="attention_forward",
    )(me.reshape(1), x, x, *parts)


def lane_mean(v):
    return jnp.sum(v, axis=-1, keepdims=True) * (1.0 / D)


NSUB = 1


def rows_body(ways, cnt_ref, x_ref, o_ref, li_ref, c_ref, *refs):
    parts, (sp_ref,
            out_ref, d1_ref, do_ref, keep_ref, send_ref, gs_ref, go_ref, gi_ref, gb_ref,
            gbs, dus, dfs, hbs, das, osc, *placed) = refs[:ways], refs[ways:]
    w_ref = placed[0] if placed else parts[0]
    me = cnt_ref[cnt_ref.shape[0] - 1]
    pieces, small = 2 * keep_ref.shape[0], 2 * gs_ref.shape[0]
    n, rb = pl.program_id(0), pl.program_id(1)
    first = jnp.logical_and(n == 0, rb == 0)
    last = jnp.logical_and(n == pl.num_programs(0) - 1, rb == NRBL - 1)

    @pl.when(first)
    def _():
        go_ref[...] = jnp.zeros_like(go_ref)
        gi_ref[...] = jnp.zeros_like(gi_ref)
        gb_ref[...] = jnp.zeros_like(gb_ref)
        gs_ref[...] = jnp.zeros_like(gs_ref)
        if placed:
            put_in_order(me, parts, w_ref)

    per = w_ref.shape[1] // 5
    wo = w_ref[:, 0:per].reshape(D, D)
    wi = w_ref[:, per : 3 * per].reshape(FF, D)
    wb = w_ref[:, 3 * per :].reshape(FF, D)
    gain1, shift1 = sp_ref[0:1], sp_ref[1:2]
    bias2, gain2, shift2 = sp_ref[4:5], sp_ref[5:6], sp_ref[6:7]
    bias1 = jnp.concatenate([sp_ref[2:3], sp_ref[3:4]], axis=1)
    size = RBL // NSUB
    sums = []

    def chain(part):
        rs = slice(part * size, (part + 1) * size)
        here = pl.ds(pl.multiple_of(rb * RBL, RBL) + part * size, size)
        osc[here] = o_ref[0, rs]
        rows = rb * RBL + part * size + lax.broadcasted_iota(jnp.int32, (size, 1), 0)
        valid = rows < SLOTS
        live = rows < CTX + cnt_ref[n]
        at = nt(o_ref[0, rs], wo)
        yield
        r1 = jnp.where(valid, x_ref[0, rs].astype(f32), 0.0) + at
        c1 = r1 - lane_mean(r1)
        is1 = lax.rsqrt(lane_mean(c1 * c1) + eps_norm)
        xh1 = c1 * is1
        h = xh1 * gain1 + shift1
        hb = h.astype(bf16)
        hbs[here] = hb
        yield
        u = nt(hb, wi)
        yield
        u = u + bias1
        ex = jnp.exp2((-0.7213475204444817 * u) * u)
        t = 1.0 / (1.0 + 0.23164189 * jnp.abs(u))
        poly = t * (0.127414796 + t * (-0.142248368 + t * (0.7107068705 + t * (-0.7265760135 + t * 0.5307027145))))
        tail = poly * ex
        phi = jnp.where(u >= 0.0, 1.0 - tail, tail)
        gb = (u * phi).astype(bf16)
        gbs[here] = gb
        dgelu = phi + u * ex * 0.3989422804014327
        yield
        r2 = nn(gb, wb)
        yield
        r2 = h + r2 + bias2
        c2 = r2 - lane_mean(r2)
        is2 = lax.rsqrt(lane_mean(c2 * c2) + eps_norm)
        xh2 = c2 * is2
        out_ref[0, rs] = jnp.where(live, xh2 * gain2 + shift2, 0.0).astype(bf16)
        dy = jnp.where(live, c_ref[0, rs].astype(f32), 0.0)
        s5 = jnp.sum(dy * xh2, axis=0, keepdims=True)
        s6 = jnp.sum(dy, axis=0, keepdims=True)
        e2 = dy * gain2
        d2 = (e2 - lane_mean(e2) - xh2 * lane_mean(e2 * xh2)) * is2
        df = d2.astype(bf16)
        dfs[here] = df
        s4 = jnp.sum(df.astype(f32), axis=0, keepdims=True)
        yield
        dg = nt(df, wb)
        yield
        du = (dg * dgelu).astype(bf16)
        dus[here] = du
        s2 = jnp.sum(du.astype(f32), axis=0, keepdims=True)
        yield
        dh = nn(du, wi)
        yield
        dh = d2 + dh
        s0 = jnp.sum(dh * xh1, axis=0, keepdims=True)
        s1 = jnp.sum(dh, axis=0, keepdims=True)
        e1 = dh * gain1
        d1 = (e1 - lane_mean(e1) - xh1 * lane_mean(e1 * xh1)) * is1
        d1_ref[0, rs] = d1
        da = d1.astype(bf16)
        das[here] = da
        sums.append((s0, s1, s2[:, :D], s2[:, D:], s4, s5, s6))
        yield
        dm = nn(da, wo)
        yield
        for h in range(HEADS):
            hs = slice(h * HD, (h + 1) * HD)
            li = li_ref[0, rs, h * (HD // HEADS) : h * (HD // HEADS) + 1]
            do_ref[0, rs, hs] = (dm[:, hs] * li).astype(bf16)

    chains = [chain(i) for i in range(NSUB)]
    for i, c in enumerate(chains):
        for _ in range(len(chains) - 1 - i):
            next(c)
    done = 0
    while done < len(chains):
        done = 0
        for c in chains:
            try:
                next(c)
            except StopIteration:
                done += 1
    for i in range(7):
        total_i = sums[0][i]
        for s in sums[1:]:
            total_i = total_i + s[i]
        gs_ref[i : i + 1] += total_i

    @pl.when(rb == NRBL - 1)
    def _():
        for target, left, right in ((gi_ref, dus, hbs), (gb_ref, gbs, dfs), (go_ref, das, osc)):
            target[...] += tn(left[...], right[...])

    def write(core):
        for p in range(pieces):
            out = keep_ref if p % 2 == core else send_ref
            if p < 2:
                high = gs_ref[...].astype(bf16)
                out[0, : small // 2] = high
                out[0, small // 2 : small] = (gs_ref[...] - high.astype(f32)).astype(bf16)
            else:
                out[p // 2, :small] = jnp.zeros((small, D), bf16)
            at = small
            for target in (gi_ref, gb_ref, go_ref):
                size = target.shape[0] // pieces
                out[p // 2, at : at + size] = target[p * size : (p + 1) * size].astype(bf16)
                at += size

    for core in range(2):
        pl.when(jnp.logical_and(last, me % 2 == core))(functools.partial(write, core))


def rows_pass(counts, x, o, li, cot, rest, sp, pieces):
    n = x.shape[0]
    placed = []
    if len(rest) > 1:
        placed = [pltpu.VMEM((2 * rest[0].shape[0],) + rest[0].shape[1:], bf16)]
    cut = (pieces // 2, 16 + (D + 2 * FF) // pieces, D)
    sd = jax.ShapeDtypeStruct
    blk = pl.BlockSpec((1, RBL, D), lambda i, r, c: (i, r, 0))
    const = lambda *s: pl.BlockSpec(s, lambda i, r, c: (0,) * len(s))
    return pl.pallas_call(
        functools.partial(rows_body, len(rest)),
        grid_spec=pltpu.PrefetchScalarGridSpec(
            num_scalar_prefetch=1,
            grid=(n, NRBL),
            in_specs=[
                blk,
                blk,
                pl.BlockSpec((1, RBL, HD), lambda i, r, c: (i, r, 0)),
                blk,
            ]
            + [const(*w.shape) for w in rest]
            + [const(8, D)],
            out_specs=[blk, blk, blk, const(*cut), const(*cut)],
            scratch_shapes=[
                pltpu.VMEM((8, D), f32),
                pltpu.VMEM((D, D), f32),
                pltpu.VMEM((FF, D), f32),
                pltpu.VMEM((FF, D), f32),
                pltpu.VMEM((PAD, FF), bf16),
                pltpu.VMEM((PAD, FF), bf16),
                pltpu.VMEM((PAD, D), bf16),
                pltpu.VMEM((PAD, D), bf16),
                pltpu.VMEM((PAD, D), bf16),
                pltpu.VMEM((PAD, D), bf16),
            ]
            + placed,
        ),
        out_shape=[
            sd((n, SLOTS, D), bf16),
            sd((n, SLOTS, D), f32),
            sd((n, PAD, D), bf16),
            sd(cut, bf16),
            sd(cut, bf16),
        ],
        compiler_params=pltpu.CompilerParams(
            dimension_semantics=("arbitrary", "arbitrary"), vmem_limit_bytes=VLIM_ROWS
        ),
        cost_estimate=pl.CostEstimate(
            flops=n * 18_000_000_000 // 2, transcendentals=n * PAD * FF * 2, bytes_accessed=n * 15_000_000
        ),
        name="rows_forward_backward",
    )(counts, x, o, li, cot, *rest, sp)


def attn_bwd_body(cut, *refs):
    x_ref, q_ref, k_ref, v_ref, e_ref, o_ref, do_ref, acc_ref, w_ref, *refs = refs
    (me_ref, other_ref), refs = (refs[:2], refs[2:]) if cut else ((None, None), refs)
    gi_ref, *outs = refs[:-4]
    dkt_ref, dvt_ref, gw_ref, xs_ref = refs[-4:]
    n, rb = pl.program_id(0), pl.program_id(1)

    @pl.when(jnp.logical_and(n == 0, rb == 0))
    def _():
        gw_ref[...] = jnp.zeros_like(gw_ref)

    @pl.when(rb == 0)
    def _():
        dkt_ref[...] = jnp.zeros_like(dkt_ref)
        dvt_ref[...] = jnp.zeros_like(dvt_ref)

    rows = rb * RBL + lax.broadcasted_iota(jnp.int32, (RBL, 1), 0)
    x = jnp.where(rows < SLOTS, x_ref[0].astype(f32), 0.0).astype(bf16)
    here = pl.ds(pl.multiple_of(rb * RBL, RBL), RBL)
    xs_ref[here] = x
    dqs = []
    for h in range(2):
        hs = slice(h * HD, (h + 1) * HD)
        do = do_ref[0, :, hs]
        t = jnp.sum(do.astype(f32) * o_ref[0, :, hs].astype(f32), axis=-1, keepdims=True)
        dp = nt(do, v_ref[0, :, hs])
        e = e_ref[0, h]
        ds = (e.astype(f32) * (dp - t)).astype(bf16)
        dqs.append(nn(ds, k_ref[0, :, hs]).astype(bf16))
        dvt_ref[hs] += tn(do, e)
        dkt_ref[hs] += tn(q_ref[0, :, hs], ds)
    dq = jnp.concatenate(dqs, axis=1)
    wq, wk, wv = (w_ref[:, i].reshape(2 * HD, D) for i in range(3))
    gw_ref[0] += tn(dq, x) * scaling
    gi_ref[0, here] = acc_ref[0] + nn(dq, wq) * scaling

    @pl.when(rb == NRBL - 1)
    def _():
        dkt, dvt = dkt_ref[...].astype(bf16), dvt_ref[...].astype(bf16)
        xc = xs_ref[0:CTX]
        gw_ref[1] += nn(dkt, xc)
        gw_ref[2] += nn(dvt, xc)
        gi_ref[0, 0:CTX] += tn(dkt, wk) + tn(dvt, wv)

    last = jnp.logical_and(n == pl.num_programs(0) - 1, rb == NRBL - 1)
    if not cut:

        @pl.when(last)
        def _():
            outs[0][...] = gw_ref[...]

        return

    def write(core):
        pieces, size = 2 * outs[0].shape[0], outs[0].shape[2]
        for p in range(pieces):
            out = outs[0] if p % 2 == core else outs[1]
            half, row = divmod(p * size, 2 * HD)
            for i in range(3):
                out[p // 2, i] = (gw_ref if half else other_ref)[i, row : row + size].astype(bf16)

    for core in range(2):
        pl.when(jnp.logical_and(last, me_ref[0] % 2 == core))(functools.partial(write, core))


def attn_bwd(pair, x, q, k, v, e, o, do, acc, wqkv, cut=()):
    n = x.shape[0]
    sd = jax.ShapeDtypeStruct
    ways = wqkv.shape[0]
    if ways > 1:
        wspec = pl.BlockSpec((ways // 2,) + wqkv.shape[1:], lambda i, r: (pair, 0, 0, 0))
    else:
        wspec = pl.BlockSpec((1, 3, 2 * HD, D), lambda i, r: (0, 0, pair, 0))
    heads = pl.BlockSpec((1, RBL, 2 * HD), lambda i, r: (i, r, pair))
    context = pl.BlockSpec((1, CTX, 2 * HD), lambda i, r: (i, 0, pair))
    rows = pl.BlockSpec((1, RBL, D), lambda i, r: (i, r, 0))
    grads = lambda shape: pl.BlockSpec(shape, lambda i, r: (0,) * len(shape))
    outs = [sd((cut[2] // 2, 3, D // cut[2], D), bf16)] * 2 if cut else [sd((3, 2 * HD, D), f32)]
    return pl.pallas_call(
        functools.partial(attn_bwd_body, bool(cut)),
        grid=(n, NRBL),
        in_specs=[
            rows,
            heads,
            context,
            context,
            pl.BlockSpec((1, 2, RBL, CTX), lambda i, r: (i, pair, r, 0)),
            heads,
            heads,
            rows,
            wspec,
        ]
        + ([pl.BlockSpec(memory_space=pltpu.SMEM), grads((3, 2 * HD, D))] if cut else []),
        out_specs=[pl.BlockSpec((1, PAD, D), lambda i, r: (i, 0, 0))] + [grads(g.shape) for g in outs],
        out_shape=[sd((n, SLOTS, D), f32)] + outs,
        scratch_shapes=[
            pltpu.VMEM((2 * HD, CTX), f32),
            pltpu.VMEM((2 * HD, CTX), f32),
            pltpu.VMEM((3, 2 * HD, D), f32),
            pltpu.VMEM((PAD, D), bf16),
        ],
        input_output_aliases={7: 0},
        compiler_params=pltpu.CompilerParams(
            dimension_semantics=("arbitrary", "arbitrary"), vmem_limit_bytes=VLIM_BWD
        ),
        cost_estimate=pl.CostEstimate(
            flops=9_000_000_000, transcendentals=0, bytes_accessed=24_000_000
        ),
        name="attention_backward",
    )(x, q, k, v, e, o, do, acc, wqkv, *([cut[0].reshape(1), cut[1]] if cut else []))


def adam_direction(first_new, second_new):
    return (first_new * (1.0 / (1.0 - beta_one**STEP))) / (
        jnp.sqrt(second_new * (1.0 / (1.0 - beta_two**STEP))) + eps_adam
    )


def rotate(grad, rows_basis, cols_basis, first_old, second_old):
    r = nn(tn(rows_basis, grad).astype(bf16), cols_basis)
    first_new = beta_one * first_old.astype(f32) + (1.0 - beta_one) * r
    second_new = beta_two * second_old.astype(f32) + (1.0 - beta_two) * r * r
    step = adam_direction(first_new, second_new).astype(bf16)
    return r.astype(bf16), nn(rows_basis, nt(step, cols_basis).astype(bf16)).astype(bf16)


def rotate_body(g_ref, a_ref, b_ref, m_ref, r_ref, u_ref):
    r_ref[...], u_ref[...] = rotate(g_ref[...], a_ref[...], b_ref[...], m_ref[0], m_ref[1])


def rotated_step(grad, rows_basis, cols_basis, moments):
    rows = grad.shape[0]
    sd = jax.ShapeDtypeStruct
    return pl.pallas_call(
        rotate_body,
        out_shape=[sd((rows, D), bf16), sd((rows, D), bf16)],
        compiler_params=pltpu.CompilerParams(vmem_limit_bytes=VLIM_STEP),
        cost_estimate=pl.CostEstimate(
            flops=4 * rows * D * (rows + D), transcendentals=rows * D, bytes_accessed=2 * rows * (rows + 5 * D)
        ),
        name="rotated_step",
    )(grad, rows_basis, cols_basis, moments)


def rotate_parts_body(me_ref, *refs):
    grads, a_ref, b_ref, olds, outs = refs[:2], refs[2], refs[3], refs[4:6], refs[6:10]
    g_ref, m_ref, r_ref, u_ref = refs[10:]
    me = me_ref[0]
    planes, inner, rows = len(outs), g_ref.shape[0], r_ref.shape[0]
    per = rows // (planes * inner)
    put_in_order(me & (inner - 1), grads, g_ref)
    put_in_order(me, olds, m_ref)
    r_ref[...], u_ref[...] = rotate(
        g_ref[...].reshape(rows, D), a_ref[...], b_ref[...],
        m_ref[:, 0].reshape(rows, D), m_ref[:, 1].reshape(rows, D),
    )
    n = g_ref.shape[1]
    for rel, out in enumerate(outs):
        row = pl.multiple_of((me ^ (rel * inner)) * per, per)
        out[0] = g_ref[row // n, pl.ds(pl.multiple_of(row % n, per), per)]
        out[1] = r_ref[pl.ds(row, per)]
        out[2] = u_ref[pl.ds(row, per)]


def rotated_step_parts(me, grads, rows_basis, cols_basis, olds, block):
    rows = rows_basis.shape[0]
    inner = 2 * grads[0].shape[0]
    count = 2 * olds[0].shape[0]
    per = rows // count
    full = lambda shape: pl.BlockSpec(shape, lambda i: (0,) * len(shape))
    return pl.pallas_call(
        rotate_parts_body,
        grid=(1,),
        in_specs=[pl.BlockSpec(memory_space=pltpu.SMEM)]
        + [full(g.shape) for g in grads]
        + [full(rows_basis.shape), full(cols_basis.shape)]
        + [pl.BlockSpec((count // 2, 2, per, D), lambda i: (0, 0, block, 0))] * 2,
        out_specs=[full((3, per, D))] * (count // inner),
        out_shape=[jax.ShapeDtypeStruct((3, per, D), bf16)] * (count // inner),
        scratch_shapes=[
            pltpu.VMEM((inner, rows // inner, D), bf16),
            pltpu.VMEM((count, 2, per, D), bf16),
            pltpu.VMEM((rows, D), bf16),
            pltpu.VMEM((rows, D), bf16),
        ],
        compiler_params=pltpu.CompilerParams(vmem_limit_bytes=VLIM_STEP),
        cost_estimate=pl.CostEstimate(
            flops=4 * rows * D * (rows + D), transcendentals=rows * D, bytes_accessed=2 * rows * (rows + 5 * D)
        ),
        name="rotated_step",
    )(me.reshape(1), *grads, rows_basis, cols_basis, *(pltpu.with_memory_space_constraint(v, pltpu.HBM) for v in olds))


class Net:
    def __init__(self, mesh):
        self.count = mesh.size
        self.bits = self.count.bit_length() - 1
        self.inner_bits = self.bits - 2
        self.inner = 1 << self.inner_bits
        self.me = lax.axis_index(axes)
        self.local = self.me & (self.inner - 1)
        self.plane = self.me >> self.inner_bits
        stages = [(0, 1)]
        while stages[-1][0] + stages[-1][1] < self.inner_bits:
            low = stages[-1][0] + stages[-1][1]
            stages.append((low, min(2, self.inner_bits - low)))
        self.stages = stages
        self.top = (self.inner_bits, 2)

    def swap(self, value, offset, targets=(0, 1, 2, 3), sources=(0, 1, 2, 3)):
        pairs = [(i, i ^ offset) for i in range(self.count)]
        pairs = [
            (i, j) for i, j in pairs
            if (i >> self.inner_bits) in sources and (j >> self.inner_bits) in targets
        ]
        return lax.ppermute(value, axes, pairs)

    def digit(self, stage):
        return (self.me >> stage[0]) & ((1 << stage[1]) - 1)

    def collect(self, value, stage):
        return [value] + [self.swap(value, rel << stage[0]) for rel in range(1, 1 << stage[1])]

    def widen(self, value, stage):
        return interleave(self.collect(value, stage))

    def cut(self, pick, stage):
        mine = self.digit(stage)
        return [pick(mine ^ rel) for rel in range(1 << stage[1])]

    def trade(self, terms, stage, targets=(0, 1, 2, 3), sources=(0, 1, 2, 3)):
        return list(terms[:1]) + [
            self.swap(term, rel << stage[0], targets, sources) for rel, term in enumerate(terms) if rel
        ]


def after(value, *earlier):
    return lax.optimization_barrier((value, earlier))[0]


def interleave(parts):
    value = jnp.stack(parts, axis=1)
    return value.reshape((-1,) + value.shape[2:])


def total(parts):
    parts = [p.astype(f32) for p in parts]
    while len(parts) > 1:
        parts = [a + b for a, b in zip(parts[0::2], parts[1::2])]
    return parts[0]


def take_at(value, index, axis):
    return lax.dynamic_index_in_dim(value, index, axis, keepdims=False)


def join_high(pair):
    half = pair.shape[0] // 2
    return pair[:half].astype(f32) + pair[half:].astype(f32)


def sum_cut_body(low, bits, small, me_ref, *refs):
    size = 1 << bits
    parts, terms = refs[:-size], refs[-size:]
    digit = (me_ref[0] >> low) & (size - 1)
    if small:
        whole = total([join_high(p[0, :small]) for p in parts])
        high = whole.astype(bf16)
        pair = jnp.concatenate([high, (whole - high.astype(f32)).astype(bf16)])
    for rel, term in enumerate(terms):
        for j in range(term.shape[0]):
            piece = j * size + (digit ^ rel)
            if small:
                term[j, :small] = pair
                term[j, small:] = total([p[piece, small:] for p in parts]).astype(bf16)
            else:
                term[j] = total([p[piece] for p in parts]).astype(bf16)


def sum_top_body(low, small, me_ref, *refs):
    parts, terms = refs[:-4], refs[-4:]
    plane = (me_ref[0] >> low) & 3
    for rel, term in enumerate(terms):
        goal = plane ^ rel
        if not small:
            piece = jnp.minimum(goal, 2)
            term[...] = total([p[0, piece] for p in parts]).astype(bf16)
            continue
        rows = term.shape[0] - small
        whole = total([join_high(p[0, :small]) for p in parts])
        high = whole.astype(bf16)
        term[:small] = jnp.concatenate([high, (whole - high.astype(f32)).astype(bf16)])

        def give(k):
            count = min(rows, parts[0].shape[1] - small - k * rows)
            begin = small + k * rows
            term[small : small + count] = total([p[0, begin : begin + count] for p in parts]).astype(bf16)
            if count < rows:
                term[small + count :] = jnp.zeros((rows - count, D), bf16)

        for k in range(3):
            pl.when(jnp.maximum(goal, 1) == k + 1)(functools.partial(give, k))


def deal(body, me, parts, term, count):
    full = lambda dims: pl.BlockSpec(dims, lambda i: (0,) * len(dims))
    return pl.pallas_call(
        body,
        grid=(1,),
        in_specs=[pl.BlockSpec(memory_space=pltpu.SMEM)] + [full(p.shape) for p in parts],
        out_specs=[full(term)] * count,
        out_shape=[pltpu.HBM(term, bf16)] * count,
        compiler_params=pltpu.CompilerParams(vmem_limit_bytes=VLIM_STEP),
        cost_estimate=pl.CostEstimate(
            flops=0, transcendentals=0, bytes_accessed=4 * len(parts) * parts[0].size
        ),
        name="sum_and_deal",
    )(me.reshape(1), *parts)


def sum_cut(net, parts, stage, small=0):
    size = 1 << stage[1]
    shape = parts[0].shape
    body = functools.partial(sum_cut_body, *stage, small)
    return deal(body, net.me, parts, (shape[0] // size,) + shape[1:], size)


def sum_top(net, parts, rows, small=0):
    body = functools.partial(sum_top_body, net.top[0], small)
    return deal(body, net.me, parts, (small + rows, D), 4)


def place_body(me_ref, *refs):
    *parts, out = refs
    put_in_order(me_ref[0] & (out.shape[0] - 1), parts, out)


def place(me, parts):
    size = len(parts) * parts[0].shape[0]
    shape = jax.ShapeDtypeStruct((size,) + parts[0].shape[1:], parts[0].dtype)
    return pl.pallas_call(
        place_body,
        in_specs=[pl.BlockSpec(memory_space=pltpu.SMEM)]
        + [pl.BlockSpec(memory_space=pltpu.VMEM)] * len(parts),
        out_specs=pl.BlockSpec(memory_space=pltpu.VMEM),
        out_shape=shape,
        compiler_params=pltpu.CompilerParams(vmem_limit_bytes=24 * 1024 * 1024),
        cost_estimate=pl.CostEstimate(flops=0, transcendentals=0, bytes_accessed=4 * shape.size),
        name="place",
    )(me.reshape(1), *parts)


def finish_body(low, me_ref, *refs):
    attn, ffn = refs[:4], refs[4:8]
    moments_ref, weights_ref, grad_ref, new_ref, out_ref = refs[8:]
    plane = (me_ref[0] >> low) & 3
    per = attn[0].shape[1]
    rows = 8 * per

    def choose(parts, plain, kind):
        value = parts[0][kind].astype(f32)
        for rel in range(1, 4):
            value = jnp.where(plane == (plain ^ rel), parts[rel][kind].astype(f32), value)
        return value.astype(bf16)

    row = lax.broadcasted_iota(jnp.int32, (rows, rows), 0)
    source = lax.broadcasted_iota(jnp.int32, (rows, rows), 1)
    group, slot = row // 8, row % 8
    wanted = jnp.where(
        slot < 4, slot * per + group, (4 + 2 * ((slot - 4) // 2)) * per + 2 * group + slot % 2
    )
    order = jnp.where(source == wanted, 1.0, 0.0).astype(bf16)

    def plain(kind):
        parts = [choose(attn, b, kind) for b in range(4)] + [choose(ffn, f, kind) for f in (1, 2)]
        return nn(order, jnp.concatenate(parts))

    grad_ref[...] = plain(0)
    turned = plain(1)
    new_ref[0] = beta_one * moments_ref[0] + (1.0 - beta_one) * turned
    new_ref[1] = beta_two * moments_ref[1] + (1.0 - beta_two) * turned * turned
    out_ref[...] = weights_ref[...] - rate_mats * plain(2)


def finish(net, attn, ffn, moments, weights):
    full = lambda shape: pl.BlockSpec(shape, lambda i: (0,) * len(shape))
    arrays = [*attn, *ffn, moments, weights]
    outs = [weights, moments, weights]
    return pl.pallas_call(
        functools.partial(finish_body, net.top[0]),
        grid=(1,),
        in_specs=[pl.BlockSpec(memory_space=pltpu.SMEM)] + [full(v.shape) for v in arrays],
        out_specs=[full(v.shape) for v in outs],
        out_shape=[jax.ShapeDtypeStruct(v.shape, f32) for v in outs],
        compiler_params=pltpu.CompilerParams(vmem_limit_bytes=VLIM_STEP),
        cost_estimate=pl.CostEstimate(flops=50_000_000, transcendentals=0, bytes_accessed=3_000_000),
        name="finish",
    )(net.me.reshape(1), *arrays)


def by_index(parts, index):
    return [
        functools.reduce(
            lambda rest, r: jnp.where(index == (b ^ r), parts[r], rest), range(1, len(parts)), parts[0]
        )
        for b in range(len(parts))
    ]


def on_device(mesh, features, cotangent, counts, weights, small_params, moments_old, small_moments,
              basis_attn, basis_ffn, basis_cols):
    net = Net(mesh)
    per = weights.shape[0] // 8
    everyone = net.stages + [net.top]

    def by_matrix(stacked):
        groups = stacked.reshape(per, 8, D)
        return (
            jnp.transpose(groups[:, 0:4], (1, 0, 2)),
            groups[:, 4:6].reshape(2 * per, D),
            groups[:, 6:8].reshape(2 * per, D),
        )

    def stacked(attn, inner, outer):
        return jnp.concatenate(
            [jnp.stack(attn, axis=1), inner.reshape(per, 2, D), outer.reshape(per, 2, D)], axis=1
        ).reshape(8 * per, D)

    inner = net.inner
    n_attn, n_ffn = D // inner, FF // inner
    ffn_of = lambda plane: jnp.clip(plane - 1, 0, 1)
    stages, top = net.stages, net.top

    own_attn, own_in, own_out = by_matrix(weights.astype(bf16))
    first = own_attn[None, 0:3]
    rest = jnp.concatenate([own_attn[3], own_in, own_out])[None]
    olds = [by_matrix(moments_old[i].astype(bf16)) for i in range(2)]
    old_attn = jnp.stack([m[0] for m in olds], axis=1)
    old_ffn = jnp.stack([jnp.stack([m[1], m[2]]) for m in olds], axis=1)
    old_terms = net.cut(
        lambda d: jnp.concatenate([take_at(old_ffn, ffn_of(d), 0), take_at(old_attn, d, 0)], axis=1), top
    )
    mine = ffn_of(net.plane)
    sp = jnp.concatenate([small_params.reshape(7, D), jnp.zeros((1, D), f32)])
    counts_me = jnp.concatenate([counts, net.me.reshape(1)])

    whole_tiles = per % 16 == 0
    order = list(reversed(everyone))
    first = interleave(net.collect(first, order[0]))
    rest_parts = net.collect(after(rest, first), order[0])
    for i, stage in enumerate(order[1:]):
        first_parts = net.collect(first, stage)
        if stage is not order[-1]:
            first = interleave(first_parts)
            rest_parts, first, old_terms, sp, counts_me = after(
                (rest_parts, first, old_terms, sp, counts_me), first_parts
            )
            rest = interleave(rest_parts)
            rest_parts = net.collect(rest, stage)
    if not whole_tiles:
        first_parts = [jnp.transpose(place(net.me, first_parts), (1, 0, 2, 3)).reshape(1, 3, D, D)]
    first_parts, sp, counts_me = lax.optimization_barrier((first_parts, sp, counts_me, rest, old_terms))[:3]
    old_parts = net.trade(after(old_terms, rest), top)
    q, k, v, e, o, li, wqkv = attn_fwd(features, first_parts, net.me)
    rest_parts, old_parts = after((rest_parts, old_parts), o)
    rest, olds = interleave(rest_parts), jnp.stack(old_parts)
    for stage in reversed(stages[2:]):
        olds = net.widen(olds, stage)
    rest_parts = net.collect(after(rest, olds), order[-1])
    old_parts = net.collect(olds, stages[1])
    if not whole_tiles:
        rest = place(net.me, rest_parts)
        rest_parts = [
            jnp.concatenate(
                [rest[:, lo * per : hi * per].reshape(-1, D) for lo, hi in ((0, 1), (1, 3), (3, 5))]
            )[None]
        ]
    output, d1, do, *terms = rows_pass(
        counts_me, features, o, li, cotangent, after(rest_parts, olds), sp, inner
    )

    n_small = 16
    terms, old_parts = after((terms, old_parts), output)
    early_parts = net.trade(terms, stages[0])
    olds = interleave(old_parts)
    early_parts = after(early_parts, olds)
    for stage in stages[2:]:
        early_parts = net.trade(sum_cut(net, early_parts, stage, n_small), stage)
    terms = sum_cut(net, early_parts, stages[1], n_small)
    early_parts = net.trade(terms, stages[1])
    old_parts = net.collect(olds, stages[0])
    back = functools.partial(attn_bwd, x=features, q=q, k=k, v=v, e=e, o=o, do=do)
    acc, gw0 = back(0, acc=d1, wqkv=after(wqkv, terms, olds))
    early_parts, old_parts = after((early_parts, old_parts), gw0)
    top_terms = sum_top(net, early_parts, n_ffn, n_small)
    top_parts = net.trade(top_terms, top)
    grad_input, *terms = back(1, acc=acc, wqkv=after(wqkv, top_terms, old_parts), cut=(net.me, gw0, inner))

    terms, top_parts = lax.optimization_barrier((terms, top_parts))
    late_parts = net.trade(terms, stages[0])
    ffn = total([p[n_small:] for p in top_parts]).astype(bf16)
    ffn_parts = net.collect(ffn[None], stages[-1])
    late_parts = after(late_parts, ffn)
    for stage in stages[2:]:
        late_parts = net.trade(sum_cut(net, late_parts, stage), stage)
    terms = sum_cut(net, late_parts, stages[1])
    late_parts = net.trade(terms, stages[1])
    a_ffn, b_ffn = after((basis_ffn, basis_cols), terms)
    a_ffn, b_ffn = take_at(a_ffn, mine, 0).astype(bf16), take_at(b_ffn, 4 + mine, 0).astype(bf16)
    early_part, ffn_parts, a_ffn, b_ffn = lax.optimization_barrier((late_parts[1], ffn_parts, a_ffn, b_ffn))
    wide = interleave(ffn_parts)
    late_parts, wide = lax.optimization_barrier((late_parts[:1] + [early_part] + late_parts[2:], wide))
    terms = sum_top(net, late_parts, n_attn)
    late_parts = net.trade(terms, top)
    wide = after(wide, terms)
    ffn_parts = net.collect(wide, stages[len(stages) - 2])
    for stage in reversed(stages[:-2]):
        ffn_parts = net.collect(interleave(ffn_parts), stage)

    if whole_tiles:
        back_ffn = rotated_step_parts(net.me, ffn_parts, a_ffn, b_ffn, old_parts, 0)
    else:
        olds = jnp.transpose(place(net.me, old_parts), (1, 0, 2, 3))
        full = place(net.me, ffn_parts).reshape(FF, D)
        both = rotated_step(full, a_ffn, b_ffn, olds[:, :, : 2 * per].reshape(2, FF, D))
        back_ffn = take_at(jnp.stack([full, *both]).reshape(3, 4, inner, 2 * per, D), net.local, 2)
        back_ffn = net.cut(lambda d: take_at(back_ffn, d, 1), top)
    late_parts = after(late_parts, back_ffn)
    attn = total(late_parts).astype(bf16)
    attn = jnp.where(net.plane == 3, ffn[:n_attn], attn)[None]
    gs = total([join_high(p[:n_small]) for p in after(top_parts, attn)])
    a_attn, b_attn = after((basis_attn, basis_cols), attn)
    a_attn, b_attn = (take_at(basis, net.plane, 0).astype(bf16) for basis in (a_attn, b_attn))
    for stage in reversed(stages[1:]):
        attn_parts = net.collect(attn, stage)
        attn_parts, gs, a_attn, b_attn = lax.optimization_barrier((attn_parts, gs, a_attn, b_attn))
        attn = interleave(attn_parts)
    attn_parts = net.collect(attn, stages[0])
    back_ffn = net.trade(back_ffn, top)
    if whole_tiles:
        back_attn = rotated_step_parts(net.me, attn_parts, a_attn, b_attn, old_parts, 2)
    else:
        full = place(net.me, attn_parts).reshape(D, D)
        both = rotated_step(full, a_attn, b_attn, olds[:, :, 2 * per :].reshape(2, D, D))
        back_attn = take_at(jnp.stack([full, *both]).reshape(3, 4, inner, per, D), net.local, 2)
        back_attn = net.cut(lambda d: take_at(back_attn, d, 1), top)
    back_ffn, gs = after((back_ffn, gs), back_attn)
    back_attn = net.trade(back_attn, top)
    grad_small = gs[0:7].reshape(-1)
    small_first = beta_one * small_moments[0] + (1.0 - beta_one) * grad_small
    small_second = beta_two * small_moments[1] + (1.0 - beta_two) * grad_small * grad_small
    small_new = small_params - rate_small * adam_direction(small_first, small_second)
    small_moments_new = jnp.stack([small_first, small_second])
    back_attn, small_new, small_moments_new = lax.optimization_barrier(
        (back_attn, small_new, small_moments_new)
    )
    if whole_tiles:
        grad_weights, moments_new, weights_new = finish(net, back_attn, back_ffn, moments_old, weights)
    else:
        back_attn = by_index(back_attn, net.plane)
        back_ffn = by_index(back_ffn, net.plane)
        grad_weights, rotated, update = (
            stacked([part[i] for part in back_attn], back_ffn[1][i], back_ffn[2][i]).astype(f32) for i in range(3)
        )
        moments_new = jnp.stack(
            [
                beta_one * moments_old[0] + (1.0 - beta_one) * rotated,
                beta_two * moments_old[1] + (1.0 - beta_two) * rotated * rotated,
            ]
        )
        weights_new = weights - rate_mats * update
    return (
        output,
        grad_input,
        grad_weights,
        moments_new,
        weights_new,
        grad_small,
        small_moments_new,
        small_new,
    )


def solution(mesh):
    rows = P(("dp", "fsdp"), None)
    blocks = P(("dp", "fsdp"), None, None)
    pair = P(None, ("dp", "fsdp"), None)
    return jax.shard_map(
        lambda *arrays: on_device(mesh, *arrays),
        mesh=mesh,
        in_specs=(blocks, blocks, P(("dp", "fsdp")), rows, P(), pair, P(), P(), P(), P()),
        out_specs=(blocks, blocks, rows, pair, rows, P(), P(), P()),
        check_vma=False,
    )
```

```python
import functools
import jax
import jax.numpy as jnp
from jax import lax
from jax.sharding import PartitionSpec as P
from jax.experimental import pallas as pl
from jax.experimental.pallas import tpu as pltpu

D = 512
HEADS = 4
FF = 1024
HD = 128
CTX = 1024
SLOTS = 1128
STEP = 10
PAD = 1152
RB = 576
NRB = PAD // RB
RBL = 576
SUB = 144
NRBL = PAD // RBL
scaling = HD ** (-0.5)
eps_norm = 1e-05
eps_adam = 1e-08
beta_one = 0.9
beta_two = 0.999
rate_mats = 0.1
rate_small = 0.5
axes = ("dp", "fsdp")
bf16 = jnp.bfloat16
f32 = jnp.float32
VLIM_FWD = 52 * 1024 * 1024
VLIM_ROWS = 46 * 1024 * 1024
VLIM_BWD = 46 * 1024 * 1024
VLIM_STEP = 20 * 1024 * 1024


def nt(a, b):
    return lax.dot_general(a, b, (((1,), (1,)), ((), ())), preferred_element_type=f32)


def nn(a, b):
    return lax.dot_general(a, b, (((1,), (0,)), ((), ())), preferred_element_type=f32)


def tn(a, b):
    return lax.dot_general(a, b, (((0,), (0,)), ((), ())), preferred_element_type=f32)


def put_in_order(me, parts, out):
    def move(j, carry):
        for c, part in enumerate(parts):
            out[(j * len(parts) + c) ^ me] = part[j]
        return carry

    lax.fori_loop(0, parts[0].shape[0], move, 0)


def attn_fwd_body(ways, *refs):
    me_ref, xc_ref, xr_ref, *refs = refs
    parts, (q_ref, k_ref, v_ref, e_ref, o_ref, li_ref, w_ref, ve_ref) = refs[:ways], refs[ways:]
    n, rb = pl.program_id(0), pl.program_id(1)

    @pl.when(jnp.logical_and(n == 0, rb == 0))
    def _():
        put_in_order(me_ref[0] & (w_ref.shape[0] - 1), parts, w_ref)

    @pl.when(rb == 0)
    def _():
        xc = xc_ref[0]
        k_ref[0] = nt(xc, w_ref[:, 1].reshape(D, D)).astype(bf16)
        v_ref[0] = nt(xc, w_ref[:, 2].reshape(D, D)).astype(bf16)
        for h in range(HEADS):
            ve_ref[h, :, 0:HD] = v_ref[0, :, h * HD : (h + 1) * HD]
            ve_ref[h, :, HD : 2 * HD] = jnp.ones((CTX, HD), bf16)

    rows = rb * RB + lax.broadcasted_iota(jnp.int32, (RB, 1), 0)
    xr = jnp.where(rows < SLOTS, xr_ref[0].astype(f32), 0.0).astype(bf16)
    q_ref[0] = (nt(xr, w_ref[:, 0].reshape(D, D)) * scaling).astype(bf16)
    lane = lax.broadcasted_iota(jnp.int32, (SUB, HD), 1) // (HD // HEADS)
    for r in range(0, RB, SUB):
        rs = slice(r, r + SUB)
        for h in range(HEADS):
            hs = slice(h * HD, (h + 1) * HD)
            s = nt(q_ref[0, rs, hs], k_ref[0, :, hs])
            m = jnp.max(s, axis=-1, keepdims=True)
            e = jnp.exp(s - m).astype(bf16)
            e_ref[0, h, rs] = e
            ov = nn(e, ve_ref[h])
            li = 1.0 / ov[:, HD:]
            scales = li if h == 0 else jnp.where(lane == h, li, scales)
            o_ref[0, rs, hs] = (ov[:, :HD] * li).astype(bf16)
        li_ref[0, rs] = scales


def attn_fwd(x, parts, me):
    n = x.shape[0]
    sd = jax.ShapeDtypeStruct
    everything = lambda shape: pl.BlockSpec(shape, lambda i, r: (0,) * len(shape))
    wshape = (len(parts) * parts[0].shape[0],) + parts[0].shape[1:]
    block = lambda w: pl.BlockSpec((1, RB, w), lambda i, r: (i, r, 0))
    context = pl.BlockSpec((1, CTX, D), lambda i, r: (i, 0, 0))
    return pl.pallas_call(
        functools.partial(attn_fwd_body, len(parts)),
        grid=(n, NRB),
        in_specs=[pl.BlockSpec(memory_space=pltpu.SMEM), context, block(D)]
        + [everything(w.shape) for w in parts],
        out_specs=[
            block(D),
            context,
            context,
            pl.BlockSpec((1, HEADS, RB, CTX), lambda i, r: (i, 0, r, 0)),
            block(D),
            block(HD),
            everything(wshape),
        ],
        out_shape=[
            sd((n, PAD, D), bf16),
            sd((n, CTX, D), bf16),
            sd((n, CTX, D), bf16),
            sd((n, HEADS, PAD, CTX), bf16),
            sd((n, PAD, D), bf16),
            sd((n, PAD, HD), f32),
            sd(wshape, bf16),
        ],
        scratch_shapes=[pltpu.VMEM((HEADS, CTX, 2 * HD), bf16)],
        compiler_params=pltpu.CompilerParams(
            dimension_semantics=("arbitrary", "arbitrary"), vmem_limit_bytes=VLIM_FWD
        ),
        cost_estimate=pl.CostEstimate(
            flops=14_000_000_000, transcendentals=n * HEADS * PAD * CTX, bytes_accessed=40_000_000
        ),
        name="attention_forward",
    )(me.reshape(1), x, x, *parts)


def lane_mean(v):
    return jnp.sum(v, axis=-1, keepdims=True) * (1.0 / D)


NSUB = 1


def rows_body(ways, cnt_ref, x_ref, o_ref, li_ref, c_ref, *refs):
    parts, (sp_ref,
            out_ref, d1_ref, do_ref, keep_ref, send_ref, gs_ref, go_ref, gi_ref, gb_ref,
            gbs, dus, dfs, hbs, das, osc, *placed) = refs[:ways], refs[ways:]
    w_ref = placed[0] if placed else parts[0]
    me = cnt_ref[cnt_ref.shape[0] - 1]
    pieces, small = 2 * keep_ref.shape[0], 2 * gs_ref.shape[0]
    n, rb = pl.program_id(0), pl.program_id(1)
    first = jnp.logical_and(n == 0, rb == 0)
    last = jnp.logical_and(n == pl.num_programs(0) - 1, rb == NRBL - 1)

    @pl.when(first)
    def _():
        go_ref[...] = jnp.zeros_like(go_ref)
        gi_ref[...] = jnp.zeros_like(gi_ref)
        gb_ref[...] = jnp.zeros_like(gb_ref)
        gs_ref[...] = jnp.zeros_like(gs_ref)
        if placed:
            put_in_order(me, parts, w_ref)

    per = w_ref.shape[1] // 5
    wo = w_ref[:, 0:per].reshape(D, D)
    wi = w_ref[:, per : 3 * per].reshape(FF, D)
    wb = w_ref[:, 3 * per :].reshape(FF, D)
    gain1, shift1 = sp_ref[0:1], sp_ref[1:2]
    bias2, gain2, shift2 = sp_ref[4:5], sp_ref[5:6], sp_ref[6:7]
    bias1 = jnp.concatenate([sp_ref[2:3], sp_ref[3:4]], axis=1)
    size = RBL // NSUB
    sums = []

    def chain(part):
        rs = slice(part * size, (part + 1) * size)
        here = pl.ds(pl.multiple_of(rb * RBL, RBL) + part * size, size)
        osc[here] = o_ref[0, rs]
        rows = rb * RBL + part * size + lax.broadcasted_iota(jnp.int32, (size, 1), 0)
        valid = rows < SLOTS
        live = rows < CTX + cnt_ref[n]
        at = nt(o_ref[0, rs], wo)
        yield
        r1 = jnp.where(valid, x_ref[0, rs].astype(f32), 0.0) + at
        c1 = r1 - lane_mean(r1)
        is1 = lax.rsqrt(lane_mean(c1 * c1) + eps_norm)
        xh1 = c1 * is1
        h = xh1 * gain1 + shift1
        hb = h.astype(bf16)
        hbs[here] = hb
        yield
        u = nt(hb, wi)
        yield
        u = u + bias1
        ex = jnp.exp2((-0.7213475204444817 * u) * u)
        t = 1.0 / (1.0 + 0.23164189 * jnp.abs(u))
        poly = t * (0.127414796 + t * (-0.142248368 + t * (0.7107068705 + t * (-0.7265760135 + t * 0.5307027145))))
        tail = poly * ex
        phi = jnp.where(u >= 0.0, 1.0 - tail, tail)
        gb = (u * phi).astype(bf16)
        gbs[here] = gb
        dgelu = phi + u * ex * 0.3989422804014327
        yield
        r2 = nn(gb, wb)
        yield
        r2 = h + r2 + bias2
        c2 = r2 - lane_mean(r2)
        is2 = lax.rsqrt(lane_mean(c2 * c2) + eps_norm)
        xh2 = c2 * is2
        out_ref[0, rs] = jnp.where(live, xh2 * gain2 + shift2, 0.0).astype(bf16)
        dy = jnp.where(live, c_ref[0, rs].astype(f32), 0.0)
        s5 = jnp.sum(dy * xh2, axis=0, keepdims=True)
        s6 = jnp.sum(dy, axis=0, keepdims=True)
        e2 = dy * gain2
        d2 = (e2 - lane_mean(e2) - xh2 * lane_mean(e2 * xh2)) * is2
        df = d2.astype(bf16)
        dfs[here] = df
        s4 = jnp.sum(df.astype(f32), axis=0, keepdims=True)
        yield
        dg = nt(df, wb)
        yield
        du = (dg * dgelu).astype(bf16)
        dus[here] = du
        s2 = jnp.sum(du.astype(f32), axis=0, keepdims=True)
        yield
        dh = nn(du, wi)
        yield
        dh = d2 + dh
        s0 = jnp.sum(dh * xh1, axis=0, keepdims=True)
        s1 = jnp.sum(dh, axis=0, keepdims=True)
        e1 = dh * gain1
        d1 = (e1 - lane_mean(e1) - xh1 * lane_mean(e1 * xh1)) * is1
        d1_ref[0, rs] = d1
        da = d1.astype(bf16)
        das[here] = da
        sums.append((s0, s1, s2[:, :D], s2[:, D:], s4, s5, s6))
        yield
        dm = nn(da, wo)
        yield
        for h in range(HEADS):
            hs = slice(h * HD, (h + 1) * HD)
            li = li_ref[0, rs, h * (HD // HEADS) : h * (HD // HEADS) + 1]
            do_ref[0, rs, hs] = (dm[:, hs] * li).astype(bf16)

    chains = [chain(i) for i in range(NSUB)]
    for i, c in enumerate(chains):
        for _ in range(len(chains) - 1 - i):
            next(c)
    done = 0
    while done < len(chains):
        done = 0
        for c in chains:
            try:
                next(c)
            except StopIteration:
                done += 1
    for i in range(7):
        total_i = sums[0][i]
        for s in sums[1:]:
            total_i = total_i + s[i]
        gs_ref[i : i + 1] += total_i

    @pl.when(rb == NRBL - 1)
    def _():
        for target, left, right in ((gi_ref, dus, hbs), (gb_ref, gbs, dfs), (go_ref, das, osc)):
            target[...] += tn(left[...], right[...])

    def write(core):
        for p in range(pieces):
            out = keep_ref if p % 2 == core else send_ref
            if p < 2:
                high = gs_ref[...].astype(bf16)
                out[0, : small // 2] = high
                out[0, small // 2 : small] = (gs_ref[...] - high.astype(f32)).astype(bf16)
            else:
                out[p // 2, :small] = jnp.zeros((small, D), bf16)
            at = small
            for target in (gi_ref, gb_ref, go_ref):
                size = target.shape[0] // pieces
                out[p // 2, at : at + size] = target[p * size : (p + 1) * size].astype(bf16)
                at += size

    for core in range(2):
        pl.when(jnp.logical_and(last, me % 2 == core))(functools.partial(write, core))


def rows_pass(counts, x, o, li, cot, rest, sp, pieces):
    n = x.shape[0]
    placed = []
    if len(rest) > 1:
        placed = [pltpu.VMEM((2 * rest[0].shape[0],) + rest[0].shape[1:], bf16)]
    cut = (pieces // 2, 16 + (D + 2 * FF) // pieces, D)
    sd = jax.ShapeDtypeStruct
    blk = pl.BlockSpec((1, RBL, D), lambda i, r, c: (i, r, 0))
    const = lambda *s: pl.BlockSpec(s, lambda i, r, c: (0,) * len(s))
    return pl.pallas_call(
        functools.partial(rows_body, len(rest)),
        grid_spec=pltpu.PrefetchScalarGridSpec(
            num_scalar_prefetch=1,
            grid=(n, NRBL),
            in_specs=[
                blk,
                blk,
                pl.BlockSpec((1, RBL, HD), lambda i, r, c: (i, r, 0)),
                blk,
            ]
            + [const(*w.shape) for w in rest]
            + [const(8, D)],
            out_specs=[blk, blk, blk, const(*cut), const(*cut)],
            scratch_shapes=[
                pltpu.VMEM((8, D), f32),
                pltpu.VMEM((D, D), f32),
                pltpu.VMEM((FF, D), f32),
                pltpu.VMEM((FF, D), f32),
                pltpu.VMEM((PAD, FF), bf16),
                pltpu.VMEM((PAD, FF), bf16),
                pltpu.VMEM((PAD, D), bf16),
                pltpu.VMEM((PAD, D), bf16),
                pltpu.VMEM((PAD, D), bf16),
                pltpu.VMEM((PAD, D), bf16),
            ]
            + placed,
        ),
        out_shape=[
            sd((n, SLOTS, D), bf16),
            sd((n, SLOTS, D), f32),
            sd((n, PAD, D), bf16),
            sd(cut, bf16),
            sd(cut, bf16),
        ],
        compiler_params=pltpu.CompilerParams(
            dimension_semantics=("arbitrary", "arbitrary"), vmem_limit_bytes=VLIM_ROWS
        ),
        cost_estimate=pl.CostEstimate(
            flops=n * 18_000_000_000 // 2, transcendentals=n * PAD * FF * 2, bytes_accessed=n * 15_000_000
        ),
        name="rows_forward_backward",
    )(counts, x, o, li, cot, *rest, sp)


def attn_bwd_body(cut, *refs):
    x_ref, q_ref, k_ref, v_ref, e_ref, o_ref, do_ref, acc_ref, w_ref, *refs = refs
    (me_ref, other_ref), refs = (refs[:2], refs[2:]) if cut else ((None, None), refs)
    gi_ref, *outs = refs[:-4]
    dkt_ref, dvt_ref, gw_ref, xs_ref = refs[-4:]
    n, rb = pl.program_id(0), pl.program_id(1)

    @pl.when(jnp.logical_and(n == 0, rb == 0))
    def _():
        gw_ref[...] = jnp.zeros_like(gw_ref)

    @pl.when(rb == 0)
    def _():
        dkt_ref[...] = jnp.zeros_like(dkt_ref)
        dvt_ref[...] = jnp.zeros_like(dvt_ref)

    rows = rb * RBL + lax.broadcasted_iota(jnp.int32, (RBL, 1), 0)
    x = jnp.where(rows < SLOTS, x_ref[0].astype(f32), 0.0).astype(bf16)
    here = pl.ds(pl.multiple_of(rb * RBL, RBL), RBL)
    xs_ref[here] = x
    dqs = []
    for h in range(2):
        hs = slice(h * HD, (h + 1) * HD)
        do = do_ref[0, :, hs]
        t = jnp.sum(do.astype(f32) * o_ref[0, :, hs].astype(f32), axis=-1, keepdims=True)
        dp = nt(do, v_ref[0, :, hs])
        e = e_ref[0, h]
        ds = (e.astype(f32) * (dp - t)).astype(bf16)
        dqs.append(nn(ds, k_ref[0, :, hs]).astype(bf16))
        dvt_ref[hs] += tn(do, e)
        dkt_ref[hs] += tn(q_ref[0, :, hs], ds)
    dq = jnp.concatenate(dqs, axis=1)
    wq, wk, wv = (w_ref[:, i].reshape(2 * HD, D) for i in range(3))
    gw_ref[0] += tn(dq, x) * scaling
    gi_ref[0, here] = acc_ref[0] + nn(dq, wq) * scaling

    @pl.when(rb == NRBL - 1)
    def _():
        dkt, dvt = dkt_ref[...].astype(bf16), dvt_ref[...].astype(bf16)
        xc = xs_ref[0:CTX]
        gw_ref[1] += nn(dkt, xc)
        gw_ref[2] += nn(dvt, xc)
        gi_ref[0, 0:CTX] += tn(dkt, wk) + tn(dvt, wv)

    last = jnp.logical_and(n == pl.num_programs(0) - 1, rb == NRBL - 1)
    if not cut:

        @pl.when(last)
        def _():
            outs[0][...] = gw_ref[...]

        return

    def write(core):
        pieces, size = 2 * outs[0].shape[0], outs[0].shape[2]
        for p in range(pieces):
            out = outs[0] if p % 2 == core else outs[1]
            half, row = divmod(p * size, 2 * HD)
            for i in range(3):
                out[p // 2, i] = (gw_ref if half else other_ref)[i, row : row + size].astype(bf16)

    for core in range(2):
        pl.when(jnp.logical_and(last, me_ref[0] % 2 == core))(functools.partial(write, core))


def attn_bwd(pair, x, q, k, v, e, o, do, acc, wqkv, cut=()):
    n = x.shape[0]
    sd = jax.ShapeDtypeStruct
    ways = wqkv.shape[0]
    if ways > 1:
        wspec = pl.BlockSpec((ways // 2,) + wqkv.shape[1:], lambda i, r: (pair, 0, 0, 0))
    else:
        wspec = pl.BlockSpec((1, 3, 2 * HD, D), lambda i, r: (0, 0, pair, 0))
    heads = pl.BlockSpec((1, RBL, 2 * HD), lambda i, r: (i, r, pair))
    context = pl.BlockSpec((1, CTX, 2 * HD), lambda i, r: (i, 0, pair))
    rows = pl.BlockSpec((1, RBL, D), lambda i, r: (i, r, 0))
    grads = lambda shape: pl.BlockSpec(shape, lambda i, r: (0,) * len(shape))
    outs = [sd((cut[2] // 2, 3, D // cut[2], D), bf16)] * 2 if cut else [sd((3, 2 * HD, D), f32)]
    return pl.pallas_call(
        functools.partial(attn_bwd_body, bool(cut)),
        grid=(n, NRBL),
        in_specs=[
            rows,
            heads,
            context,
            context,
            pl.BlockSpec((1, 2, RBL, CTX), lambda i, r: (i, pair, r, 0)),
            heads,
            heads,
            rows,
            wspec,
        ]
        + ([pl.BlockSpec(memory_space=pltpu.SMEM), grads((3, 2 * HD, D))] if cut else []),
        out_specs=[pl.BlockSpec((1, PAD, D), lambda i, r: (i, 0, 0))] + [grads(g.shape) for g in outs],
        out_shape=[sd((n, SLOTS, D), f32)] + outs,
        scratch_shapes=[
            pltpu.VMEM((2 * HD, CTX), f32),
            pltpu.VMEM((2 * HD, CTX), f32),
            pltpu.VMEM((3, 2 * HD, D), f32),
            pltpu.VMEM((PAD, D), bf16),
        ],
        input_output_aliases={7: 0},
        compiler_params=pltpu.CompilerParams(
            dimension_semantics=("arbitrary", "arbitrary"), vmem_limit_bytes=VLIM_BWD
        ),
        cost_estimate=pl.CostEstimate(
            flops=9_000_000_000, transcendentals=0, bytes_accessed=24_000_000
        ),
        name="attention_backward",
    )(x, q, k, v, e, o, do, acc, wqkv, *([cut[0].reshape(1), cut[1]] if cut else []))


def adam_direction(first_new, second_new):
    return (first_new * (1.0 / (1.0 - beta_one**STEP))) / (
        jnp.sqrt(second_new * (1.0 / (1.0 - beta_two**STEP))) + eps_adam
    )


def rotate(grad, rows_basis, cols_basis, first_old, second_old):
    r = nn(tn(rows_basis, grad).astype(bf16), cols_basis)
    first_new = beta_one * first_old.astype(f32) + (1.0 - beta_one) * r
    second_new = beta_two * second_old.astype(f32) + (1.0 - beta_two) * r * r
    step = adam_direction(first_new, second_new).astype(bf16)
    return r.astype(bf16), nn(rows_basis, nt(step, cols_basis).astype(bf16)).astype(bf16)


def rotate_body(g_ref, a_ref, b_ref, m_ref, r_ref, u_ref):
    r_ref[...], u_ref[...] = rotate(g_ref[...], a_ref[...], b_ref[...], m_ref[0], m_ref[1])


def rotated_step(grad, rows_basis, cols_basis, moments):
    rows = grad.shape[0]
    sd = jax.ShapeDtypeStruct
    return pl.pallas_call(
        rotate_body,
        out_shape=[sd((rows, D), bf16), sd((rows, D), bf16)],
        compiler_params=pltpu.CompilerParams(vmem_limit_bytes=VLIM_STEP),
        cost_estimate=pl.CostEstimate(
            flops=4 * rows * D * (rows + D), transcendentals=rows * D, bytes_accessed=2 * rows * (rows + 5 * D)
        ),
        name="rotated_step",
    )(grad, rows_basis, cols_basis, moments)


def rotate_parts_body(me_ref, *refs):
    grads, a_ref, b_ref, olds, outs = refs[:2], refs[2], refs[3], refs[4:6], refs[6:10]
    g_ref, m_ref, r_ref, u_ref = refs[10:]
    me = me_ref[0]
    planes, inner, rows = len(outs), g_ref.shape[0], r_ref.shape[0]
    per = rows // (planes * inner)
    put_in_order(me & (inner - 1), grads, g_ref)
    put_in_order(me, olds, m_ref)
    r_ref[...], u_ref[...] = rotate(
        g_ref[...].reshape(rows, D), a_ref[...], b_ref[...],
        m_ref[:, 0].reshape(rows, D), m_ref[:, 1].reshape(rows, D),
    )
    n = g_ref.shape[1]
    for rel, out in enumerate(outs):
        row = pl.multiple_of((me ^ (rel * inner)) * per, per)
        out[0] = g_ref[row // n, pl.ds(pl.multiple_of(row % n, per), per)]
        out[1] = r_ref[pl.ds(row, per)]
        out[2] = u_ref[pl.ds(row, per)]


def rotated_step_parts(me, grads, rows_basis, cols_basis, olds, block):
    rows = rows_basis.shape[0]
    inner = 2 * grads[0].shape[0]
    count = 2 * olds[0].shape[0]
    per = rows // count
    full = lambda shape: pl.BlockSpec(shape, lambda i: (0,) * len(shape))
    return pl.pallas_call(
        rotate_parts_body,
        grid=(1,),
        in_specs=[pl.BlockSpec(memory_space=pltpu.SMEM)]
        + [full(g.shape) for g in grads]
        + [full(rows_basis.shape), full(cols_basis.shape)]
        + [pl.BlockSpec((count // 2, 2, per, D), lambda i: (0, 0, block, 0))] * 2,
        out_specs=[full((3, per, D))] * (count // inner),
        out_shape=[jax.ShapeDtypeStruct((3, per, D), bf16)] * (count // inner),
        scratch_shapes=[
            pltpu.VMEM((inner, rows // inner, D), bf16),
            pltpu.VMEM((count, 2, per, D), bf16),
            pltpu.VMEM((rows, D), bf16),
            pltpu.VMEM((rows, D), bf16),
        ],
        compiler_params=pltpu.CompilerParams(vmem_limit_bytes=VLIM_STEP),
        cost_estimate=pl.CostEstimate(
            flops=4 * rows * D * (rows + D), transcendentals=rows * D, bytes_accessed=2 * rows * (rows + 5 * D)
        ),
        name="rotated_step",
    )(me.reshape(1), *grads, rows_basis, cols_basis, *(pltpu.with_memory_space_constraint(v, pltpu.HBM) for v in olds))


class Net:
    def __init__(self, mesh):
        self.count = mesh.size
        self.bits = self.count.bit_length() - 1
        self.inner_bits = self.bits - 2
        self.inner = 1 << self.inner_bits
        self.me = lax.axis_index(axes)
        self.local = self.me & (self.inner - 1)
        self.plane = self.me >> self.inner_bits
        stages = [(0, 1)]
        while stages[-1][0] + stages[-1][1] < self.inner_bits:
            low = stages[-1][0] + stages[-1][1]
            stages.append((low, min(2, self.inner_bits - low)))
        self.stages = stages
        self.top = (self.inner_bits, 2)

    def swap(self, value, offset, targets=(0, 1, 2, 3), sources=(0, 1, 2, 3)):
        pairs = [(i, i ^ offset) for i in range(self.count)]
        pairs = [
            (i, j) for i, j in pairs
            if (i >> self.inner_bits) in sources and (j >> self.inner_bits) in targets
        ]
        return lax.ppermute(value, axes, pairs)

    def digit(self, stage):
        return (self.me >> stage[0]) & ((1 << stage[1]) - 1)

    def collect(self, value, stage):
        return [value] + [self.swap(value, rel << stage[0]) for rel in range(1, 1 << stage[1])]

    def widen(self, value, stage):
        return interleave(self.collect(value, stage))

    def cut(self, pick, stage):
        mine = self.digit(stage)
        return [pick(mine ^ rel) for rel in range(1 << stage[1])]

    def trade(self, terms, stage, targets=(0, 1, 2, 3), sources=(0, 1, 2, 3)):
        return list(terms[:1]) + [
            self.swap(term, rel << stage[0], targets, sources) for rel, term in enumerate(terms) if rel
        ]


def after(value, *earlier):
    return lax.optimization_barrier((value, earlier))[0]


def interleave(parts):
    value = jnp.stack(parts, axis=1)
    return value.reshape((-1,) + value.shape[2:])


def total(parts):
    parts = [p.astype(f32) for p in parts]
    while len(parts) > 1:
        parts = [a + b for a, b in zip(parts[0::2], parts[1::2])]
    return parts[0]


def take_at(value, index, axis):
    return lax.dynamic_index_in_dim(value, index, axis, keepdims=False)


def join_high(pair):
    half = pair.shape[0] // 2
    return pair[:half].astype(f32) + pair[half:].astype(f32)


def sum_cut_body(low, bits, small, me_ref, *refs):
    size = 1 << bits
    parts, terms = refs[:-size], refs[-size:]
    digit = (me_ref[0] >> low) & (size - 1)
    if small:
        whole = total([join_high(p[0, :small]) for p in parts])
        high = whole.astype(bf16)
        pair = jnp.concatenate([high, (whole - high.astype(f32)).astype(bf16)])
    for rel, term in enumerate(terms):
        for j in range(term.shape[0]):
            piece = j * size + (digit ^ rel)
            if small:
                term[j, :small] = pair
                term[j, small:] = total([p[piece, small:] for p in parts]).astype(bf16)
            else:
                term[j] = total([p[piece] for p in parts]).astype(bf16)


def sum_top_body(low, small, me_ref, *refs):
    parts, terms = refs[:-4], refs[-4:]
    plane = (me_ref[0] >> low) & 3
    for rel, term in enumerate(terms):
        goal = plane ^ rel
        if not small:
            piece = jnp.minimum(goal, 2)
            term[...] = total([p[0, piece] for p in parts]).astype(bf16)
            continue
        rows = term.shape[0] - small
        whole = total([join_high(p[0, :small]) for p in parts])
        high = whole.astype(bf16)
        term[:small] = jnp.concatenate([high, (whole - high.astype(f32)).astype(bf16)])

        def give(k):
            count = min(rows, parts[0].shape[1] - small - k * rows)
            begin = small + k * rows
            term[small : small + count] = total([p[0, begin : begin + count] for p in parts]).astype(bf16)
            if count < rows:
                term[small + count :] = jnp.zeros((rows - count, D), bf16)

        for k in range(3):
            pl.when(jnp.maximum(goal, 1) == k + 1)(functools.partial(give, k))


def deal(body, me, parts, term, count):
    full = lambda dims: pl.BlockSpec(dims, lambda i: (0,) * len(dims))
    return pl.pallas_call(
        body,
        grid=(1,),
        in_specs=[pl.BlockSpec(memory_space=pltpu.SMEM)] + [full(p.shape) for p in parts],
        out_specs=[full(term)] * count,
        out_shape=[pltpu.HBM(term, bf16)] * count,
        compiler_params=pltpu.CompilerParams(vmem_limit_bytes=VLIM_STEP),
        cost_estimate=pl.CostEstimate(
            flops=0, transcendentals=0, bytes_accessed=4 * len(parts) * parts[0].size
        ),
        name="sum_and_deal",
    )(me.reshape(1), *parts)


def sum_cut(net, parts, stage, small=0):
    size = 1 << stage[1]
    shape = parts[0].shape
    body = functools.partial(sum_cut_body, *stage, small)
    return deal(body, net.me, parts, (shape[0] // size,) + shape[1:], size)


def sum_top(net, parts, rows, small=0):
    body = functools.partial(sum_top_body, net.top[0], small)
    return deal(body, net.me, parts, (small + rows, D), 4)


def place_body(me_ref, *refs):
    *parts, out = refs
    put_in_order(me_ref[0] & (out.shape[0] - 1), parts, out)


def place(me, parts):
    size = len(parts) * parts[0].shape[0]
    shape = jax.ShapeDtypeStruct((size,) + parts[0].shape[1:], parts[0].dtype)
    return pl.pallas_call(
        place_body,
        in_specs=[pl.BlockSpec(memory_space=pltpu.SMEM)]
        + [pl.BlockSpec(memory_space=pltpu.VMEM)] * len(parts),
        out_specs=pl.BlockSpec(memory_space=pltpu.VMEM),
        out_shape=shape,
        compiler_params=pltpu.CompilerParams(vmem_limit_bytes=24 * 1024 * 1024),
        cost_estimate=pl.CostEstimate(flops=0, transcendentals=0, bytes_accessed=4 * shape.size),
        name="place",
    )(me.reshape(1), *parts)


def finish_body(low, me_ref, *refs):
    attn, ffn = refs[:4], refs[4:8]
    moments_ref, weights_ref, grad_ref, new_ref, out_ref = refs[8:]
    plane = (me_ref[0] >> low) & 3
    per = attn[0].shape[1]
    rows = 8 * per

    def choose(parts, plain, kind):
        value = parts[0][kind].astype(f32)
        for rel in range(1, 4):
            value = jnp.where(plane == (plain ^ rel), parts[rel][kind].astype(f32), value)
        return value.astype(bf16)

    row = lax.broadcasted_iota(jnp.int32, (rows, rows), 0)
    source = lax.broadcasted_iota(jnp.int32, (rows, rows), 1)
    group, slot = row // 8, row % 8
    wanted = jnp.where(
        slot < 4, slot * per + group, (4 + 2 * ((slot - 4) // 2)) * per + 2 * group + slot % 2
    )
    order = jnp.where(source == wanted, 1.0, 0.0).astype(bf16)

    def plain(kind):
        parts = [choose(attn, b, kind) for b in range(4)] + [choose(ffn, f, kind) for f in (1, 2)]
        return nn(order, jnp.concatenate(parts))

    grad_ref[...] = plain(0)
    turned = plain(1)
    new_ref[0] = beta_one * moments_ref[0] + (1.0 - beta_one) * turned
    new_ref[1] = beta_two * moments_ref[1] + (1.0 - beta_two) * turned * turned
    out_ref[...] = weights_ref[...] - rate_mats * plain(2)


def finish(net, attn, ffn, moments, weights):
    full = lambda shape: pl.BlockSpec(shape, lambda i: (0,) * len(shape))
    arrays = [*attn, *ffn, moments, weights]
    outs = [weights, moments, weights]
    return pl.pallas_call(
        functools.partial(finish_body, net.top[0]),
        grid=(1,),
        in_specs=[pl.BlockSpec(memory_space=pltpu.SMEM)] + [full(v.shape) for v in arrays],
        out_specs=[full(v.shape) for v in outs],
        out_shape=[jax.ShapeDtypeStruct(v.shape, f32) for v in outs],
        compiler_params=pltpu.CompilerParams(vmem_limit_bytes=VLIM_STEP),
        cost_estimate=pl.CostEstimate(flops=50_000_000, transcendentals=0, bytes_accessed=3_000_000),
        name="finish",
    )(net.me.reshape(1), *arrays)


def by_index(parts, index):
    return [
        functools.reduce(
            lambda rest, r: jnp.where(index == (b ^ r), parts[r], rest), range(1, len(parts)), parts[0]
        )
        for b in range(len(parts))
    ]


def on_device(mesh, features, cotangent, counts, weights, small_params, moments_old, small_moments,
              basis_attn, basis_ffn, basis_cols):
    net = Net(mesh)
    per = weights.shape[0] // 8
    everyone = net.stages + [net.top]

    def by_matrix(stacked):
        groups = stacked.reshape(per, 8, D)
        return (
            jnp.transpose(groups[:, 0:4], (1, 0, 2)),
            groups[:, 4:6].reshape(2 * per, D),
            groups[:, 6:8].reshape(2 * per, D),
        )

    def stacked(attn, inner, outer):
        return jnp.concatenate(
            [jnp.stack(attn, axis=1), inner.reshape(per, 2, D), outer.reshape(per, 2, D)], axis=1
        ).reshape(8 * per, D)

    inner = net.inner
    n_attn, n_ffn = D // inner, FF // inner
    ffn_of = lambda plane: jnp.clip(plane - 1, 0, 1)
    stages, top = net.stages, net.top

    own_attn, own_in, own_out = by_matrix(weights.astype(bf16))
    first = own_attn[None, 0:3]
    rest = jnp.concatenate([own_attn[3], own_in, own_out])[None]
    olds = [by_matrix(moments_old[i].astype(bf16)) for i in range(2)]
    old_attn = jnp.stack([m[0] for m in olds], axis=1)
    old_ffn = jnp.stack([jnp.stack([m[1], m[2]]) for m in olds], axis=1)
    old_terms = net.cut(
        lambda d: jnp.concatenate([take_at(old_ffn, ffn_of(d), 0), take_at(old_attn, d, 0)], axis=1), top
    )
    mine = ffn_of(net.plane)
    sp = jnp.concatenate([small_params.reshape(7, D), jnp.zeros((1, D), f32)])
    counts_me = jnp.concatenate([counts, net.me.reshape(1)])

    whole_tiles = per % 16 == 0
    order = list(reversed(everyone))
    first = interleave(net.collect(first, order[0]))
    rest_parts = net.collect(after(rest, first), order[0])
    for i, stage in enumerate(order[1:]):
        first_parts = net.collect(first, stage)
        if stage is not order[-1]:
            first = interleave(first_parts)
            rest_parts, first, old_terms, sp, counts_me = after(
                (rest_parts, first, old_terms, sp, counts_me), first_parts
            )
            rest = interleave(rest_parts)
            rest_parts = net.collect(rest, stage)
    if not whole_tiles:
        first_parts = [jnp.transpose(place(net.me, first_parts), (1, 0, 2, 3)).reshape(1, 3, D, D)]
    first_parts, sp, counts_me = lax.optimization_barrier((first_parts, sp, counts_me, rest, old_terms))[:3]
    old_parts = net.trade(after(old_terms, rest), top)
    q, k, v, e, o, li, wqkv = attn_fwd(features, first_parts, net.me)
    rest_parts, old_parts = after((rest_parts, old_parts), o)
    rest, olds = interleave(rest_parts), jnp.stack(old_parts)
    for stage in reversed(stages[2:]):
        olds = net.widen(olds, stage)
    rest_parts = net.collect(after(rest, olds), order[-1])
    old_parts = net.collect(olds, stages[1])
    if not whole_tiles:
        rest = place(net.me, rest_parts)
        rest_parts = [
            jnp.concatenate(
                [rest[:, lo * per : hi * per].reshape(-1, D) for lo, hi in ((0, 1), (1, 3), (3, 5))]
            )[None]
        ]
    output, d1, do, *terms = rows_pass(
        counts_me, features, o, li, cotangent, after(rest_parts, olds), sp, inner
    )

    n_small = 16
    terms, old_parts = after((terms, old_parts), output)
    early_parts = net.trade(terms, stages[0])
    olds = interleave(old_parts)
    early_parts = after(early_parts, olds)
    for stage in stages[2:]:
        early_parts = net.trade(sum_cut(net, early_parts, stage, n_small), stage)
    terms = sum_cut(net, early_parts, stages[1], n_small)
    early_parts = net.trade(terms, stages[1])
    old_parts = net.collect(olds, stages[0])
    back = functools.partial(attn_bwd, x=features, q=q, k=k, v=v, e=e, o=o, do=do)
    acc, gw0 = back(0, acc=d1, wqkv=after(wqkv, terms, olds))
    early_parts, old_parts = after((early_parts, old_parts), gw0)
    top_terms = sum_top(net, early_parts, n_ffn, n_small)
    top_parts = net.trade(top_terms, top)
    grad_input, *terms = back(1, acc=acc, wqkv=after(wqkv, top_terms, old_parts), cut=(net.me, gw0, inner))

    terms, top_parts = lax.optimization_barrier((terms, top_parts))
    late_parts = net.trade(terms, stages[0])
    ffn = total([p[n_small:] for p in top_parts]).astype(bf16)
    ffn_parts = net.collect(ffn[None], stages[-1])
    late_parts = after(late_parts, ffn)
    for stage in stages[2:]:
        late_parts = net.trade(sum_cut(net, late_parts, stage), stage)
    terms = sum_cut(net, late_parts, stages[1])
    late_parts = net.trade(terms, stages[1])
    a_ffn, b_ffn = after((basis_ffn, basis_cols), terms)
    a_ffn, b_ffn = take_at(a_ffn, mine, 0).astype(bf16), take_at(b_ffn, 4 + mine, 0).astype(bf16)
    early_part, ffn_parts, a_ffn, b_ffn = lax.optimization_barrier((late_parts[1], ffn_parts, a_ffn, b_ffn))
    wide = interleave(ffn_parts)
    late_parts, wide = lax.optimization_barrier((late_parts[:1] + [early_part] + late_parts[2:], wide))
    terms = sum_top(net, late_parts, n_attn)
    late_parts = net.trade(terms, top)
    wide = after(wide, terms)
    ffn_parts = net.collect(wide, stages[len(stages) - 2])
    for stage in reversed(stages[:-2]):
        ffn_parts = net.collect(interleave(ffn_parts), stage)

    if whole_tiles:
        back_ffn = rotated_step_parts(net.me, ffn_parts, a_ffn, b_ffn, old_parts, 0)
    else:
        olds = jnp.transpose(place(net.me, old_parts), (1, 0, 2, 3))
        full = place(net.me, ffn_parts).reshape(FF, D)
        both = rotated_step(full, a_ffn, b_ffn, olds[:, :, : 2 * per].reshape(2, FF, D))
        back_ffn = take_at(jnp.stack([full, *both]).reshape(3, 4, inner, 2 * per, D), net.local, 2)
        back_ffn = net.cut(lambda d: take_at(back_ffn, d, 1), top)
    late_parts = after(late_parts, back_ffn)
    attn = total(late_parts).astype(bf16)
    attn = jnp.where(net.plane == 3, ffn[:n_attn], attn)[None]
    a_attn, b_attn = after((basis_attn, basis_cols), attn)
    a_attn, b_attn = (take_at(basis, net.plane, 0).astype(bf16) for basis in (a_attn, b_attn))
    for stage in reversed(stages[1:]):
        attn_parts = net.collect(attn, stage)
        attn_parts, a_attn, b_attn = lax.optimization_barrier((attn_parts, a_attn, b_attn))
        attn = interleave(attn_parts)
    attn_parts = net.collect(attn, stages[0])
    back_ffn = net.trade(back_ffn, top)
    if whole_tiles:
        back_attn = rotated_step_parts(net.me, attn_parts, a_attn, b_attn, old_parts, 2)
    else:
        full = place(net.me, attn_parts).reshape(D, D)
        both = rotated_step(full, a_attn, b_attn, olds[:, :, 2 * per :].reshape(2, D, D))
        back_attn = take_at(jnp.stack([full, *both]).reshape(3, 4, inner, per, D), net.local, 2)
        back_attn = net.cut(lambda d: take_at(back_attn, d, 1), top)
    back_ffn, top_parts = after((back_ffn, top_parts), back_attn)
    gs = total([join_high(p[:n_small]) for p in top_parts])
    back_attn = net.trade(back_attn, top)
    grad_small = gs[0:7].reshape(-1)
    small_first = beta_one * small_moments[0] + (1.0 - beta_one) * grad_small
    small_second = beta_two * small_moments[1] + (1.0 - beta_two) * grad_small * grad_small
    small_new = small_params - rate_small * adam_direction(small_first, small_second)
    small_moments_new = jnp.stack([small_first, small_second])
    back_attn, small_new, small_moments_new = lax.optimization_barrier(
        (back_attn, small_new, small_moments_new)
    )
    if whole_tiles:
        grad_weights, moments_new, weights_new = finish(net, back_attn, back_ffn, moments_old, weights)
    else:
        back_attn = by_index(back_attn, net.plane)
        back_ffn = by_index(back_ffn, net.plane)
        grad_weights, rotated, update = (
            stacked([part[i] for part in back_attn], back_ffn[1][i], back_ffn[2][i]).astype(f32) for i in range(3)
        )
        moments_new = jnp.stack(
            [
                beta_one * moments_old[0] + (1.0 - beta_one) * rotated,
                beta_two * moments_old[1] + (1.0 - beta_two) * rotated * rotated,
            ]
        )
        weights_new = weights - rate_mats * update
    return (
        output,
        grad_input,
        grad_weights,
        moments_new,
        weights_new,
        grad_small,
        small_moments_new,
        small_new,
    )


def solution(mesh):
    rows = P(("dp", "fsdp"), None)
    blocks = P(("dp", "fsdp"), None, None)
    pair = P(None, ("dp", "fsdp"), None)
    return jax.shard_map(
        lambda *arrays: on_device(mesh, *arrays),
        mesh=mesh,
        in_specs=(blocks, blocks, P(("dp", "fsdp")), rows, P(), pair, P(), P(), P(), P()),
        out_specs=(blocks, blocks, rows, pair, rows, P(), P(), P()),
        check_vma=False,
    )
```
